256 devices in a mesh: row: 32 (over z_hi, y, x), col: 8 (over z_lo, core).
Axes of the slice: x: 4, y: 4, z: 8 (z_hi: 2, z_lo: 4; z = z_hi * 4 + z_lo), core: 2. Of those that a mesh axis runs over, the one named last changes fastest.
Arguments:
- tile_values: float32 [32, 8, 64, 128, 128], P('row', 'col'), may hold values from -0.09375 to 0.09375
- tile_row: int32 [32, 8, 64], P('row', 'col'), may hold values from 0 to 31
- tile_col: int32 [32, 8, 64], P('row', 'col'), may hold values from 0 to 127
- counts: int32 [32, 8], P('row', 'col'), may hold values from 21 to 64, as said below
- diagonal: float32 [131072], P(('row', 'col')), may hold values from 1 to 3
- current: float32 [8, 131072], P(None, ('row', 'col')), may hold values from -6 to 6
- previous: float32 [8, 131072], P(None, ('row', 'col')), may hold values from -6 to 6
- previous_image: float32 [8, 131072], P(None, ('row', 'col')), may hold values from -6 to 6
Outputs:
- image: float32 [8, 131072], P(None, ('row', 'col'))
- residual: float32 [8, 131072], P(None, ('row', 'col'))
- residual_image: float32 [8, 131072], P(None, ('row', 'col'))
- reduced: float32 [24, 24], replicated
The draws below stay inside these ranges and needn't reach their ends.
Inputs may be any that keep to these rules, and one draw needn't show every extreme that they name: `counts`: every device has between 21 and 64 live slots; in every draw one device has exactly 64 and one exactly 21.
All inputs are finite; a program needn't handle non-finite values.
Results may differ from the reference program's by a relative error of at most 0.0003.
Values sent between devices are 32-bit elements; how exact they have to be, the bound alone decides.
A program may use at most 64 MiB of HBM per device.

```python
import jax
import jax.numpy as jnp
from jax import lax

K = 8
TILE = 128
VT = 4
SLOTS = 64
NDIM = 131072
N_ROW = 32
N_COL = 8


def draw_counts(key, part):
    owners = N_ROW * N_COL
    least_count = SLOTS // 3
    spread = SLOTS - least_count
    first_key, second_key, pick_key = jax.random.split(key, 3)
    first_draw = jax.random.randint(first_key, (owners,), 0, spread + 1, dtype=jnp.int32)
    second_draw = jax.random.randint(second_key, (owners,), 0, spread + 1, dtype=jnp.int32)
    values = least_count + first_draw * second_draw // spread
    picked = jax.random.permutation(pick_key, owners)
    values = values.at[picked[0]].set(SLOTS).at[picked[1]].set(least_count)
    return values.astype(jnp.int32).reshape(N_ROW, N_COL)


def place_ends(drawn, key, low, high):
    longest = drawn.shape.index(max(drawn.shape))
    spots = []
    for shift in (0, 1):
        where = [jax.random.randint(jax.random.fold_in(key, axis), (), 0, length) for axis, length in enumerate(drawn.shape)]
        where[longest] = (where[longest] + shift) % drawn.shape[longest]
        spots.append(tuple(where))
    return drawn.at[spots[0]].set(low).at[spots[1]].set(high)


def level_of(key, shape, cuts, smallest, largest):
    gain, own = 1.0, jax.random.fold_in(key, 6)
    for dim, parts in cuts:
        draws = jnp.exp(jax.random.uniform(jax.random.fold_in(own, dim), (parts,), jnp.float32, smallest / len(cuts), largest / len(cuts)))
        gain = gain * jnp.repeat(draws, shape[dim] // parts).reshape([-1 if axis == dim else 1 for axis in range(len(shape))])
    return gain


def gaussian(stream_key, extent, scale, limit, shards=(), held_as=jnp.bfloat16):
    result = jax.random.normal(stream_key, extent, jnp.float32) * scale
    if len(shards) > 0:
        result = level_of(stream_key, extent, shards, -0.22, 0.18) * result
    return jnp.clip(result, min=-limit, max=limit).astype(held_as)


def setup_inputs(seed: int = 0) -> dict:
    arg_keys = jax.random.split(jax.random.key(seed), 9)
    return {
        "tile_values": gaussian(arg_keys[0], (N_ROW, N_COL, SLOTS, TILE, TILE), (2 * SLOTS * TILE // VT) ** -0.5, 0.09375, ((0, 32), (1, 8)), jnp.float32),
        "tile_row": place_ends(jax.random.randint(arg_keys[1], (N_ROW, N_COL, SLOTS), 0, N_COL * VT), jax.random.fold_in(arg_keys[1], 1), 0, (N_COL * VT) - 1).astype(jnp.int32),
        "tile_col": place_ends(jax.random.randint(arg_keys[2], (N_ROW, N_COL, SLOTS), 0, N_ROW * VT), jax.random.fold_in(arg_keys[2], 1), 0, (N_ROW * VT) - 1).astype(jnp.int32),
        "counts": draw_counts(jax.random.fold_in(arg_keys[8], 71), 0),
        "diagonal": jnp.clip(1.0 + 2.0 * jax.random.uniform(arg_keys[4], (NDIM,), jnp.float32) ** level_of(arg_keys[4], (NDIM,), ((0, 256),), -0.2, 0.2), 1.0, 3.0),
        "current": gaussian(arg_keys[5], (K, NDIM), 1.0, 6.0, ((1, 256),), jnp.float32),
        "previous": gaussian(arg_keys[6], (K, NDIM), 1.0, 6.0, ((1, 256),), jnp.float32),
        "previous_image": gaussian(arg_keys[7], (K, NDIM), 1.0, 6.0, ((1, 256),), jnp.float32),
    }


highest = lax.Precision.HIGHEST

def apply_operator(vectors, diagonal, tile_values, tile_row, tile_col, counts):
    vector_count = vectors.shape[0]
    columns = vectors.reshape(vector_count, -1, TILE)
    owners = N_ROW * N_COL
    owner_ids = jnp.arange(owners, dtype=jnp.int32)
    flat_tiles = tile_values.reshape(owners, SLOTS, TILE, TILE)
    flat_rows = tile_row.reshape(owners, SLOTS)
    flat_cols = tile_col.reshape(owners, SLOTS)
    flat_counts = counts.reshape(owners)
    slot_ids = jnp.arange(SLOTS, dtype=jnp.int32)

    def one_device(running_sum, device_item):
        blocks, rows_here, cols_here, live_count, owner = device_item
        row_owner = owner // N_COL
        col_owner = owner % N_COL
        global_rows = row_owner * (N_COL * VT) + rows_here
        global_cols = (cols_here // VT * N_COL + col_owner) * VT + cols_here % VT
        weight = (slot_ids < live_count).astype(jnp.float32)[None, :, None]
        direct = jnp.einsum('sij,ksj->ksi', blocks, columns[:, global_cols, :], precision=highest) * weight
        mirror = jnp.einsum('sij,ksi->ksj', blocks, columns[:, global_rows, :], precision=highest) * weight
        running_sum = running_sum.at[:, global_rows, :].add(direct)
        running_sum = running_sum.at[:, global_cols, :].add(mirror)
        return (running_sum, None)
    zero_sum = jnp.zeros_like(columns)
    running_sum, unused = lax.scan(one_device, zero_sum, (flat_tiles, flat_rows, flat_cols, flat_counts, owner_ids))
    return diagonal[None, :] * vectors + running_sum.reshape(vector_count, -1)

def dot_rows(left, right):
    return jnp.dot(left, right.T, precision=highest)

def reference(tile_values, tile_row, tile_col, counts, diagonal, current, previous, previous_image):
    image = apply_operator(current, diagonal, tile_values, tile_row, tile_col, counts)
    small_gram = dot_rows(current, current)
    small_proj = dot_rows(current, image)
    factor = jnp.linalg.cholesky(small_gram)
    ritz_matrix = jax.scipy.linalg.cho_solve((factor, True), small_proj)
    residual = image - jnp.dot(ritz_matrix.T, current, precision=highest)
    residual_image = apply_operator(residual, diagonal, tile_values, tile_row, tile_col, counts)
    search_basis = jnp.concatenate([current, residual, previous], 0)
    basis_image = jnp.concatenate([image, residual_image, previous_image], 0)
    correlation = dot_rows(search_basis, search_basis)
    mixed_terms = dot_rows(search_basis, basis_image)
    pencil = 0.5 * (mixed_terms + mixed_terms.T)
    lower_factor = jnp.linalg.cholesky(correlation)
    half_solve = jax.scipy.linalg.solve_triangular(lower_factor, pencil, lower=True)
    reduced = jax.scipy.linalg.solve_triangular(lower_factor, half_solve.T, lower=True)
    return (image, residual, residual_image, reduced)
```

```python
import functools

import jax
import jax.numpy as jnp
from jax import lax
from jax.experimental import pallas as pl
from jax.experimental.pallas import tpu as pltpu
from jax.sharding import PartitionSpec as P

highest = lax.Precision.HIGHEST
group_width = 8
MESH = pl.DeviceIdType.MESH


def _barrier(n_row, n_col, r, c):
    barrier = pltpu.get_barrier_semaphore()

    def greet_col(k, carry):
        pl.semaphore_signal(barrier, 1, device_id=(r, lax.rem(c + k, n_col)), device_id_type=MESH)
        return carry

    def greet_row(k, carry):
        pl.semaphore_signal(barrier, 1, device_id=(lax.rem(r + k, n_row), c), device_id_type=MESH)
        return carry

    lax.fori_loop(1, n_col, greet_col, 0)
    lax.fori_loop(1, n_row, greet_row, 0)
    pl.semaphore_wait(barrier, n_row + n_col - 2)


def _gather_kernel(n_row, n_col, x_ref, rowv_ref, colv_ref, send_row, recv_row, send_col, recv_col, local_sem):
    vt = x_ref.shape[0]
    r = lax.axis_index("row")
    c = lax.axis_index("col")
    _barrier(n_row, n_col, r, c)

    def row_copy(j, src):
        return pltpu.make_async_remote_copy(
            src_ref=x_ref,
            dst_ref=rowv_ref.at[pl.ds(src * vt, vt)],
            send_sem=send_row.at[j],
            recv_sem=recv_row.at[src],
            device_id=(r, j),
            device_id_type=MESH,
        )

    def col_copy(i, src):
        return pltpu.make_async_remote_copy(
            src_ref=x_ref,
            dst_ref=colv_ref.at[pl.ds(src * vt, vt)],
            send_sem=send_col.at[i],
            recv_sem=recv_col.at[src],
            device_id=(i, c),
            device_id_type=MESH,
        )

    own_row = pltpu.make_async_copy(x_ref, rowv_ref.at[pl.ds(c * vt, vt)], local_sem.at[0])
    own_col = pltpu.make_async_copy(x_ref, colv_ref.at[pl.ds(r * vt, vt)], local_sem.at[1])
    own_row.start()
    own_col.start()

    def start_col(k, carry):
        row_copy(lax.rem(c + k, n_col), c).start()
        return carry

    def start_row(k, carry):
        col_copy(lax.rem(r + k, n_row), r).start()
        return carry

    lax.fori_loop(1, n_col, start_col, 0)
    lax.fori_loop(1, n_row, start_row, 0)

    def wait_col(k, carry):
        row_copy(lax.rem(c + k, n_col), c).wait_send()
        row_copy(c, lax.rem(c + n_col - k, n_col)).wait_recv()
        return carry

    def wait_row(k, carry):
        col_copy(lax.rem(r + k, n_row), r).wait_send()
        col_copy(r, lax.rem(r + n_row - k, n_row)).wait_recv()
        return carry

    lax.fori_loop(1, n_col, wait_col, 0)
    lax.fori_loop(1, n_row, wait_row, 0)
    own_row.wait()
    own_col.wait()


def gather_tiles(x_tiles, n_row, n_col):
    vt, k, t = x_tiles.shape
    vmem = pl.BlockSpec(memory_space=pltpu.VMEM)
    return pl.pallas_call(
        functools.partial(_gather_kernel, n_row, n_col),
        out_shape=(
            jax.ShapeDtypeStruct((n_col * vt, k, t), x_tiles.dtype),
            jax.ShapeDtypeStruct((n_row * vt, k, t), x_tiles.dtype),
        ),
        in_specs=[vmem],
        out_specs=(vmem, vmem),
        scratch_shapes=[
            pltpu.SemaphoreType.DMA((n_col,)),
            pltpu.SemaphoreType.DMA((n_col,)),
            pltpu.SemaphoreType.DMA((n_row,)),
            pltpu.SemaphoreType.DMA((n_row,)),
            pltpu.SemaphoreType.DMA((2,)),
        ],
        compiler_params=pltpu.CompilerParams(collective_id=0, has_side_effects=True),
    )(x_tiles)


def _reduce_kernel(n_row, n_col, base_ref, rsum_ref, csum_ref, out_ref, got_row, got_col,
                   send_row, recv_row, send_col, recv_col, local_sem):
    vt = base_ref.shape[0]
    r = lax.axis_index("row")
    c = lax.axis_index("col")
    _barrier(n_row, n_col, r, c)

    def row_copy(j, src):
        return pltpu.make_async_remote_copy(
            src_ref=rsum_ref.at[pl.ds(j * vt, vt)],
            dst_ref=got_row.at[src],
            send_sem=send_row.at[j],
            recv_sem=recv_row.at[src],
            device_id=(r, j),
            device_id_type=MESH,
        )

    def col_copy(i, src):
        return pltpu.make_async_remote_copy(
            src_ref=csum_ref.at[pl.ds(i * vt, vt)],
            dst_ref=got_col.at[src],
            send_sem=send_col.at[i],
            recv_sem=recv_col.at[src],
            device_id=(i, c),
            device_id_type=MESH,
        )

    own_row = pltpu.make_async_copy(rsum_ref.at[pl.ds(c * vt, vt)], got_row.at[c], local_sem.at[0])
    own_col = pltpu.make_async_copy(csum_ref.at[pl.ds(r * vt, vt)], got_col.at[r], local_sem.at[1])
    own_row.start()
    own_col.start()

    def start_col(k, carry):
        row_copy(lax.rem(c + k, n_col), c).start()
        return carry

    def start_row(k, carry):
        col_copy(lax.rem(r + k, n_row), r).start()
        return carry

    lax.fori_loop(1, n_col, start_col, 0)
    lax.fori_loop(1, n_row, start_row, 0)

    def wait_col(k, carry):
        row_copy(lax.rem(c + k, n_col), c).wait_send()
        row_copy(c, lax.rem(c + n_col - k, n_col)).wait_recv()
        return carry

    def wait_row(k, carry):
        col_copy(lax.rem(r + k, n_row), r).wait_send()
        col_copy(r, lax.rem(r + n_row - k, n_row)).wait_recv()
        return carry

    lax.fori_loop(1, n_col, wait_col, 0)
    lax.fori_loop(1, n_row, wait_row, 0)
    own_row.wait()
    own_col.wait()
    out_ref[...] = base_ref[...] + jnp.sum(got_row[...], axis=0) + jnp.sum(got_col[...], axis=0)


def reduce_tiles(base_tiles, row_sum, col_sum, n_row, n_col):
    vt, k, t = base_tiles.shape
    vmem = pl.BlockSpec(memory_space=pltpu.VMEM)
    return pl.pallas_call(
        functools.partial(_reduce_kernel, n_row, n_col),
        out_shape=jax.ShapeDtypeStruct((vt, k, t), base_tiles.dtype),
        in_specs=[vmem, vmem, vmem],
        out_specs=vmem,
        scratch_shapes=[
            pltpu.VMEM((n_col, vt, k, t), jnp.float32),
            pltpu.VMEM((n_row, vt, k, t), jnp.float32),
            pltpu.SemaphoreType.DMA((n_col,)),
            pltpu.SemaphoreType.DMA((n_col,)),
            pltpu.SemaphoreType.DMA((n_row,)),
            pltpu.SemaphoreType.DMA((n_row,)),
            pltpu.SemaphoreType.DMA((2,)),
        ],
        compiler_params=pltpu.CompilerParams(collective_id=1, has_side_effects=True),
    )(base_tiles, row_sum, col_sum)


def apply_operator(vectors, diagonal, tile_values, tile_row, tile_col, counts, n_row, n_col):
    vector_count = vectors.shape[0]
    tile_size = tile_values.shape[-1]
    slot_count = tile_values.shape[2]
    blocks = tile_values.reshape(slot_count, tile_size, tile_size)
    rows_here = tile_row.reshape(slot_count)
    cols_here = tile_col.reshape(slot_count)
    live_count = counts.reshape(())
    x_tiles = vectors.reshape(vector_count, -1, tile_size).transpose(1, 0, 2)
    row_tiles, column_tiles = gather_tiles(x_tiles, n_row, n_col)
    slot_ids = jnp.arange(group_width, dtype=jnp.int32)

    def visit(group_index, carry):
        row_sum, column_sum = carry
        first_slot = group_index * group_width
        chosen = lax.dynamic_slice_in_dim(blocks, first_slot, group_width, 0)
        rows_now = lax.dynamic_slice_in_dim(rows_here, first_slot, group_width, 0)
        cols_now = lax.dynamic_slice_in_dim(cols_here, first_slot, group_width, 0)
        weight = (first_slot + slot_ids < live_count).astype(jnp.float32)[:, None, None]
        direct = (
            jnp.einsum("sij,skj->ski", chosen, column_tiles[cols_now], precision=highest)
            * weight
        )
        mirror = (
            jnp.einsum("sij,ski->skj", chosen, row_tiles[rows_now], precision=highest)
            * weight
        )
        return (row_sum.at[rows_now].add(direct), column_sum.at[cols_now].add(mirror))

    groups = (live_count + group_width - 1) // group_width
    row_sum, column_sum = lax.fori_loop(
        0, groups, visit, (jnp.zeros_like(row_tiles), jnp.zeros_like(column_tiles))
    )
    base = (diagonal[None, :] * vectors).reshape(vector_count, -1, tile_size).transpose(1, 0, 2)
    owned = reduce_tiles(base, row_sum, column_sum, n_row, n_col)
    return owned.transpose(1, 0, 2).reshape(vector_count, -1)


def dot_rows(left, right):
    return jnp.dot(left, right.T, precision=highest)


def local(n_row, n_col, tile_values, tile_row, tile_col, counts, diagonal, current, previous, previous_image):
    op = functools.partial(apply_operator, n_row=n_row, n_col=n_col)
    image = op(current, diagonal, tile_values, tile_row, tile_col, counts)
    small_gram, small_proj = lax.psum(
        (dot_rows(current, current), dot_rows(current, image)), ("row", "col")
    )
    factor = jnp.linalg.cholesky(small_gram)
    ritz_matrix = jax.scipy.linalg.cho_solve((factor, True), small_proj)
    residual = image - jnp.dot(ritz_matrix.T, current, precision=highest)
    residual_image = op(residual, diagonal, tile_values, tile_row, tile_col, counts)
    search_basis = jnp.concatenate([current, residual, previous], 0)
    basis_image = jnp.concatenate([image, residual_image, previous_image], 0)
    correlation, mixed_terms = lax.psum(
        (dot_rows(search_basis, search_basis), dot_rows(search_basis, basis_image)), ("row", "col")
    )
    pencil = 0.5 * (mixed_terms + mixed_terms.T)
    lower_factor = jnp.linalg.cholesky(correlation)
    half_solve = jax.scipy.linalg.solve_triangular(lower_factor, pencil, lower=True)
    reduced = jax.scipy.linalg.solve_triangular(lower_factor, half_solve.T, lower=True)
    return (image, residual, residual_image, reduced)


def solution(mesh):
    n_row = mesh.shape["row"]
    n_col = mesh.shape["col"]
    return jax.shard_map(
        functools.partial(local, n_row, n_col),
        mesh=mesh,
        in_specs=(
            P("row", "col", None, None, None),
            P("row", "col", None),
            P("row", "col", None),
            P("row", "col"),
            P(("row", "col")),
            P(None, ("row", "col")),
            P(None, ("row", "col")),
            P(None, ("row", "col")),
        ),
        out_specs=(P(None, ("row", "col")), P(None, ("row", "col")), P(None, ("row", "col")), P()),
        check_vma=False,
    )
```

```python
import functools

import jax
import jax.numpy as jnp
from jax import lax
from jax.experimental import pallas as pl
from jax.experimental.pallas import tpu as pltpu
from jax.sharding import PartitionSpec as P

highest = lax.Precision.HIGHEST
group_width = 8
MESH = pl.DeviceIdType.MESH


def _barrier(n_row, n_col, r, c):
    barrier = pltpu.get_barrier_semaphore()

    def greet_col(k, carry):
        pl.semaphore_signal(barrier, 1, device_id=(r, lax.rem(c + k, n_col)), device_id_type=MESH)
        return carry

    def greet_row(k, carry):
        pl.semaphore_signal(barrier, 1, device_id=(lax.rem(r + k, n_row), c), device_id_type=MESH)
        return carry

    lax.fori_loop(1, n_col, greet_col, 0)
    lax.fori_loop(1, n_row, greet_row, 0)
    pl.semaphore_wait(barrier, n_row + n_col - 2)


def _gather_kernel(n_row, n_col, x_ref, rowv_ref, colv_ref, send_row, recv_row, send_col, recv_col, local_sem):
    vt = x_ref.shape[0]
    r = lax.axis_index("row")
    c = lax.axis_index("col")
    _barrier(n_row, n_col, r, c)

    def row_copy(j, src):
        return pltpu.make_async_remote_copy(
            src_ref=x_ref,
            dst_ref=rowv_ref.at[pl.ds(src * vt, vt)],
            send_sem=send_row.at[j],
            recv_sem=recv_row.at[src],
            device_id=(r, j),
            device_id_type=MESH,
        )

    def col_copy(i, src):
        return pltpu.make_async_remote_copy(
            src_ref=x_ref,
            dst_ref=colv_ref.at[pl.ds(src * vt, vt)],
            send_sem=send_col.at[i],
            recv_sem=recv_col.at[src],
            device_id=(i, c),
            device_id_type=MESH,
        )

    own_row = pltpu.make_async_copy(x_ref, rowv_ref.at[pl.ds(c * vt, vt)], local_sem.at[0])
    own_col = pltpu.make_async_copy(x_ref, colv_ref.at[pl.ds(r * vt, vt)], local_sem.at[1])
    own_row.start()
    own_col.start()

    def start_col(k, carry):
        row_copy(lax.rem(c + k, n_col), c).start()
        return carry

    def start_row(k, carry):
        col_copy(lax.rem(r + k, n_row), r).start()
        return carry

    lax.fori_loop(1, n_col, start_col, 0)
    lax.fori_loop(1, n_row, start_row, 0)

    def wait_col(k, carry):
        row_copy(lax.rem(c + k, n_col), c).wait_send()
        row_copy(c, lax.rem(c + n_col - k, n_col)).wait_recv()
        return carry

    def wait_row(k, carry):
        col_copy(lax.rem(r + k, n_row), r).wait_send()
        col_copy(r, lax.rem(r + n_row - k, n_row)).wait_recv()
        return carry

    lax.fori_loop(1, n_col, wait_col, 0)
    lax.fori_loop(1, n_row, wait_row, 0)
    own_row.wait()
    own_col.wait()


def gather_tiles(x_tiles, n_row, n_col):
    vt, k, t = x_tiles.shape
    vmem = pl.BlockSpec(memory_space=pltpu.VMEM)
    return pl.pallas_call(
        functools.partial(_gather_kernel, n_row, n_col),
        out_shape=(
            jax.ShapeDtypeStruct((n_col * vt, k, t), x_tiles.dtype),
            jax.ShapeDtypeStruct((n_row * vt, k, t), x_tiles.dtype),
        ),
        in_specs=[vmem],
        out_specs=(vmem, vmem),
        scratch_shapes=[
            pltpu.SemaphoreType.DMA((n_col,)),
            pltpu.SemaphoreType.DMA((n_col,)),
            pltpu.SemaphoreType.DMA((n_row,)),
            pltpu.SemaphoreType.DMA((n_row,)),
            pltpu.SemaphoreType.DMA((2,)),
        ],
        compiler_params=pltpu.CompilerParams(collective_id=0, has_side_effects=True),
    )(x_tiles)


def _reduce_kernel(n_row, n_col, base_ref, rsum_ref, csum_ref, out_ref, got_row, got_col,
                   send_row, recv_row, send_col, recv_col, local_sem):
    vt = base_ref.shape[0]
    r = lax.axis_index("row")
    c = lax.axis_index("col")
    _barrier(n_row, n_col, r, c)

    def row_copy(j, src):
        return pltpu.make_async_remote_copy(
            src_ref=rsum_ref.at[pl.ds(j * vt, vt)],
            dst_ref=got_row.at[src],
            send_sem=send_row.at[j],
            recv_sem=recv_row.at[src],
            device_id=(r, j),
            device_id_type=MESH,
        )

    def col_copy(i, src):
        return pltpu.make_async_remote_copy(
            src_ref=csum_ref.at[pl.ds(i * vt, vt)],
            dst_ref=got_col.at[src],
            send_sem=send_col.at[i],
            recv_sem=recv_col.at[src],
            device_id=(i, c),
            device_id_type=MESH,
        )

    own_row = pltpu.make_async_copy(rsum_ref.at[pl.ds(c * vt, vt)], got_row.at[c], local_sem.at[0])
    own_col = pltpu.make_async_copy(csum_ref.at[pl.ds(r * vt, vt)], got_col.at[r], local_sem.at[1])
    own_row.start()
    own_col.start()

    def start_col(k, carry):
        row_copy(lax.rem(c + k, n_col), c).start()
        return carry

    def start_row(k, carry):
        col_copy(lax.rem(r + k, n_row), r).start()
        return carry

    lax.fori_loop(1, n_col, start_col, 0)
    lax.fori_loop(1, n_row, start_row, 0)

    def wait_col(k, carry):
        row_copy(lax.rem(c + k, n_col), c).wait_send()
        row_copy(c, lax.rem(c + n_col - k, n_col)).wait_recv()
        return carry

    def wait_row(k, carry):
        col_copy(lax.rem(r + k, n_row), r).wait_send()
        col_copy(r, lax.rem(r + n_row - k, n_row)).wait_recv()
        return carry

    lax.fori_loop(1, n_col, wait_col, 0)
    lax.fori_loop(1, n_row, wait_row, 0)
    own_row.wait()
    own_col.wait()
    out_ref[...] = base_ref[...] + jnp.sum(got_row[...], axis=0) + jnp.sum(got_col[...], axis=0)


def reduce_tiles(base_tiles, row_sum, col_sum, n_row, n_col):
    vt, k, t = base_tiles.shape
    vmem = pl.BlockSpec(memory_space=pltpu.VMEM)
    return pl.pallas_call(
        functools.partial(_reduce_kernel, n_row, n_col),
        out_shape=jax.ShapeDtypeStruct((vt, k, t), base_tiles.dtype),
        in_specs=[vmem, vmem, vmem],
        out_specs=vmem,
        scratch_shapes=[
            pltpu.VMEM((n_col, vt, k, t), jnp.float32),
            pltpu.VMEM((n_row, vt, k, t), jnp.float32),
            pltpu.SemaphoreType.DMA((n_col,)),
            pltpu.SemaphoreType.DMA((n_col,)),
            pltpu.SemaphoreType.DMA((n_row,)),
            pltpu.SemaphoreType.DMA((n_row,)),
            pltpu.SemaphoreType.DMA((2,)),
        ],
        compiler_params=pltpu.CompilerParams(collective_id=1, has_side_effects=True),
    )(base_tiles, row_sum, col_sum)


def _psum_kernel(n_row, n_col, x_ref, out_ref, got_col, mid, got_row,
                 send_col, recv_col, send_row, recv_row, local_sem):
    r = lax.axis_index("row")
    c = lax.axis_index("col")
    _barrier(n_row, n_col, r, c)

    def col_copy(j, src):
        return pltpu.make_async_remote_copy(
            src_ref=x_ref,
            dst_ref=got_col.at[src],
            send_sem=send_col.at[j],
            recv_sem=recv_col.at[src],
            device_id=(r, j),
            device_id_type=MESH,
        )

    def row_copy(i, src):
        return pltpu.make_async_remote_copy(
            src_ref=mid,
            dst_ref=got_row.at[src],
            send_sem=send_row.at[i],
            recv_sem=recv_row.at[src],
            device_id=(i, c),
            device_id_type=MESH,
        )

    own_col = pltpu.make_async_copy(x_ref, got_col.at[c], local_sem.at[0])
    own_col.start()

    def start_col(k, carry):
        col_copy(lax.rem(c + k, n_col), c).start()
        return carry

    def wait_col(k, carry):
        col_copy(lax.rem(c + k, n_col), c).wait_send()
        col_copy(c, lax.rem(c + n_col - k, n_col)).wait_recv()
        return carry

    lax.fori_loop(1, n_col, start_col, 0)
    lax.fori_loop(1, n_col, wait_col, 0)
    own_col.wait()
    mid[...] = jnp.sum(got_col[...], axis=0)

    own_row = pltpu.make_async_copy(mid, got_row.at[r], local_sem.at[1])
    own_row.start()

    def start_row(k, carry):
        row_copy(lax.rem(r + k, n_row), r).start()
        return carry

    def wait_row(k, carry):
        row_copy(lax.rem(r + k, n_row), r).wait_send()
        row_copy(r, lax.rem(r + n_row - k, n_row)).wait_recv()
        return carry

    lax.fori_loop(1, n_row, start_row, 0)
    lax.fori_loop(1, n_row, wait_row, 0)
    own_row.wait()
    out_ref[...] = jnp.sum(got_row[...], axis=0)


def psum_small(values, n_row, n_col, collective_id):
    flat = jnp.concatenate([v.reshape(-1) for v in values])
    tile = 8 * 128
    padded = -(-flat.shape[0] // tile) * tile
    packed = jnp.pad(flat, (0, padded - flat.shape[0])).reshape(-1, 128)
    s, t = packed.shape
    vmem = pl.BlockSpec(memory_space=pltpu.VMEM)
    total = pl.pallas_call(
        functools.partial(_psum_kernel, n_row, n_col),
        out_shape=jax.ShapeDtypeStruct((s, t), jnp.float32),
        in_specs=[vmem],
        out_specs=vmem,
        scratch_shapes=[
            pltpu.VMEM((n_col, s, t), jnp.float32),
            pltpu.VMEM((s, t), jnp.float32),
            pltpu.VMEM((n_row, s, t), jnp.float32),
            pltpu.SemaphoreType.DMA((n_col,)),
            pltpu.SemaphoreType.DMA((n_col,)),
            pltpu.SemaphoreType.DMA((n_row,)),
            pltpu.SemaphoreType.DMA((n_row,)),
            pltpu.SemaphoreType.DMA((2,)),
        ],
        compiler_params=pltpu.CompilerParams(collective_id=collective_id, has_side_effects=True),
    )(packed).reshape(-1)
    out, start = [], 0
    for v in values:
        out.append(total[start:start + v.size].reshape(v.shape))
        start += v.size
    return out


def apply_operator(vectors, diagonal, tile_values, tile_row, tile_col, counts, n_row, n_col):
    vector_count = vectors.shape[0]
    tile_size = tile_values.shape[-1]
    slot_count = tile_values.shape[2]
    blocks = tile_values.reshape(slot_count, tile_size, tile_size)
    rows_here = tile_row.reshape(slot_count)
    cols_here = tile_col.reshape(slot_count)
    live_count = counts.reshape(())
    x_tiles = vectors.reshape(vector_count, -1, tile_size).transpose(1, 0, 2)
    row_tiles, column_tiles = gather_tiles(x_tiles, n_row, n_col)
    slot_ids = jnp.arange(group_width, dtype=jnp.int32)

    def visit(group_index, carry):
        row_sum, column_sum = carry
        first_slot = group_index * group_width
        chosen = lax.dynamic_slice_in_dim(blocks, first_slot, group_width, 0)
        rows_now = lax.dynamic_slice_in_dim(rows_here, first_slot, group_width, 0)
        cols_now = lax.dynamic_slice_in_dim(cols_here, first_slot, group_width, 0)
        weight = (first_slot + slot_ids < live_count).astype(jnp.float32)[:, None, None]
        direct = (
            jnp.einsum("sij,skj->ski", chosen, column_tiles[cols_now], precision=highest)
            * weight
        )
        mirror = (
            jnp.einsum("sij,ski->skj", chosen, row_tiles[rows_now], precision=highest)
            * weight
        )
        return (row_sum.at[rows_now].add(direct), column_sum.at[cols_now].add(mirror))

    groups = (live_count + group_width - 1) // group_width
    row_sum, column_sum = lax.fori_loop(
        0, groups, visit, (jnp.zeros_like(row_tiles), jnp.zeros_like(column_tiles))
    )
    base = (diagonal[None, :] * vectors).reshape(vector_count, -1, tile_size).transpose(1, 0, 2)
    owned = reduce_tiles(base, row_sum, column_sum, n_row, n_col)
    return owned.transpose(1, 0, 2).reshape(vector_count, -1)


def dot_rows(left, right):
    return jnp.dot(left, right.T, precision=highest)


def local(n_row, n_col, tile_values, tile_row, tile_col, counts, diagonal, current, previous, previous_image):
    op = functools.partial(apply_operator, n_row=n_row, n_col=n_col)
    image = op(current, diagonal, tile_values, tile_row, tile_col, counts)
    small_gram, small_proj = psum_small(
        (dot_rows(current, current), dot_rows(current, image)), n_row, n_col, 2
    )
    factor = jnp.linalg.cholesky(small_gram)
    ritz_matrix = jax.scipy.linalg.cho_solve((factor, True), small_proj)
    residual = image - jnp.dot(ritz_matrix.T, current, precision=highest)
    residual_image = op(residual, diagonal, tile_values, tile_row, tile_col, counts)
    search_basis = jnp.concatenate([current, residual, previous], 0)
    basis_image = jnp.concatenate([image, residual_image, previous_image], 0)
    correlation, mixed_terms = psum_small(
        (dot_rows(search_basis, search_basis), dot_rows(search_basis, basis_image)), n_row, n_col, 3
    )
    pencil = 0.5 * (mixed_terms + mixed_terms.T)
    lower_factor = jnp.linalg.cholesky(correlation)
    half_solve = jax.scipy.linalg.solve_triangular(lower_factor, pencil, lower=True)
    reduced = jax.scipy.linalg.solve_triangular(lower_factor, half_solve.T, lower=True)
    return (image, residual, residual_image, reduced)


def solution(mesh):
    n_row = mesh.shape["row"]
    n_col = mesh.shape["col"]
    return jax.shard_map(
        functools.partial(local, n_row, n_col),
        mesh=mesh,
        in_specs=(
            P("row", "col", None, None, None),
            P("row", "col", None),
            P("row", "col", None),
            P("row", "col"),
            P(("row", "col")),
            P(None, ("row", "col")),
            P(None, ("row", "col")),
            P(None, ("row", "col")),
        ),
        out_specs=(P(None, ("row", "col")), P(None, ("row", "col")), P(None, ("row", "col")), P()),
        check_vma=False,
    )
```

```python
import functools

import jax
import jax.numpy as jnp
from jax import lax
from jax.experimental import pallas as pl
from jax.experimental.pallas import tpu as pltpu
from jax.sharding import PartitionSpec as P

highest = lax.Precision.HIGHEST
group_width = 8
MESH = pl.DeviceIdType.MESH


def _barrier(n_row, n_col, r, c):
    barrier = pltpu.get_barrier_semaphore()

    def greet_col(k, carry):
        pl.semaphore_signal(barrier, 1, device_id=(r, lax.rem(c + k, n_col)), device_id_type=MESH)
        return carry

    def greet_row(k, carry):
        pl.semaphore_signal(barrier, 1, device_id=(lax.rem(r + k, n_row), c), device_id_type=MESH)
        return carry

    lax.fori_loop(1, n_col, greet_col, 0)
    lax.fori_loop(1, n_row, greet_row, 0)
    pl.semaphore_wait(barrier, n_row + n_col - 2)


def _gather_kernel(n_row, n_col, x_ref, rowv_ref, colv_ref, send_row, recv_row, send_col, recv_col, local_sem):
    vt = x_ref.shape[0]
    r = lax.axis_index("row")
    c = lax.axis_index("col")
    _barrier(n_row, n_col, r, c)

    def row_copy(j, src):
        return pltpu.make_async_remote_copy(
            src_ref=x_ref,
            dst_ref=rowv_ref.at[pl.ds(src * vt, vt)],
            send_sem=send_row.at[j],
            recv_sem=recv_row.at[src],
            device_id=(r, j),
            device_id_type=MESH,
        )

    def col_copy(i, src):
        return pltpu.make_async_remote_copy(
            src_ref=x_ref,
            dst_ref=colv_ref.at[pl.ds(src * vt, vt)],
            send_sem=send_col.at[i],
            recv_sem=recv_col.at[src],
            device_id=(i, c),
            device_id_type=MESH,
        )

    own_row = pltpu.make_async_copy(x_ref, rowv_ref.at[pl.ds(c * vt, vt)], local_sem.at[0])
    own_col = pltpu.make_async_copy(x_ref, colv_ref.at[pl.ds(r * vt, vt)], local_sem.at[1])
    own_row.start()
    own_col.start()

    def start_col(k, carry):
        row_copy(lax.rem(c + k, n_col), c).start()
        return carry

    def start_row(k, carry):
        col_copy(lax.rem(r + k, n_row), r).start()
        return carry

    lax.fori_loop(1, n_col, start_col, 0)
    lax.fori_loop(1, n_row, start_row, 0)

    def wait_col(k, carry):
        row_copy(lax.rem(c + k, n_col), c).wait_send()
        row_copy(c, lax.rem(c + n_col - k, n_col)).wait_recv()
        return carry

    def wait_row(k, carry):
        col_copy(lax.rem(r + k, n_row), r).wait_send()
        col_copy(r, lax.rem(r + n_row - k, n_row)).wait_recv()
        return carry

    lax.fori_loop(1, n_col, wait_col, 0)
    lax.fori_loop(1, n_row, wait_row, 0)
    own_row.wait()
    own_col.wait()


def gather_tiles(x_tiles, n_row, n_col):
    vt, k, t = x_tiles.shape
    vmem = pl.BlockSpec(memory_space=pltpu.VMEM)
    return pl.pallas_call(
        functools.partial(_gather_kernel, n_row, n_col),
        out_shape=(
            jax.ShapeDtypeStruct((n_col * vt, k, t), x_tiles.dtype),
            jax.ShapeDtypeStruct((n_row * vt, k, t), x_tiles.dtype),
        ),
        in_specs=[vmem],
        out_specs=(vmem, vmem),
        scratch_shapes=[
            pltpu.SemaphoreType.DMA((n_col,)),
            pltpu.SemaphoreType.DMA((n_col,)),
            pltpu.SemaphoreType.DMA((n_row,)),
            pltpu.SemaphoreType.DMA((n_row,)),
            pltpu.SemaphoreType.DMA((2,)),
        ],
        compiler_params=pltpu.CompilerParams(collective_id=0, has_side_effects=True),
    )(x_tiles)


def _reduce_kernel(n_row, n_col, base_ref, rsum_ref, csum_ref, out_ref, got_row, got_col,
                   send_row, recv_row, send_col, recv_col, local_sem):
    vt = base_ref.shape[0]
    r = lax.axis_index("row")
    c = lax.axis_index("col")
    _barrier(n_row, n_col, r, c)

    def row_copy(j, src):
        return pltpu.make_async_remote_copy(
            src_ref=rsum_ref.at[pl.ds(j * vt, vt)],
            dst_ref=got_row.at[src],
            send_sem=send_row.at[j],
            recv_sem=recv_row.at[src],
            device_id=(r, j),
            device_id_type=MESH,
        )

    def col_copy(i, src):
        return pltpu.make_async_remote_copy(
            src_ref=csum_ref.at[pl.ds(i * vt, vt)],
            dst_ref=got_col.at[src],
            send_sem=send_col.at[i],
            recv_sem=recv_col.at[src],
            device_id=(i, c),
            device_id_type=MESH,
        )

    own_row = pltpu.make_async_copy(rsum_ref.at[pl.ds(c * vt, vt)], got_row.at[c], local_sem.at[0])
    own_col = pltpu.make_async_copy(csum_ref.at[pl.ds(r * vt, vt)], got_col.at[r], local_sem.at[1])
    own_row.start()
    own_col.start()

    def start_col(k, carry):
        row_copy(lax.rem(c + k, n_col), c).start()
        return carry

    def start_row(k, carry):
        col_copy(lax.rem(r + k, n_row), r).start()
        return carry

    lax.fori_loop(1, n_col, start_col, 0)
    lax.fori_loop(1, n_row, start_row, 0)

    def wait_col(k, carry):
        row_copy(lax.rem(c + k, n_col), c).wait_send()
        row_copy(c, lax.rem(c + n_col - k, n_col)).wait_recv()
        return carry

    def wait_row(k, carry):
        col_copy(lax.rem(r + k, n_row), r).wait_send()
        col_copy(r, lax.rem(r + n_row - k, n_row)).wait_recv()
        return carry

    lax.fori_loop(1, n_col, wait_col, 0)
    lax.fori_loop(1, n_row, wait_row, 0)
    own_row.wait()
    own_col.wait()
    out_ref[...] = base_ref[...] + jnp.sum(got_row[...], axis=0) + jnp.sum(got_col[...], axis=0)


def reduce_tiles(base_tiles, row_sum, col_sum, n_row, n_col):
    vt, k, t = base_tiles.shape
    vmem = pl.BlockSpec(memory_space=pltpu.VMEM)
    return pl.pallas_call(
        functools.partial(_reduce_kernel, n_row, n_col),
        out_shape=jax.ShapeDtypeStruct((vt, k, t), base_tiles.dtype),
        in_specs=[vmem, vmem, vmem],
        out_specs=vmem,
        scratch_shapes=[
            pltpu.VMEM((n_col, vt, k, t), jnp.float32),
            pltpu.VMEM((n_row, vt, k, t), jnp.float32),
            pltpu.SemaphoreType.DMA((n_col,)),
            pltpu.SemaphoreType.DMA((n_col,)),
            pltpu.SemaphoreType.DMA((n_row,)),
            pltpu.SemaphoreType.DMA((n_row,)),
            pltpu.SemaphoreType.DMA((2,)),
        ],
        compiler_params=pltpu.CompilerParams(collective_id=1, has_side_effects=True),
    )(base_tiles, row_sum, col_sum)


def _psum_kernel(n_row, n_col, x_ref, out_ref, got_col, mid, got_row,
                 send_col, recv_col, send_row, recv_row, local_sem):
    r = lax.axis_index("row")
    c = lax.axis_index("col")
    _barrier(n_row, n_col, r, c)

    def col_copy(j, src):
        return pltpu.make_async_remote_copy(
            src_ref=x_ref,
            dst_ref=got_col.at[src],
            send_sem=send_col.at[j],
            recv_sem=recv_col.at[src],
            device_id=(r, j),
            device_id_type=MESH,
        )

    def row_copy(i, src):
        return pltpu.make_async_remote_copy(
            src_ref=mid,
            dst_ref=got_row.at[src],
            send_sem=send_row.at[i],
            recv_sem=recv_row.at[src],
            device_id=(i, c),
            device_id_type=MESH,
        )

    own_col = pltpu.make_async_copy(x_ref, got_col.at[c], local_sem.at[0])
    own_col.start()

    def start_col(k, carry):
        col_copy(lax.rem(c + k, n_col), c).start()
        return carry

    def wait_col(k, carry):
        col_copy(lax.rem(c + k, n_col), c).wait_send()
        col_copy(c, lax.rem(c + n_col - k, n_col)).wait_recv()
        return carry

    lax.fori_loop(1, n_col, start_col, 0)
    lax.fori_loop(1, n_col, wait_col, 0)
    own_col.wait()
    mid[...] = jnp.sum(got_col[...], axis=0)

    own_row = pltpu.make_async_copy(mid, got_row.at[r], local_sem.at[1])
    own_row.start()

    def start_row(k, carry):
        row_copy(lax.rem(r + k, n_row), r).start()
        return carry

    def wait_row(k, carry):
        row_copy(lax.rem(r + k, n_row), r).wait_send()
        row_copy(r, lax.rem(r + n_row - k, n_row)).wait_recv()
        return carry

    lax.fori_loop(1, n_row, start_row, 0)
    lax.fori_loop(1, n_row, wait_row, 0)
    own_row.wait()
    out_ref[...] = jnp.sum(got_row[...], axis=0)


def psum_small(values, n_row, n_col, collective_id):
    flat = jnp.concatenate([v.reshape(-1) for v in values])
    tile = 8 * 128
    padded = -(-flat.shape[0] // tile) * tile
    packed = jnp.pad(flat, (0, padded - flat.shape[0])).reshape(-1, 128)
    s, t = packed.shape
    vmem = pl.BlockSpec(memory_space=pltpu.VMEM)
    total = pl.pallas_call(
        functools.partial(_psum_kernel, n_row, n_col),
        out_shape=jax.ShapeDtypeStruct((s, t), jnp.float32),
        in_specs=[vmem],
        out_specs=vmem,
        scratch_shapes=[
            pltpu.VMEM((n_col, s, t), jnp.float32),
            pltpu.VMEM((s, t), jnp.float32),
            pltpu.VMEM((n_row, s, t), jnp.float32),
            pltpu.SemaphoreType.DMA((n_col,)),
            pltpu.SemaphoreType.DMA((n_col,)),
            pltpu.SemaphoreType.DMA((n_row,)),
            pltpu.SemaphoreType.DMA((n_row,)),
            pltpu.SemaphoreType.DMA((2,)),
        ],
        compiler_params=pltpu.CompilerParams(collective_id=collective_id, has_side_effects=True),
    )(packed).reshape(-1)
    out, start = [], 0
    for v in values:
        out.append(total[start:start + v.size].reshape(v.shape))
        start += v.size
    return out


def _slots_kernel(group, rows_ref, cols_ref, count_ref, tiles_ref, rowv_ref, colv_ref,
                  rsum_ref, csum_ref):
    g = pl.program_id(0)

    @pl.when(g == 0)
    def _():
        rsum_ref[...] = jnp.zeros_like(rsum_ref)
        csum_ref[...] = jnp.zeros_like(csum_ref)

    for s in range(group):
        slot = g * group + s

        @pl.when(slot < count_ref[0])
        def _():
            a = rows_ref[slot]
            b = cols_ref[slot]
            block = tiles_ref[s]
            direct = lax.dot_general(
                colv_ref[b], block, (((1,), (1,)), ((), ())),
                precision=highest, preferred_element_type=jnp.float32,
            )
            rsum_ref[a] += direct
            mirror = jnp.dot(rowv_ref[a], block, precision=highest,
                             preferred_element_type=jnp.float32)
            csum_ref[b] += mirror


def slot_products(blocks, rows_here, cols_here, live_count, row_tiles, column_tiles):
    slot_count, tile, _ = blocks.shape
    group = group_width
    groups = slot_count // group

    def tile_map(g, rows, cols, count):
        last = jnp.maximum(count[0] - 1, 0) // group
        return (jnp.minimum(g, last), 0, 0)

    def whole(g, rows, cols, count):
        return (0, 0, 0)

    grid_spec = pltpu.PrefetchScalarGridSpec(
        num_scalar_prefetch=3,
        grid=(groups,),
        in_specs=[
            pl.BlockSpec((group, tile, tile), tile_map),
            pl.BlockSpec(row_tiles.shape, whole),
            pl.BlockSpec(column_tiles.shape, whole),
        ],
        out_specs=[
            pl.BlockSpec(row_tiles.shape, whole),
            pl.BlockSpec(column_tiles.shape, whole),
        ],
    )
    return pl.pallas_call(
        functools.partial(_slots_kernel, group),
        grid_spec=grid_spec,
        out_shape=(
            jax.ShapeDtypeStruct(row_tiles.shape, jnp.float32),
            jax.ShapeDtypeStruct(column_tiles.shape, jnp.float32),
        ),
        compiler_params=pltpu.CompilerParams(dimension_semantics=("arbitrary",)),
    )(rows_here, cols_here, live_count.reshape(1), blocks, row_tiles, column_tiles)


def apply_operator(vectors, diagonal, tile_values, tile_row, tile_col, counts, n_row, n_col):
    vector_count = vectors.shape[0]
    tile_size = tile_values.shape[-1]
    slot_count = tile_values.shape[2]
    blocks = tile_values.reshape(slot_count, tile_size, tile_size)
    rows_here = tile_row.reshape(slot_count)
    cols_here = tile_col.reshape(slot_count)
    live_count = counts.reshape(())
    x_tiles = vectors.reshape(vector_count, -1, tile_size).transpose(1, 0, 2)
    row_tiles, column_tiles = gather_tiles(x_tiles, n_row, n_col)
    row_sum, column_sum = slot_products(blocks, rows_here, cols_here, live_count, row_tiles, column_tiles)
    base = (diagonal[None, :] * vectors).reshape(vector_count, -1, tile_size).transpose(1, 0, 2)
    owned = reduce_tiles(base, row_sum, column_sum, n_row, n_col)
    return owned.transpose(1, 0, 2).reshape(vector_count, -1)


def dot_rows(left, right):
    return jnp.dot(left, right.T, precision=highest)


def local(n_row, n_col, tile_values, tile_row, tile_col, counts, diagonal, current, previous, previous_image):
    op = functools.partial(apply_operator, n_row=n_row, n_col=n_col)
    image = op(current, diagonal, tile_values, tile_row, tile_col, counts)
    small_gram, small_proj = psum_small(
        (dot_rows(current, current), dot_rows(current, image)), n_row, n_col, 2
    )
    factor = jnp.linalg.cholesky(small_gram)
    ritz_matrix = jax.scipy.linalg.cho_solve((factor, True), small_proj)
    residual = image - jnp.dot(ritz_matrix.T, current, precision=highest)
    residual_image = op(residual, diagonal, tile_values, tile_row, tile_col, counts)
    search_basis = jnp.concatenate([current, residual, previous], 0)
    basis_image = jnp.concatenate([image, residual_image, previous_image], 0)
    correlation, mixed_terms = psum_small(
        (dot_rows(search_basis, search_basis), dot_rows(search_basis, basis_image)), n_row, n_col, 3
    )
    pencil = 0.5 * (mixed_terms + mixed_terms.T)
    lower_factor = jnp.linalg.cholesky(correlation)
    half_solve = jax.scipy.linalg.solve_triangular(lower_factor, pencil, lower=True)
    reduced = jax.scipy.linalg.solve_triangular(lower_factor, half_solve.T, lower=True)
    return (image, residual, residual_image, reduced)


def solution(mesh):
    n_row = mesh.shape["row"]
    n_col = mesh.shape["col"]
    return jax.shard_map(
        functools.partial(local, n_row, n_col),
        mesh=mesh,
        in_specs=(
            P("row", "col", None, None, None),
            P("row", "col", None),
            P("row", "col", None),
            P("row", "col"),
            P(("row", "col")),
            P(None, ("row", "col")),
            P(None, ("row", "col")),
            P(None, ("row", "col")),
        ),
        out_specs=(P(None, ("row", "col")), P(None, ("row", "col")), P(None, ("row", "col")), P()),
        check_vma=False,
    )
```

```python
import functools

import jax
import jax.numpy as jnp
from jax import lax
from jax.experimental import pallas as pl
from jax.experimental.pallas import tpu as pltpu
from jax.sharding import PartitionSpec as P

highest = lax.Precision.HIGHEST
group_width = 8
MESH = pl.DeviceIdType.MESH


def _barrier(n_row, n_col, r, c):
    barrier = pltpu.get_barrier_semaphore()

    def greet_col(k, carry):
        pl.semaphore_signal(barrier, 1, device_id=(r, lax.rem(c + k, n_col)), device_id_type=MESH)
        return carry

    def greet_row(k, carry):
        pl.semaphore_signal(barrier, 1, device_id=(lax.rem(r + k, n_row), c), device_id_type=MESH)
        return carry

    lax.fori_loop(1, n_col, greet_col, 0)
    lax.fori_loop(1, n_row, greet_row, 0)
    pl.semaphore_wait(barrier, n_row + n_col - 2)


def _gather_kernel(n_row, n_col, x_ref, rowv_ref, colv_ref, send_row, recv_row, send_col, recv_col, local_sem):
    vt = x_ref.shape[0]
    r = lax.axis_index("row")
    c = lax.axis_index("col")
    _barrier(n_row, n_col, r, c)

    def row_copy(j, src):
        return pltpu.make_async_remote_copy(
            src_ref=x_ref,
            dst_ref=rowv_ref.at[pl.ds(src * vt, vt)],
            send_sem=send_row.at[j],
            recv_sem=recv_row.at[src],
            device_id=(r, j),
            device_id_type=MESH,
        )

    def col_copy(i, src):
        return pltpu.make_async_remote_copy(
            src_ref=x_ref,
            dst_ref=colv_ref.at[pl.ds(src * vt, vt)],
            send_sem=send_col.at[i],
            recv_sem=recv_col.at[src],
            device_id=(i, c),
            device_id_type=MESH,
        )

    own_row = pltpu.make_async_copy(x_ref, rowv_ref.at[pl.ds(c * vt, vt)], local_sem.at[0])
    own_col = pltpu.make_async_copy(x_ref, colv_ref.at[pl.ds(r * vt, vt)], local_sem.at[1])
    own_row.start()
    own_col.start()

    def start_col(k, carry):
        row_copy(lax.rem(c + k, n_col), c).start()
        return carry

    def start_row(k, carry):
        col_copy(lax.rem(r + k, n_row), r).start()
        return carry

    lax.fori_loop(1, n_col, start_col, 0)
    lax.fori_loop(1, n_row, start_row, 0)

    def wait_col(k, carry):
        row_copy(lax.rem(c + k, n_col), c).wait_send()
        row_copy(c, lax.rem(c + n_col - k, n_col)).wait_recv()
        return carry

    def wait_row(k, carry):
        col_copy(lax.rem(r + k, n_row), r).wait_send()
        col_copy(r, lax.rem(r + n_row - k, n_row)).wait_recv()
        return carry

    lax.fori_loop(1, n_col, wait_col, 0)
    lax.fori_loop(1, n_row, wait_row, 0)
    own_row.wait()
    own_col.wait()


def gather_tiles(x_tiles, n_row, n_col, collective_id):
    vt, k, t = x_tiles.shape
    vmem = pl.BlockSpec(memory_space=pltpu.VMEM)
    return pl.pallas_call(
        functools.partial(_gather_kernel, n_row, n_col),
        out_shape=(
            jax.ShapeDtypeStruct((n_col * vt, k, t), x_tiles.dtype),
            jax.ShapeDtypeStruct((n_row * vt, k, t), x_tiles.dtype),
        ),
        in_specs=[vmem],
        out_specs=(vmem, vmem),
        scratch_shapes=[
            pltpu.SemaphoreType.DMA((n_col,)),
            pltpu.SemaphoreType.DMA((n_col,)),
            pltpu.SemaphoreType.DMA((n_row,)),
            pltpu.SemaphoreType.DMA((n_row,)),
            pltpu.SemaphoreType.DMA((2,)),
        ],
        compiler_params=pltpu.CompilerParams(collective_id=collective_id, has_side_effects=True),
    )(x_tiles)


def _reduce_kernel(n_row, n_col, base_ref, rsum_ref, csum_ref, small_ref, out_ref, small_out,
                   got_row, got_col, got_small_col, mid, got_small_row,
                   send_row, recv_row, send_col, recv_col,
                   send_small_col, recv_small_col, send_small_row, recv_small_row, local_sem):
    vt = base_ref.shape[0]
    r = lax.axis_index("row")
    c = lax.axis_index("col")
    _barrier(n_row, n_col, r, c)

    def small_col_copy(j, src):
        return pltpu.make_async_remote_copy(
            src_ref=small_ref,
            dst_ref=got_small_col.at[src],
            send_sem=send_small_col.at[j],
            recv_sem=recv_small_col.at[src],
            device_id=(r, j),
            device_id_type=MESH,
        )

    def small_row_copy(i, src):
        return pltpu.make_async_remote_copy(
            src_ref=mid,
            dst_ref=got_small_row.at[src],
            send_sem=send_small_row.at[i],
            recv_sem=recv_small_row.at[src],
            device_id=(i, c),
            device_id_type=MESH,
        )

    def row_copy(j, src):
        return pltpu.make_async_remote_copy(
            src_ref=rsum_ref.at[pl.ds(j * vt, vt)],
            dst_ref=got_row.at[src],
            send_sem=send_row.at[j],
            recv_sem=recv_row.at[src],
            device_id=(r, j),
            device_id_type=MESH,
        )

    def col_copy(i, src):
        return pltpu.make_async_remote_copy(
            src_ref=csum_ref.at[pl.ds(i * vt, vt)],
            dst_ref=got_col.at[src],
            send_sem=send_col.at[i],
            recv_sem=recv_col.at[src],
            device_id=(i, c),
            device_id_type=MESH,
        )

    own_small = pltpu.make_async_copy(small_ref, got_small_col.at[c], local_sem.at[2])
    own_small.start()

    def start_small_col(k, carry):
        small_col_copy(lax.rem(c + k, n_col), c).start()
        return carry

    lax.fori_loop(1, n_col, start_small_col, 0)

    own_row = pltpu.make_async_copy(rsum_ref.at[pl.ds(c * vt, vt)], got_row.at[c], local_sem.at[0])
    own_col = pltpu.make_async_copy(csum_ref.at[pl.ds(r * vt, vt)], got_col.at[r], local_sem.at[1])
    own_row.start()
    own_col.start()

    def start_col(k, carry):
        row_copy(lax.rem(c + k, n_col), c).start()
        return carry

    def start_row(k, carry):
        col_copy(lax.rem(r + k, n_row), r).start()
        return carry

    lax.fori_loop(1, n_row, start_row, 0)
    lax.fori_loop(1, n_col, start_col, 0)

    def wait_small_col(k, carry):
        small_col_copy(lax.rem(c + k, n_col), c).wait_send()
        small_col_copy(c, lax.rem(c + n_col - k, n_col)).wait_recv()
        return carry

    lax.fori_loop(1, n_col, wait_small_col, 0)
    own_small.wait()
    mid[...] = jnp.sum(got_small_col[...], axis=0)

    own_mid = pltpu.make_async_copy(mid, got_small_row.at[r], local_sem.at[3])
    own_mid.start()

    def start_small_row(k, carry):
        small_row_copy(lax.rem(r + k, n_row), r).start()
        return carry

    lax.fori_loop(1, n_row, start_small_row, 0)

    def wait_col(k, carry):
        row_copy(lax.rem(c + k, n_col), c).wait_send()
        row_copy(c, lax.rem(c + n_col - k, n_col)).wait_recv()
        return carry

    def wait_row(k, carry):
        col_copy(lax.rem(r + k, n_row), r).wait_send()
        col_copy(r, lax.rem(r + n_row - k, n_row)).wait_recv()
        return carry

    lax.fori_loop(1, n_col, wait_col, 0)
    lax.fori_loop(1, n_row, wait_row, 0)
    own_row.wait()
    own_col.wait()
    out_ref[...] = base_ref[...] + jnp.sum(got_row[...], axis=0) + jnp.sum(got_col[...], axis=0)

    def wait_small_row(k, carry):
        small_row_copy(lax.rem(r + k, n_row), r).wait_send()
        small_row_copy(r, lax.rem(r + n_row - k, n_row)).wait_recv()
        return carry

    lax.fori_loop(1, n_row, wait_small_row, 0)
    own_mid.wait()
    small_out[...] = jnp.sum(got_small_row[...], axis=0)


def pack_small(values):
    flat = jnp.concatenate([v.reshape(-1) for v in values])
    tile = 8 * 128
    padded = -(-flat.shape[0] // tile) * tile
    return jnp.pad(flat, (0, padded - flat.shape[0])).reshape(-1, 128)


def unpack_small(total, values):
    total = total.reshape(-1)
    out, start = [], 0
    for v in values:
        out.append(total[start:start + v.size].reshape(v.shape))
        start += v.size
    return out


def reduce_tiles(base_tiles, row_sum, col_sum, small, n_row, n_col, collective_id):
    vt, k, t = base_tiles.shape
    s = small.shape[0]
    vmem = pl.BlockSpec(memory_space=pltpu.VMEM)
    return pl.pallas_call(
        functools.partial(_reduce_kernel, n_row, n_col),
        out_shape=(
            jax.ShapeDtypeStruct((vt, k, t), base_tiles.dtype),
            jax.ShapeDtypeStruct((s, 128), jnp.float32),
        ),
        in_specs=[vmem, vmem, vmem, vmem],
        out_specs=(vmem, vmem),
        scratch_shapes=[
            pltpu.VMEM((n_col, vt, k, t), jnp.float32),
            pltpu.VMEM((n_row, vt, k, t), jnp.float32),
            pltpu.VMEM((n_col, s, 128), jnp.float32),
            pltpu.VMEM((s, 128), jnp.float32),
            pltpu.VMEM((n_row, s, 128), jnp.float32),
            pltpu.SemaphoreType.DMA((n_col,)),
            pltpu.SemaphoreType.DMA((n_col,)),
            pltpu.SemaphoreType.DMA((n_row,)),
            pltpu.SemaphoreType.DMA((n_row,)),
            pltpu.SemaphoreType.DMA((n_col,)),
            pltpu.SemaphoreType.DMA((n_col,)),
            pltpu.SemaphoreType.DMA((n_row,)),
            pltpu.SemaphoreType.DMA((n_row,)),
            pltpu.SemaphoreType.DMA((4,)),
        ],
        compiler_params=pltpu.CompilerParams(collective_id=collective_id, has_side_effects=True),
    )(base_tiles, row_sum, col_sum, small)


def _slots_kernel(group, rows_k, rows_ref, cols_ref, count_ref, tiles_ref, rowv_ref, colv_ref,
                  rsum_ref, csum_ref):
    g = pl.program_id(0)

    @pl.when(g == 0)
    def _():
        rsum_ref[...] = jnp.zeros_like(rsum_ref)
        csum_ref[...] = jnp.zeros_like(csum_ref)

    for s in range(group):
        slot = g * group + s

        @pl.when(slot < count_ref[0])
        def _():
            a = rows_ref[slot]
            b = cols_ref[slot]
            block = tiles_ref[s]
            direct = lax.dot_general(
                colv_ref[b, pl.ds(0, rows_k), :], block, (((1,), (1,)), ((), ())),
                precision=highest, preferred_element_type=jnp.float32,
            )
            rsum_ref[a] += direct
            mirror = jnp.dot(rowv_ref[a, pl.ds(0, rows_k), :], block, precision=highest,
                             preferred_element_type=jnp.float32)
            csum_ref[b] += mirror


def slot_products(blocks, rows_here, cols_here, live_count, row_tiles, column_tiles, rows_k):
    slot_count, tile, _ = blocks.shape
    sums_shape = lambda v: (v.shape[0], rows_k, v.shape[2])
    group = group_width
    groups = slot_count // group

    def tile_map(g, rows, cols, count):
        last = jnp.maximum(count[0] - 1, 0) // group
        return (jnp.minimum(g, last), 0, 0)

    def whole(g, rows, cols, count):
        return (0, 0, 0)

    grid_spec = pltpu.PrefetchScalarGridSpec(
        num_scalar_prefetch=3,
        grid=(groups,),
        in_specs=[
            pl.BlockSpec((group, tile, tile), tile_map),
            pl.BlockSpec(row_tiles.shape, whole),
            pl.BlockSpec(column_tiles.shape, whole),
        ],
        out_specs=[
            pl.BlockSpec(sums_shape(row_tiles), whole),
            pl.BlockSpec(sums_shape(column_tiles), whole),
        ],
    )
    return pl.pallas_call(
        functools.partial(_slots_kernel, group, rows_k),
        grid_spec=grid_spec,
        out_shape=(
            jax.ShapeDtypeStruct(sums_shape(row_tiles), jnp.float32),
            jax.ShapeDtypeStruct(sums_shape(column_tiles), jnp.float32),
        ),
        compiler_params=pltpu.CompilerParams(dimension_semantics=("arbitrary",)),
    )(rows_here, cols_here, live_count.reshape(1), blocks, row_tiles, column_tiles)


def to_tiles(vectors, tile):
    return vectors.reshape(vectors.shape[0], -1, tile).transpose(1, 0, 2)


def from_tiles(tiles):
    return tiles.transpose(1, 0, 2).reshape(tiles.shape[1], -1)


def tile_dot(left, right):
    return jnp.einsum("tki,tli->kl", left, right, precision=highest)


def dot_rows(left, right):
    return jnp.dot(left, right.T, precision=highest)


def local(n_row, n_col, tile_values, tile_row, tile_col, counts, diagonal, current, previous, previous_image):
    k = current.shape[0]
    tile = tile_values.shape[-1]
    slot_count = tile_values.shape[2]
    blocks = tile_values.reshape(slot_count, tile, tile)
    rows_here = tile_row.reshape(slot_count)
    cols_here = tile_col.reshape(slot_count)
    live_count = counts.reshape(())

    row_cp, col_cp = gather_tiles(to_tiles(jnp.concatenate([current, previous], 0), tile), n_row, n_col, 0)
    row_sum, col_sum = slot_products(blocks, rows_here, cols_here, live_count, row_cp, col_cp, k)
    row_cur, col_cur = row_cp[:, :k], col_cp[:, :k]
    scaled = diagonal[None, :] * current
    small_gram = dot_rows(current, current)
    proj_part = dot_rows(current, scaled) + tile_dot(row_cur, row_sum) + tile_dot(col_cur, col_sum)
    image_tiles, small = reduce_tiles(
        to_tiles(scaled, tile), row_sum, col_sum, pack_small((small_gram, proj_part)), n_row, n_col, 1
    )
    image = from_tiles(image_tiles)
    small_gram, small_proj = unpack_small(small, (small_gram, proj_part))

    factor = jnp.linalg.cholesky(small_gram)
    ritz_matrix = jax.scipy.linalg.cho_solve((factor, True), small_proj)
    residual = image - jnp.dot(ritz_matrix.T, current, precision=highest)

    row_res, col_res = gather_tiles(to_tiles(residual, tile), n_row, n_col, 3)
    row_sum, col_sum = slot_products(blocks, rows_here, cols_here, live_count, row_res, col_res, k)
    search_basis = jnp.concatenate([current, residual, previous], 0)
    row_basis = jnp.concatenate([row_cur, row_res, row_cp[:, k:]], 1)
    col_basis = jnp.concatenate([col_cur, col_res, col_cp[:, k:]], 1)
    scaled = diagonal[None, :] * residual
    correlation = dot_rows(search_basis, search_basis)
    residual_part = (
        dot_rows(search_basis, scaled) + tile_dot(row_basis, row_sum) + tile_dot(col_basis, col_sum)
    )
    mixed_part = jnp.concatenate(
        [dot_rows(search_basis, image), residual_part, dot_rows(search_basis, previous_image)], 1
    )
    image_tiles, small = reduce_tiles(
        to_tiles(scaled, tile), row_sum, col_sum, pack_small((correlation, mixed_part)), n_row, n_col, 2
    )
    residual_image = from_tiles(image_tiles)
    correlation, mixed_terms = unpack_small(small, (correlation, mixed_part))
    pencil = 0.5 * (mixed_terms + mixed_terms.T)
    lower_factor = jnp.linalg.cholesky(correlation)
    half_solve = jax.scipy.linalg.solve_triangular(lower_factor, pencil, lower=True)
    reduced = jax.scipy.linalg.solve_triangular(lower_factor, half_solve.T, lower=True)
    return (image, residual, residual_image, reduced)


def solution(mesh):
    n_row = mesh.shape["row"]
    n_col = mesh.shape["col"]
    return jax.shard_map(
        functools.partial(local, n_row, n_col),
        mesh=mesh,
        in_specs=(
            P("row", "col", None, None, None),
            P("row", "col", None),
            P("row", "col", None),
            P("row", "col"),
            P(("row", "col")),
            P(None, ("row", "col")),
            P(None, ("row", "col")),
            P(None, ("row", "col")),
        ),
        out_specs=(P(None, ("row", "col")), P(None, ("row", "col")), P(None, ("row", "col")), P()),
        check_vma=False,
    )
```

```python
import functools

import jax
import jax.numpy as jnp
from jax import lax
from jax.experimental import pallas as pl
from jax.experimental.pallas import tpu as pltpu
from jax.sharding import PartitionSpec as P

highest = lax.Precision.HIGHEST
group_width = 8
MESH = pl.DeviceIdType.MESH


def _barrier(n_row, n_col, r, c):
    barrier = pltpu.get_barrier_semaphore()

    def greet_col(k, carry):
        pl.semaphore_signal(barrier, 1, device_id=(r, lax.rem(c + k, n_col)), device_id_type=MESH)
        return carry

    def greet_row(k, carry):
        pl.semaphore_signal(barrier, 1, device_id=(lax.rem(r + k, n_row), c), device_id_type=MESH)
        return carry

    lax.fori_loop(1, n_col, greet_col, 0)
    lax.fori_loop(1, n_row, greet_row, 0)
    pl.semaphore_wait(barrier, n_row + n_col - 2)


def _gather_kernel(n_row, n_col, x_ref, rowv_ref, colv_ref, send_row, recv_row, send_col, recv_col, local_sem):
    vt = x_ref.shape[0]
    r = lax.axis_index("row")
    c = lax.axis_index("col")
    _barrier(n_row, n_col, r, c)

    def row_copy(j, src):
        return pltpu.make_async_remote_copy(
            src_ref=x_ref,
            dst_ref=rowv_ref.at[pl.ds(src * vt, vt)],
            send_sem=send_row.at[j],
            recv_sem=recv_row.at[src],
            device_id=(r, j),
            device_id_type=MESH,
        )

    def col_copy(i, src):
        return pltpu.make_async_remote_copy(
            src_ref=x_ref,
            dst_ref=colv_ref.at[pl.ds(src * vt, vt)],
            send_sem=send_col.at[i],
            recv_sem=recv_col.at[src],
            device_id=(i, c),
            device_id_type=MESH,
        )

    own_row = pltpu.make_async_copy(x_ref, rowv_ref.at[pl.ds(c * vt, vt)], local_sem.at[0])
    own_col = pltpu.make_async_copy(x_ref, colv_ref.at[pl.ds(r * vt, vt)], local_sem.at[1])
    own_row.start()
    own_col.start()

    def start_col(k, carry):
        row_copy(lax.rem(c + k, n_col), c).start()
        return carry

    def start_row(k, carry):
        col_copy(lax.rem(r + k, n_row), r).start()
        return carry

    lax.fori_loop(1, n_col, start_col, 0)
    lax.fori_loop(1, n_row, start_row, 0)

    def wait_col(k, carry):
        row_copy(lax.rem(c + k, n_col), c).wait_send()
        row_copy(c, lax.rem(c + n_col - k, n_col)).wait_recv()
        return carry

    def wait_row(k, carry):
        col_copy(lax.rem(r + k, n_row), r).wait_send()
        col_copy(r, lax.rem(r + n_row - k, n_row)).wait_recv()
        return carry

    lax.fori_loop(1, n_col, wait_col, 0)
    lax.fori_loop(1, n_row, wait_row, 0)
    own_row.wait()
    own_col.wait()


def gather_tiles(x_tiles, n_row, n_col, collective_id):
    vt, k, t = x_tiles.shape
    vmem = pl.BlockSpec(memory_space=pltpu.VMEM)
    return pl.pallas_call(
        functools.partial(_gather_kernel, n_row, n_col),
        out_shape=(
            jax.ShapeDtypeStruct((n_col * vt, k, t), x_tiles.dtype),
            jax.ShapeDtypeStruct((n_row * vt, k, t), x_tiles.dtype),
        ),
        in_specs=[vmem],
        out_specs=(vmem, vmem),
        scratch_shapes=[
            pltpu.SemaphoreType.DMA((n_col,)),
            pltpu.SemaphoreType.DMA((n_col,)),
            pltpu.SemaphoreType.DMA((n_row,)),
            pltpu.SemaphoreType.DMA((n_row,)),
            pltpu.SemaphoreType.DMA((2,)),
        ],
        compiler_params=pltpu.CompilerParams(collective_id=collective_id, has_side_effects=True),
    )(x_tiles)


def _reduce_kernel(n_row, n_col, base_ref, rsum_ref, csum_ref, small_ref, out_ref, small_out,
                   got_row, got_col, got_small_col, mid, got_small_row,
                   send_row, recv_row, send_col, recv_col,
                   send_small_col, recv_small_col, send_small_row, recv_small_row, local_sem):
    vt = base_ref.shape[0]
    r = lax.axis_index("row")
    c = lax.axis_index("col")
    _barrier(n_row, n_col, r, c)

    def small_col_copy(j, src):
        return pltpu.make_async_remote_copy(
            src_ref=small_ref,
            dst_ref=got_small_col.at[src],
            send_sem=send_small_col.at[j],
            recv_sem=recv_small_col.at[src],
            device_id=(r, j),
            device_id_type=MESH,
        )

    def small_row_copy(i, src):
        return pltpu.make_async_remote_copy(
            src_ref=mid,
            dst_ref=got_small_row.at[src],
            send_sem=send_small_row.at[i],
            recv_sem=recv_small_row.at[src],
            device_id=(i, c),
            device_id_type=MESH,
        )

    def row_copy(j, src):
        return pltpu.make_async_remote_copy(
            src_ref=rsum_ref.at[pl.ds(j * vt, vt)],
            dst_ref=got_row.at[src],
            send_sem=send_row.at[j],
            recv_sem=recv_row.at[src],
            device_id=(r, j),
            device_id_type=MESH,
        )

    def col_copy(i, src):
        return pltpu.make_async_remote_copy(
            src_ref=csum_ref.at[pl.ds(i * vt, vt)],
            dst_ref=got_col.at[src],
            send_sem=send_col.at[i],
            recv_sem=recv_col.at[src],
            device_id=(i, c),
            device_id_type=MESH,
        )

    own_small = pltpu.make_async_copy(small_ref, got_small_col.at[c], local_sem.at[2])
    own_small.start()

    def start_small_col(k, carry):
        small_col_copy(lax.rem(c + k, n_col), c).start()
        return carry

    lax.fori_loop(1, n_col, start_small_col, 0)

    own_row = pltpu.make_async_copy(rsum_ref.at[pl.ds(c * vt, vt)], got_row.at[c], local_sem.at[0])
    own_col = pltpu.make_async_copy(csum_ref.at[pl.ds(r * vt, vt)], got_col.at[r], local_sem.at[1])
    own_row.start()
    own_col.start()

    def start_col(k, carry):
        row_copy(lax.rem(c + k, n_col), c).start()
        return carry

    def start_row(k, carry):
        col_copy(lax.rem(r + k, n_row), r).start()
        return carry

    lax.fori_loop(1, n_row, start_row, 0)
    lax.fori_loop(1, n_col, start_col, 0)

    def wait_small_col(k, carry):
        small_col_copy(lax.rem(c + k, n_col), c).wait_send()
        small_col_copy(c, lax.rem(c + n_col - k, n_col)).wait_recv()
        return carry

    lax.fori_loop(1, n_col, wait_small_col, 0)
    own_small.wait()
    mid[...] = jnp.sum(got_small_col[...], axis=0)

    own_mid = pltpu.make_async_copy(mid, got_small_row.at[r], local_sem.at[3])
    own_mid.start()

    def start_small_row(k, carry):
        small_row_copy(lax.rem(r + k, n_row), r).start()
        return carry

    lax.fori_loop(1, n_row, start_small_row, 0)

    def wait_col(k, carry):
        row_copy(lax.rem(c + k, n_col), c).wait_send()
        row_copy(c, lax.rem(c + n_col - k, n_col)).wait_recv()
        return carry

    def wait_row(k, carry):
        col_copy(lax.rem(r + k, n_row), r).wait_send()
        col_copy(r, lax.rem(r + n_row - k, n_row)).wait_recv()
        return carry

    lax.fori_loop(1, n_col, wait_col, 0)
    lax.fori_loop(1, n_row, wait_row, 0)
    own_row.wait()
    own_col.wait()
    out_ref[...] = base_ref[...] + jnp.sum(got_row[...], axis=0) + jnp.sum(got_col[...], axis=0)

    def wait_small_row(k, carry):
        small_row_copy(lax.rem(r + k, n_row), r).wait_send()
        small_row_copy(r, lax.rem(r + n_row - k, n_row)).wait_recv()
        return carry

    lax.fori_loop(1, n_row, wait_small_row, 0)
    own_mid.wait()
    small_out[...] = jnp.sum(got_small_row[...], axis=0)


def pack_small(values):
    flat = jnp.concatenate([v.reshape(-1) for v in values])
    tile = 8 * 128
    padded = -(-flat.shape[0] // tile) * tile
    return jnp.pad(flat, (0, padded - flat.shape[0])).reshape(-1, 128)


def unpack_small(total, values):
    total = total.reshape(-1)
    out, start = [], 0
    for v in values:
        out.append(total[start:start + v.size].reshape(v.shape))
        start += v.size
    return out


def reduce_tiles(base_tiles, row_sum, col_sum, small, n_row, n_col, collective_id):
    vt, k, t = base_tiles.shape
    s = small.shape[0]
    vmem = pl.BlockSpec(memory_space=pltpu.VMEM)
    return pl.pallas_call(
        functools.partial(_reduce_kernel, n_row, n_col),
        out_shape=(
            jax.ShapeDtypeStruct((vt, k, t), base_tiles.dtype),
            jax.ShapeDtypeStruct((s, 128), jnp.float32),
        ),
        in_specs=[vmem, vmem, vmem, vmem],
        out_specs=(vmem, vmem),
        scratch_shapes=[
            pltpu.VMEM((n_col, vt, k, t), jnp.float32),
            pltpu.VMEM((n_row, vt, k, t), jnp.float32),
            pltpu.VMEM((n_col, s, 128), jnp.float32),
            pltpu.VMEM((s, 128), jnp.float32),
            pltpu.VMEM((n_row, s, 128), jnp.float32),
            pltpu.SemaphoreType.DMA((n_col,)),
            pltpu.SemaphoreType.DMA((n_col,)),
            pltpu.SemaphoreType.DMA((n_row,)),
            pltpu.SemaphoreType.DMA((n_row,)),
            pltpu.SemaphoreType.DMA((n_col,)),
            pltpu.SemaphoreType.DMA((n_col,)),
            pltpu.SemaphoreType.DMA((n_row,)),
            pltpu.SemaphoreType.DMA((n_row,)),
            pltpu.SemaphoreType.DMA((4,)),
        ],
        compiler_params=pltpu.CompilerParams(collective_id=collective_id, has_side_effects=True),
    )(base_tiles, row_sum, col_sum, small)


def _slots_kernel(group, rows_k, rows_ref, cols_ref, count_ref, tiles_ref, rowv_ref, colv_ref,
                  rsum_ref, csum_ref):
    g = pl.program_id(0)

    @pl.when(g == 0)
    def _():
        rsum_ref[...] = jnp.zeros_like(rsum_ref)
        csum_ref[...] = jnp.zeros_like(csum_ref)

    for s in range(group):
        slot = g * group + s

        @pl.when(slot < count_ref[0])
        def _():
            a = rows_ref[slot]
            b = cols_ref[slot]
            block = split_bf16(tiles_ref[s])
            direct = dot3(split_bf16(colv_ref[b, pl.ds(0, rows_k), :]), block, (((1,), (1,)), ((), ())))
            rsum_ref[a] += direct
            mirror = dot3(split_bf16(rowv_ref[a, pl.ds(0, rows_k), :]), block, (((1,), (0,)), ((), ())))
            csum_ref[b] += mirror


def split_bf16(x):
    high = x.astype(jnp.bfloat16)
    return high, (x - high.astype(jnp.float32)).astype(jnp.bfloat16)


def dot3(left, right, dims):
    def one(x, y):
        return lax.dot_general(x, y, dims, preferred_element_type=jnp.float32)

    return one(left[0], right[0]) + (one(left[0], right[1]) + one(left[1], right[0]))


def slot_products(blocks, rows_here, cols_here, live_count, row_tiles, column_tiles, rows_k):
    slot_count, tile, _ = blocks.shape
    sums_shape = lambda v: (v.shape[0], rows_k, v.shape[2])
    group = group_width
    groups = slot_count // group

    def tile_map(g, rows, cols, count):
        last = jnp.maximum(count[0] - 1, 0) // group
        return (jnp.minimum(g, last), 0, 0)

    def whole(g, rows, cols, count):
        return (0, 0, 0)

    grid_spec = pltpu.PrefetchScalarGridSpec(
        num_scalar_prefetch=3,
        grid=(groups,),
        in_specs=[
            pl.BlockSpec((group, tile, tile), tile_map),
            pl.BlockSpec(row_tiles.shape, whole),
            pl.BlockSpec(column_tiles.shape, whole),
        ],
        out_specs=[
            pl.BlockSpec(sums_shape(row_tiles), whole),
            pl.BlockSpec(sums_shape(column_tiles), whole),
        ],
    )
    return pl.pallas_call(
        functools.partial(_slots_kernel, group, rows_k),
        grid_spec=grid_spec,
        out_shape=(
            jax.ShapeDtypeStruct(sums_shape(row_tiles), jnp.float32),
            jax.ShapeDtypeStruct(sums_shape(column_tiles), jnp.float32),
        ),
        compiler_params=pltpu.CompilerParams(dimension_semantics=("arbitrary",)),
    )(rows_here, cols_here, live_count.reshape(1), blocks, row_tiles, column_tiles)


def to_tiles(vectors, tile):
    return vectors.reshape(vectors.shape[0], -1, tile).transpose(1, 0, 2)


def from_tiles(tiles):
    return tiles.transpose(1, 0, 2).reshape(tiles.shape[1], -1)


def tile_dot(left, right):
    return jnp.einsum("tki,tli->kl", left, right, precision=highest)


def dot_rows(left, right):
    return jnp.dot(left, right.T, precision=highest)


def local(n_row, n_col, tile_values, tile_row, tile_col, counts, diagonal, current, previous, previous_image):
    k = current.shape[0]
    tile = tile_values.shape[-1]
    slot_count = tile_values.shape[2]
    blocks = tile_values.reshape(slot_count, tile, tile)
    rows_here = tile_row.reshape(slot_count)
    cols_here = tile_col.reshape(slot_count)
    live_count = counts.reshape(())

    row_cp, col_cp = gather_tiles(to_tiles(jnp.concatenate([current, previous], 0), tile), n_row, n_col, 0)
    row_sum, col_sum = slot_products(blocks, rows_here, cols_here, live_count, row_cp, col_cp, k)
    row_cur, col_cur = row_cp[:, :k], col_cp[:, :k]
    scaled = diagonal[None, :] * current
    small_gram = dot_rows(current, current)
    proj_part = dot_rows(current, scaled) + tile_dot(row_cur, row_sum) + tile_dot(col_cur, col_sum)
    image_tiles, small = reduce_tiles(
        to_tiles(scaled, tile), row_sum, col_sum, pack_small((small_gram, proj_part)), n_row, n_col, 1
    )
    image = from_tiles(image_tiles)
    small_gram, small_proj = unpack_small(small, (small_gram, proj_part))

    factor = jnp.linalg.cholesky(small_gram)
    ritz_matrix = jax.scipy.linalg.cho_solve((factor, True), small_proj)
    residual = image - jnp.dot(ritz_matrix.T, current, precision=highest)

    row_res, col_res = gather_tiles(to_tiles(residual, tile), n_row, n_col, 3)
    row_sum, col_sum = slot_products(blocks, rows_here, cols_here, live_count, row_res, col_res, k)
    search_basis = jnp.concatenate([current, residual, previous], 0)
    row_basis = jnp.concatenate([row_cur, row_res, row_cp[:, k:]], 1)
    col_basis = jnp.concatenate([col_cur, col_res, col_cp[:, k:]], 1)
    scaled = diagonal[None, :] * residual
    correlation = dot_rows(search_basis, search_basis)
    residual_part = (
        dot_rows(search_basis, scaled) + tile_dot(row_basis, row_sum) + tile_dot(col_basis, col_sum)
    )
    mixed_part = jnp.concatenate(
        [dot_rows(search_basis, image), residual_part, dot_rows(search_basis, previous_image)], 1
    )
    image_tiles, small = reduce_tiles(
        to_tiles(scaled, tile), row_sum, col_sum, pack_small((correlation, mixed_part)), n_row, n_col, 2
    )
    residual_image = from_tiles(image_tiles)
    correlation, mixed_terms = unpack_small(small, (correlation, mixed_part))
    pencil = 0.5 * (mixed_terms + mixed_terms.T)
    lower_factor = jnp.linalg.cholesky(correlation)
    half_solve = jax.scipy.linalg.solve_triangular(lower_factor, pencil, lower=True)
    reduced = jax.scipy.linalg.solve_triangular(lower_factor, half_solve.T, lower=True)
    return (image, residual, residual_image, reduced)


def solution(mesh):
    n_row = mesh.shape["row"]
    n_col = mesh.shape["col"]
    return jax.shard_map(
        functools.partial(local, n_row, n_col),
        mesh=mesh,
        in_specs=(
            P("row", "col", None, None, None),
            P("row", "col", None),
            P("row", "col", None),
            P("row", "col"),
            P(("row", "col")),
            P(None, ("row", "col")),
            P(None, ("row", "col")),
            P(None, ("row", "col")),
        ),
        out_specs=(P(None, ("row", "col")), P(None, ("row", "col")), P(None, ("row", "col")), P()),
        check_vma=False,
    )
```

```python
import functools

import jax
import jax.numpy as jnp
from jax import lax
from jax.experimental import pallas as pl
from jax.experimental.pallas import tpu as pltpu
from jax.sharding import PartitionSpec as P

highest = lax.Precision.HIGHEST
group_width = 8
MESH = pl.DeviceIdType.MESH


def _barrier(n_row, n_col, r, c):
    barrier = pltpu.get_barrier_semaphore()

    def greet_col(k, carry):
        pl.semaphore_signal(barrier, 1, device_id=(r, lax.rem(c + k, n_col)), device_id_type=MESH)
        return carry

    def greet_row(k, carry):
        pl.semaphore_signal(barrier, 1, device_id=(lax.rem(r + k, n_row), c), device_id_type=MESH)
        return carry

    lax.fori_loop(1, n_col, greet_col, 0)
    lax.fori_loop(1, n_row, greet_row, 0)
    pl.semaphore_wait(barrier, n_row + n_col - 2)


def _gather_kernel(n_row, n_col, x_ref, rowv_ref, colv_ref, send_row, recv_row, send_col, recv_col, local_sem):
    vt = x_ref.shape[0]
    r = lax.axis_index("row")
    c = lax.axis_index("col")
    _barrier(n_row, n_col, r, c)

    def row_copy(j, src):
        return pltpu.make_async_remote_copy(
            src_ref=x_ref,
            dst_ref=rowv_ref.at[pl.ds(src * vt, vt)],
            send_sem=send_row.at[j],
            recv_sem=recv_row.at[src],
            device_id=(r, j),
            device_id_type=MESH,
        )

    def col_copy(i, src):
        return pltpu.make_async_remote_copy(
            src_ref=x_ref,
            dst_ref=colv_ref.at[pl.ds(src * vt, vt)],
            send_sem=send_col.at[i],
            recv_sem=recv_col.at[src],
            device_id=(i, c),
            device_id_type=MESH,
        )

    own_row = pltpu.make_async_copy(x_ref, rowv_ref.at[pl.ds(c * vt, vt)], local_sem.at[0])
    own_col = pltpu.make_async_copy(x_ref, colv_ref.at[pl.ds(r * vt, vt)], local_sem.at[1])
    own_row.start()
    own_col.start()

    def start_col(k, carry):
        row_copy(lax.rem(c + k, n_col), c).start()
        return carry

    def start_row(k, carry):
        col_copy(lax.rem(r + k, n_row), r).start()
        return carry

    lax.fori_loop(1, n_col, start_col, 0)
    lax.fori_loop(1, n_row, start_row, 0)

    def wait_col(k, carry):
        row_copy(lax.rem(c + k, n_col), c).wait_send()
        row_copy(c, lax.rem(c + n_col - k, n_col)).wait_recv()
        return carry

    def wait_row(k, carry):
        col_copy(lax.rem(r + k, n_row), r).wait_send()
        col_copy(r, lax.rem(r + n_row - k, n_row)).wait_recv()
        return carry

    lax.fori_loop(1, n_col, wait_col, 0)
    lax.fori_loop(1, n_row, wait_row, 0)
    own_row.wait()
    own_col.wait()


def gather_tiles(x_tiles, n_row, n_col, collective_id):
    vt, k, t = x_tiles.shape
    vmem = pl.BlockSpec(memory_space=pltpu.VMEM)
    return pl.pallas_call(
        functools.partial(_gather_kernel, n_row, n_col),
        out_shape=(
            jax.ShapeDtypeStruct((n_col * vt, k, t), x_tiles.dtype),
            jax.ShapeDtypeStruct((n_row * vt, k, t), x_tiles.dtype),
        ),
        in_specs=[vmem],
        out_specs=(vmem, vmem),
        scratch_shapes=[
            pltpu.SemaphoreType.DMA((n_col,)),
            pltpu.SemaphoreType.DMA((n_col,)),
            pltpu.SemaphoreType.DMA((n_row,)),
            pltpu.SemaphoreType.DMA((n_row,)),
            pltpu.SemaphoreType.DMA((2,)),
        ],
        compiler_params=pltpu.CompilerParams(collective_id=collective_id, has_side_effects=True),
    )(x_tiles)


def _reduce_kernel(n_row, n_col, forward, base_ref, rsum_ref, csum_ref, small_ref, out_ref, small_out, *rest):
    if forward:
        img_row, img_col = rest[:2]
        rest = rest[2:]
    (got_row, got_col, got_small_col, mid, got_small_row,
     send_row, recv_row, send_col, recv_col,
     send_small_col, recv_small_col, send_small_row, recv_small_row, local_sem) = rest[:14]
    vt = base_ref.shape[0]
    r = lax.axis_index("row")
    c = lax.axis_index("col")
    _barrier(n_row, n_col, r, c)

    def small_col_copy(j, src):
        return pltpu.make_async_remote_copy(
            src_ref=small_ref,
            dst_ref=got_small_col.at[src],
            send_sem=send_small_col.at[j],
            recv_sem=recv_small_col.at[src],
            device_id=(r, j),
            device_id_type=MESH,
        )

    def small_row_copy(i, src):
        return pltpu.make_async_remote_copy(
            src_ref=mid,
            dst_ref=got_small_row.at[src],
            send_sem=send_small_row.at[i],
            recv_sem=recv_small_row.at[src],
            device_id=(i, c),
            device_id_type=MESH,
        )

    def row_copy(j, src):
        return pltpu.make_async_remote_copy(
            src_ref=rsum_ref.at[pl.ds(j * vt, vt)],
            dst_ref=got_row.at[src],
            send_sem=send_row.at[j],
            recv_sem=recv_row.at[src],
            device_id=(r, j),
            device_id_type=MESH,
        )

    def col_copy(i, src):
        return pltpu.make_async_remote_copy(
            src_ref=csum_ref.at[pl.ds(i * vt, vt)],
            dst_ref=got_col.at[src],
            send_sem=send_col.at[i],
            recv_sem=recv_col.at[src],
            device_id=(i, c),
            device_id_type=MESH,
        )

    own_small = pltpu.make_async_copy(small_ref, got_small_col.at[c], local_sem.at[2])
    own_small.start()

    def start_small_col(k, carry):
        small_col_copy(lax.rem(c + k, n_col), c).start()
        return carry

    lax.fori_loop(1, n_col, start_small_col, 0)

    own_row = pltpu.make_async_copy(rsum_ref.at[pl.ds(c * vt, vt)], got_row.at[c], local_sem.at[0])
    own_col = pltpu.make_async_copy(csum_ref.at[pl.ds(r * vt, vt)], got_col.at[r], local_sem.at[1])
    own_row.start()
    own_col.start()

    def start_col(k, carry):
        row_copy(lax.rem(c + k, n_col), c).start()
        return carry

    def start_row(k, carry):
        col_copy(lax.rem(r + k, n_row), r).start()
        return carry

    lax.fori_loop(1, n_row, start_row, 0)
    lax.fori_loop(1, n_col, start_col, 0)

    def wait_small_col(k, carry):
        small_col_copy(lax.rem(c + k, n_col), c).wait_send()
        small_col_copy(c, lax.rem(c + n_col - k, n_col)).wait_recv()
        return carry

    lax.fori_loop(1, n_col, wait_small_col, 0)
    own_small.wait()
    mid[...] = jnp.sum(got_small_col[...], axis=0)

    own_mid = pltpu.make_async_copy(mid, got_small_row.at[r], local_sem.at[3])
    own_mid.start()

    def start_small_row(k, carry):
        small_row_copy(lax.rem(r + k, n_row), r).start()
        return carry

    lax.fori_loop(1, n_row, start_small_row, 0)

    def wait_col(k, carry):
        row_copy(lax.rem(c + k, n_col), c).wait_send()
        row_copy(c, lax.rem(c + n_col - k, n_col)).wait_recv()
        return carry

    def wait_row(k, carry):
        col_copy(lax.rem(r + k, n_row), r).wait_send()
        col_copy(r, lax.rem(r + n_row - k, n_row)).wait_recv()
        return carry

    lax.fori_loop(1, n_col, wait_col, 0)
    lax.fori_loop(1, n_row, wait_row, 0)
    own_row.wait()
    own_col.wait()
    out_ref[...] = base_ref[...] + jnp.sum(got_row[...], axis=0) + jnp.sum(got_col[...], axis=0)

    if forward:
        send_fr, recv_fr, send_fc, recv_fc = rest[14:]

        def fwd_row_copy(j, src):
            return pltpu.make_async_remote_copy(
                src_ref=out_ref,
                dst_ref=img_row.at[pl.ds(src * vt, vt)],
                send_sem=send_fr.at[j],
                recv_sem=recv_fr.at[src],
                device_id=(r, j),
                device_id_type=MESH,
            )

        def fwd_col_copy(i, src):
            return pltpu.make_async_remote_copy(
                src_ref=out_ref,
                dst_ref=img_col.at[pl.ds(src * vt, vt)],
                send_sem=send_fc.at[i],
                recv_sem=recv_fc.at[src],
                device_id=(i, c),
                device_id_type=MESH,
            )

        own_fr = pltpu.make_async_copy(out_ref, img_row.at[pl.ds(c * vt, vt)], local_sem.at[4])
        own_fc = pltpu.make_async_copy(out_ref, img_col.at[pl.ds(r * vt, vt)], local_sem.at[5])
        own_fr.start()
        own_fc.start()

        def start_fr(k, carry):
            fwd_row_copy(lax.rem(c + k, n_col), c).start()
            return carry

        def start_fc(k, carry):
            fwd_col_copy(lax.rem(r + k, n_row), r).start()
            return carry

        lax.fori_loop(1, n_row, start_fc, 0)
        lax.fori_loop(1, n_col, start_fr, 0)

    def wait_small_row(k, carry):
        small_row_copy(lax.rem(r + k, n_row), r).wait_send()
        small_row_copy(r, lax.rem(r + n_row - k, n_row)).wait_recv()
        return carry

    lax.fori_loop(1, n_row, wait_small_row, 0)
    own_mid.wait()
    small_out[...] = jnp.sum(got_small_row[...], axis=0)

    if forward:
        def wait_fr(k, carry):
            fwd_row_copy(lax.rem(c + k, n_col), c).wait_send()
            fwd_row_copy(c, lax.rem(c + n_col - k, n_col)).wait_recv()
            return carry

        def wait_fc(k, carry):
            fwd_col_copy(lax.rem(r + k, n_row), r).wait_send()
            fwd_col_copy(r, lax.rem(r + n_row - k, n_row)).wait_recv()
            return carry

        lax.fori_loop(1, n_col, wait_fr, 0)
        lax.fori_loop(1, n_row, wait_fc, 0)
        own_fr.wait()
        own_fc.wait()


def pack_small(values):
    flat = jnp.concatenate([v.reshape(-1) for v in values])
    tile = 8 * 128
    padded = -(-flat.shape[0] // tile) * tile
    return jnp.pad(flat, (0, padded - flat.shape[0])).reshape(-1, 128)


def unpack_small(total, values):
    total = total.reshape(-1)
    out, start = [], 0
    for v in values:
        out.append(total[start:start + v.size].reshape(v.shape))
        start += v.size
    return out


def reduce_tiles(base_tiles, row_sum, col_sum, small, n_row, n_col, collective_id, forward=False):
    vt, k, t = base_tiles.shape
    s = small.shape[0]
    vmem = pl.BlockSpec(memory_space=pltpu.VMEM)
    out_shape = [
        jax.ShapeDtypeStruct((vt, k, t), base_tiles.dtype),
        jax.ShapeDtypeStruct((s, 128), jnp.float32),
    ]
    extra_sems = []
    if forward:
        out_shape += [
            jax.ShapeDtypeStruct((n_col * vt, k, t), base_tiles.dtype),
            jax.ShapeDtypeStruct((n_row * vt, k, t), base_tiles.dtype),
        ]
        extra_sems = [
            pltpu.SemaphoreType.DMA((n_col,)),
            pltpu.SemaphoreType.DMA((n_col,)),
            pltpu.SemaphoreType.DMA((n_row,)),
            pltpu.SemaphoreType.DMA((n_row,)),
        ]
    return pl.pallas_call(
        functools.partial(_reduce_kernel, n_row, n_col, forward),
        out_shape=tuple(out_shape),
        in_specs=[vmem, vmem, vmem, vmem],
        out_specs=tuple(vmem for _ in out_shape),
        scratch_shapes=[
            pltpu.VMEM((n_col, vt, k, t), jnp.float32),
            pltpu.VMEM((n_row, vt, k, t), jnp.float32),
            pltpu.VMEM((n_col, s, 128), jnp.float32),
            pltpu.VMEM((s, 128), jnp.float32),
            pltpu.VMEM((n_row, s, 128), jnp.float32),
            pltpu.SemaphoreType.DMA((n_col,)),
            pltpu.SemaphoreType.DMA((n_col,)),
            pltpu.SemaphoreType.DMA((n_row,)),
            pltpu.SemaphoreType.DMA((n_row,)),
            pltpu.SemaphoreType.DMA((n_col,)),
            pltpu.SemaphoreType.DMA((n_col,)),
            pltpu.SemaphoreType.DMA((n_row,)),
            pltpu.SemaphoreType.DMA((n_row,)),
            pltpu.SemaphoreType.DMA((6,)),
        ] + extra_sems,
        compiler_params=pltpu.CompilerParams(collective_id=collective_id, has_side_effects=True),
    )(base_tiles, row_sum, col_sum, small)


def _slots_kernel(group, rows_k, rows_ref, cols_ref, count_ref, tiles_ref, rowv_ref, colv_ref,
                  rsum_ref, csum_ref):
    g = pl.program_id(0)

    @pl.when(g == 0)
    def _():
        rsum_ref[...] = jnp.zeros_like(rsum_ref)
        csum_ref[...] = jnp.zeros_like(csum_ref)

    for s in range(group):
        slot = g * group + s

        @pl.when(slot < count_ref[0])
        def _():
            a = rows_ref[slot]
            b = cols_ref[slot]
            block = split_bf16(tiles_ref[s])
            direct = dot3(split_bf16(colv_ref[b, pl.ds(0, rows_k), :]), block, (((1,), (1,)), ((), ())))
            rsum_ref[a] += direct
            mirror = dot3(split_bf16(rowv_ref[a, pl.ds(0, rows_k), :]), block, (((1,), (0,)), ((), ())))
            csum_ref[b] += mirror


def split_bf16(x):
    high = x.astype(jnp.bfloat16)
    return high, (x - high.astype(jnp.float32)).astype(jnp.bfloat16)


def dot3(left, right, dims):
    def one(x, y):
        return lax.dot_general(x, y, dims, preferred_element_type=jnp.float32)

    return one(left[0], right[0]) + (one(left[0], right[1]) + one(left[1], right[0]))


def slot_products(blocks, rows_here, cols_here, live_count, row_tiles, column_tiles, rows_k):
    slot_count, tile, _ = blocks.shape
    sums_shape = lambda v: (v.shape[0], rows_k, v.shape[2])
    group = group_width
    groups = slot_count // group

    def tile_map(g, rows, cols, count):
        last = jnp.maximum(count[0] - 1, 0) // group
        return (jnp.minimum(g, last), 0, 0)

    def whole(g, rows, cols, count):
        return (0, 0, 0)

    grid_spec = pltpu.PrefetchScalarGridSpec(
        num_scalar_prefetch=3,
        grid=(groups,),
        in_specs=[
            pl.BlockSpec((group, tile, tile), tile_map),
            pl.BlockSpec(row_tiles.shape, whole),
            pl.BlockSpec(column_tiles.shape, whole),
        ],
        out_specs=[
            pl.BlockSpec(sums_shape(row_tiles), whole),
            pl.BlockSpec(sums_shape(column_tiles), whole),
        ],
    )
    return pl.pallas_call(
        functools.partial(_slots_kernel, group, rows_k),
        grid_spec=grid_spec,
        out_shape=(
            jax.ShapeDtypeStruct(sums_shape(row_tiles), jnp.float32),
            jax.ShapeDtypeStruct(sums_shape(column_tiles), jnp.float32),
        ),
        compiler_params=pltpu.CompilerParams(dimension_semantics=("arbitrary",)),
    )(rows_here, cols_here, live_count.reshape(1), blocks, row_tiles, column_tiles)


def to_tiles(vectors, tile):
    return vectors.reshape(vectors.shape[0], -1, tile).transpose(1, 0, 2)


def from_tiles(tiles):
    return tiles.transpose(1, 0, 2).reshape(tiles.shape[1], -1)


def tile_dot(left, right):
    return jnp.einsum("tki,tli->kl", left, right, precision=highest)


def dot_rows(left, right):
    return jnp.dot(left, right.T, precision=highest)


def local(n_row, n_col, tile_values, tile_row, tile_col, counts, diagonal, current, previous, previous_image):
    k = current.shape[0]
    tile = tile_values.shape[-1]
    slot_count = tile_values.shape[2]
    blocks = tile_values.reshape(slot_count, tile, tile)
    rows_here = tile_row.reshape(slot_count)
    cols_here = tile_col.reshape(slot_count)
    live_count = counts.reshape(())

    row_cp, col_cp = gather_tiles(to_tiles(jnp.concatenate([current, previous], 0), tile), n_row, n_col, 0)
    row_sum, col_sum = slot_products(blocks, rows_here, cols_here, live_count, row_cp, col_cp, k)
    row_cur, col_cur = row_cp[:, :k], col_cp[:, :k]
    scaled = diagonal[None, :] * current
    small_gram = dot_rows(current, current)
    proj_part = dot_rows(current, scaled) + tile_dot(row_cur, row_sum) + tile_dot(col_cur, col_sum)
    image_tiles, small, row_img, col_img = reduce_tiles(
        to_tiles(scaled, tile), row_sum, col_sum, pack_small((small_gram, proj_part)), n_row, n_col, 1,
        forward=True,
    )
    image = from_tiles(image_tiles)
    small_gram, small_proj = unpack_small(small, (small_gram, proj_part))

    factor = jnp.linalg.cholesky(small_gram)
    ritz_matrix = jax.scipy.linalg.cho_solve((factor, True), small_proj)
    residual = image - jnp.dot(ritz_matrix.T, current, precision=highest)

    def residual_of(img_tiles, cur_tiles):
        return img_tiles - jnp.einsum("lk,tli->tki", ritz_matrix, cur_tiles, precision=highest)

    row_res = residual_of(row_img, row_cur)
    col_res = residual_of(col_img, col_cur)
    row_sum, col_sum = slot_products(blocks, rows_here, cols_here, live_count, row_res, col_res, k)
    search_basis = jnp.concatenate([current, residual, previous], 0)
    row_basis = jnp.concatenate([row_cur, row_res, row_cp[:, k:]], 1)
    col_basis = jnp.concatenate([col_cur, col_res, col_cp[:, k:]], 1)
    scaled = diagonal[None, :] * residual
    correlation = dot_rows(search_basis, search_basis)
    residual_part = (
        dot_rows(search_basis, scaled) + tile_dot(row_basis, row_sum) + tile_dot(col_basis, col_sum)
    )
    mixed_part = jnp.concatenate(
        [dot_rows(search_basis, image), residual_part, dot_rows(search_basis, previous_image)], 1
    )
    image_tiles, small = reduce_tiles(
        to_tiles(scaled, tile), row_sum, col_sum, pack_small((correlation, mixed_part)), n_row, n_col, 2
    )
    residual_image = from_tiles(image_tiles)
    correlation, mixed_terms = unpack_small(small, (correlation, mixed_part))
    pencil = 0.5 * (mixed_terms + mixed_terms.T)
    lower_factor = jnp.linalg.cholesky(correlation)
    half_solve = jax.scipy.linalg.solve_triangular(lower_factor, pencil, lower=True)
    reduced = jax.scipy.linalg.solve_triangular(lower_factor, half_solve.T, lower=True)
    return (image, residual, residual_image, reduced)


def solution(mesh):
    n_row = mesh.shape["row"]
    n_col = mesh.shape["col"]
    return jax.shard_map(
        functools.partial(local, n_row, n_col),
        mesh=mesh,
        in_specs=(
            P("row", "col", None, None, None),
            P("row", "col", None),
            P("row", "col", None),
            P("row", "col"),
            P(("row", "col")),
            P(None, ("row", "col")),
            P(None, ("row", "col")),
            P(None, ("row", "col")),
        ),
        out_specs=(P(None, ("row", "col")), P(None, ("row", "col")), P(None, ("row", "col")), P()),
        check_vma=False,
    )
```

```python
import functools

import jax
import jax.numpy as jnp
from jax import lax
from jax.experimental import pallas as pl
from jax.experimental.pallas import tpu as pltpu
from jax.sharding import PartitionSpec as P

highest = lax.Precision.HIGHEST
group_width = 8
MESH = pl.DeviceIdType.MESH


def _barrier(n_row, n_col, r, c):
    barrier = pltpu.get_barrier_semaphore()

    def greet_col(k, carry):
        pl.semaphore_signal(barrier, 1, device_id=(r, lax.rem(c + k, n_col)), device_id_type=MESH)
        return carry

    def greet_row(k, carry):
        pl.semaphore_signal(barrier, 1, device_id=(lax.rem(r + k, n_row), c), device_id_type=MESH)
        return carry

    lax.fori_loop(1, n_col, greet_col, 0)
    lax.fori_loop(1, n_row, greet_row, 0)
    pl.semaphore_wait(barrier, n_row + n_col - 2)


def _gather_kernel(n_row, n_col, x_ref, rowv_ref, colv_ref, send_row, recv_row, send_col, recv_col, local_sem):
    vt = x_ref.shape[0]
    r = lax.axis_index("row")
    c = lax.axis_index("col")
    _barrier(n_row, n_col, r, c)

    def row_copy(j, src):
        return pltpu.make_async_remote_copy(
            src_ref=x_ref,
            dst_ref=rowv_ref.at[pl.ds(src * vt, vt)],
            send_sem=send_row.at[j],
            recv_sem=recv_row.at[src],
            device_id=(r, j),
            device_id_type=MESH,
        )

    def col_copy(i, src):
        return pltpu.make_async_remote_copy(
            src_ref=x_ref,
            dst_ref=colv_ref.at[pl.ds(src * vt, vt)],
            send_sem=send_col.at[i],
            recv_sem=recv_col.at[src],
            device_id=(i, c),
            device_id_type=MESH,
        )

    own_row = pltpu.make_async_copy(x_ref, rowv_ref.at[pl.ds(c * vt, vt)], local_sem.at[0])
    own_col = pltpu.make_async_copy(x_ref, colv_ref.at[pl.ds(r * vt, vt)], local_sem.at[1])
    own_row.start()
    own_col.start()

    def start_col(k, carry):
        row_copy(lax.rem(c + k, n_col), c).start()
        return carry

    def start_row(k, carry):
        col_copy(lax.rem(r + k, n_row), r).start()
        return carry

    lax.fori_loop(1, n_col, start_col, 0)
    lax.fori_loop(1, n_row, start_row, 0)

    def wait_col(k, carry):
        row_copy(lax.rem(c + k, n_col), c).wait_send()
        row_copy(c, lax.rem(c + n_col - k, n_col)).wait_recv()
        return carry

    def wait_row(k, carry):
        col_copy(lax.rem(r + k, n_row), r).wait_send()
        col_copy(r, lax.rem(r + n_row - k, n_row)).wait_recv()
        return carry

    lax.fori_loop(1, n_col, wait_col, 0)
    lax.fori_loop(1, n_row, wait_row, 0)
    own_row.wait()
    own_col.wait()


def gather_tiles(x_tiles, n_row, n_col, collective_id):
    vt, k, t = x_tiles.shape
    vmem = pl.BlockSpec(memory_space=pltpu.VMEM)
    return pl.pallas_call(
        functools.partial(_gather_kernel, n_row, n_col),
        out_shape=(
            jax.ShapeDtypeStruct((n_col * vt, k, t), x_tiles.dtype),
            jax.ShapeDtypeStruct((n_row * vt, k, t), x_tiles.dtype),
        ),
        in_specs=[vmem],
        out_specs=(vmem, vmem),
        scratch_shapes=[
            pltpu.SemaphoreType.DMA((n_col,)),
            pltpu.SemaphoreType.DMA((n_col,)),
            pltpu.SemaphoreType.DMA((n_row,)),
            pltpu.SemaphoreType.DMA((n_row,)),
            pltpu.SemaphoreType.DMA((2,)),
        ],
        compiler_params=pltpu.CompilerParams(collective_id=collective_id, has_side_effects=True),
    )(x_tiles)


def _reduce_kernel(n_row, n_col, forward, base_ref, rsum_ref, csum_ref, small_ref, out_ref, small_out, *rest):
    if forward:
        img_row, img_col = rest[:2]
        rest = rest[2:]
    (got_row, got_col, got_small_col, mid, got_small_row,
     send_row, recv_row, send_col, recv_col,
     send_small_col, recv_small_col, send_small_row, recv_small_row, local_sem) = rest[:14]
    vt = base_ref.shape[0]
    r = lax.axis_index("row")
    c = lax.axis_index("col")
    _barrier(n_row, n_col, r, c)

    def small_col_copy(j, src):
        return pltpu.make_async_remote_copy(
            src_ref=small_ref,
            dst_ref=got_small_col.at[src],
            send_sem=send_small_col.at[j],
            recv_sem=recv_small_col.at[src],
            device_id=(r, j),
            device_id_type=MESH,
        )

    def small_row_copy(i, src):
        return pltpu.make_async_remote_copy(
            src_ref=mid,
            dst_ref=got_small_row.at[src],
            send_sem=send_small_row.at[i],
            recv_sem=recv_small_row.at[src],
            device_id=(i, c),
            device_id_type=MESH,
        )

    def row_copy(j, src):
        return pltpu.make_async_remote_copy(
            src_ref=rsum_ref.at[pl.ds(j * vt, vt)],
            dst_ref=got_row.at[src],
            send_sem=send_row.at[j],
            recv_sem=recv_row.at[src],
            device_id=(r, j),
            device_id_type=MESH,
        )

    def col_copy(i, src):
        return pltpu.make_async_remote_copy(
            src_ref=csum_ref.at[pl.ds(i * vt, vt)],
            dst_ref=got_col.at[src],
            send_sem=send_col.at[i],
            recv_sem=recv_col.at[src],
            device_id=(i, c),
            device_id_type=MESH,
        )

    own_small = pltpu.make_async_copy(small_ref, got_small_col.at[c], local_sem.at[2])
    own_small.start()

    def start_small_col(k, carry):
        small_col_copy(lax.rem(c + k, n_col), c).start()
        return carry

    lax.fori_loop(1, n_col, start_small_col, 0)

    own_row = pltpu.make_async_copy(rsum_ref.at[pl.ds(c * vt, vt)], got_row.at[c], local_sem.at[0])
    own_col = pltpu.make_async_copy(csum_ref.at[pl.ds(r * vt, vt)], got_col.at[r], local_sem.at[1])
    own_row.start()
    own_col.start()

    def start_col(k, carry):
        row_copy(lax.rem(c + k, n_col), c).start()
        return carry

    def start_row(k, carry):
        col_copy(lax.rem(r + k, n_row), r).start()
        return carry

    lax.fori_loop(1, n_row, start_row, 0)
    lax.fori_loop(1, n_col, start_col, 0)

    def wait_small_col(k, carry):
        small_col_copy(lax.rem(c + k, n_col), c).wait_send()
        small_col_copy(c, lax.rem(c + n_col - k, n_col)).wait_recv()
        return carry

    lax.fori_loop(1, n_col, wait_small_col, 0)
    own_small.wait()
    mid[...] = jnp.sum(got_small_col[...], axis=0)

    own_mid = pltpu.make_async_copy(mid, got_small_row.at[r], local_sem.at[3])
    own_mid.start()

    def start_small_row(k, carry):
        small_row_copy(lax.rem(r + k, n_row), r).start()
        return carry

    lax.fori_loop(1, n_row, start_small_row, 0)

    def wait_col(k, carry):
        row_copy(lax.rem(c + k, n_col), c).wait_send()
        row_copy(c, lax.rem(c + n_col - k, n_col)).wait_recv()
        return carry

    def wait_row(k, carry):
        col_copy(lax.rem(r + k, n_row), r).wait_send()
        col_copy(r, lax.rem(r + n_row - k, n_row)).wait_recv()
        return carry

    lax.fori_loop(1, n_col, wait_col, 0)
    lax.fori_loop(1, n_row, wait_row, 0)
    own_row.wait()
    own_col.wait()
    out_ref[...] = base_ref[...] + jnp.sum(got_row[...], axis=0) + jnp.sum(got_col[...], axis=0)

    if forward:
        send_fr, recv_fr, send_fc, recv_fc = rest[14:]

        def fwd_row_copy(j, src):
            return pltpu.make_async_remote_copy(
                src_ref=out_ref,
                dst_ref=img_row.at[pl.ds(src * vt, vt)],
                send_sem=send_fr.at[j],
                recv_sem=recv_fr.at[src],
                device_id=(r, j),
                device_id_type=MESH,
            )

        def fwd_col_copy(i, src):
            return pltpu.make_async_remote_copy(
                src_ref=out_ref,
                dst_ref=img_col.at[pl.ds(src * vt, vt)],
                send_sem=send_fc.at[i],
                recv_sem=recv_fc.at[src],
                device_id=(i, c),
                device_id_type=MESH,
            )

        own_fr = pltpu.make_async_copy(out_ref, img_row.at[pl.ds(c * vt, vt)], local_sem.at[4])
        own_fc = pltpu.make_async_copy(out_ref, img_col.at[pl.ds(r * vt, vt)], local_sem.at[5])
        own_fr.start()
        own_fc.start()

        def start_fr(k, carry):
            fwd_row_copy(lax.rem(c + k, n_col), c).start()
            return carry

        def start_fc(k, carry):
            fwd_col_copy(lax.rem(r + k, n_row), r).start()
            return carry

        lax.fori_loop(1, n_row, start_fc, 0)
        lax.fori_loop(1, n_col, start_fr, 0)

    def wait_small_row(k, carry):
        small_row_copy(lax.rem(r + k, n_row), r).wait_send()
        small_row_copy(r, lax.rem(r + n_row - k, n_row)).wait_recv()
        return carry

    lax.fori_loop(1, n_row, wait_small_row, 0)
    own_mid.wait()
    small_out[...] = jnp.sum(got_small_row[...], axis=0)

    if forward:
        def wait_fr(k, carry):
            fwd_row_copy(lax.rem(c + k, n_col), c).wait_send()
            fwd_row_copy(c, lax.rem(c + n_col - k, n_col)).wait_recv()
            return carry

        def wait_fc(k, carry):
            fwd_col_copy(lax.rem(r + k, n_row), r).wait_send()
            fwd_col_copy(r, lax.rem(r + n_row - k, n_row)).wait_recv()
            return carry

        lax.fori_loop(1, n_col, wait_fr, 0)
        lax.fori_loop(1, n_row, wait_fc, 0)
        own_fr.wait()
        own_fc.wait()


def pack_small(values):
    flat = jnp.concatenate([v.reshape(-1) for v in values])
    tile = 8 * 128
    padded = -(-flat.shape[0] // tile) * tile
    return jnp.pad(flat, (0, padded - flat.shape[0])).reshape(-1, 128)


def unpack_small(total, values):
    total = total.reshape(-1)
    out, start = [], 0
    for v in values:
        out.append(total[start:start + v.size].reshape(v.shape))
        start += v.size
    return out


def reduce_tiles(base_tiles, row_sum, col_sum, small, n_row, n_col, collective_id, forward=False):
    vt, k, t = base_tiles.shape
    s = small.shape[0]
    vmem = pl.BlockSpec(memory_space=pltpu.VMEM)
    out_shape = [
        jax.ShapeDtypeStruct((vt, k, t), base_tiles.dtype),
        jax.ShapeDtypeStruct((s, 128), jnp.float32),
    ]
    extra_sems = []
    if forward:
        out_shape += [
            jax.ShapeDtypeStruct((n_col * vt, k, t), base_tiles.dtype),
            jax.ShapeDtypeStruct((n_row * vt, k, t), base_tiles.dtype),
        ]
        extra_sems = [
            pltpu.SemaphoreType.DMA((n_col,)),
            pltpu.SemaphoreType.DMA((n_col,)),
            pltpu.SemaphoreType.DMA((n_row,)),
            pltpu.SemaphoreType.DMA((n_row,)),
        ]
    return pl.pallas_call(
        functools.partial(_reduce_kernel, n_row, n_col, forward),
        out_shape=tuple(out_shape),
        in_specs=[vmem, vmem, vmem, vmem],
        out_specs=tuple(vmem for _ in out_shape),
        scratch_shapes=[
            pltpu.VMEM((n_col, vt, k, t), jnp.float32),
            pltpu.VMEM((n_row, vt, k, t), jnp.float32),
            pltpu.VMEM((n_col, s, 128), jnp.float32),
            pltpu.VMEM((s, 128), jnp.float32),
            pltpu.VMEM((n_row, s, 128), jnp.float32),
            pltpu.SemaphoreType.DMA((n_col,)),
            pltpu.SemaphoreType.DMA((n_col,)),
            pltpu.SemaphoreType.DMA((n_row,)),
            pltpu.SemaphoreType.DMA((n_row,)),
            pltpu.SemaphoreType.DMA((n_col,)),
            pltpu.SemaphoreType.DMA((n_col,)),
            pltpu.SemaphoreType.DMA((n_row,)),
            pltpu.SemaphoreType.DMA((n_row,)),
            pltpu.SemaphoreType.DMA((6,)),
        ] + extra_sems,
        compiler_params=pltpu.CompilerParams(collective_id=collective_id, has_side_effects=True),
    )(base_tiles, row_sum, col_sum, small)


def _slots_kernel(group, rows_k, rows_ref, cols_ref, count_ref, tiles_ref, rowv_ref, colv_ref,
                  rsum_ref, csum_ref):
    g = pl.program_id(0)

    @pl.when(g == 0)
    def _():
        rsum_ref[...] = jnp.zeros_like(rsum_ref)
        csum_ref[...] = jnp.zeros_like(csum_ref)

    for s in range(group):
        slot = g * group + s

        @pl.when(slot < count_ref[0])
        def _():
            a = rows_ref[slot]
            b = cols_ref[slot]
            block = split_bf16(tiles_ref[s])
            direct = dot3(split_bf16(colv_ref[b, pl.ds(0, rows_k), :]), block, (((1,), (1,)), ((), ())))
            rsum_ref[a] += direct
            mirror = dot3(split_bf16(rowv_ref[a, pl.ds(0, rows_k), :]), block, (((1,), (0,)), ((), ())))
            csum_ref[b] += mirror


def split_bf16(x):
    high = x.astype(jnp.bfloat16)
    return high, (x - high.astype(jnp.float32)).astype(jnp.bfloat16)


def dot3(left, right, dims):
    def one(x, y):
        return lax.dot_general(x, y, dims, preferred_element_type=jnp.float32)

    rows = left[0].shape[0]
    both = one(jnp.concatenate([left[0], left[1]], axis=0), right[0])
    return both[:rows] + (both[rows:] + one(left[0], right[1]))


def slot_products(blocks, rows_here, cols_here, live_count, row_tiles, column_tiles, rows_k):
    slot_count, tile, _ = blocks.shape
    sums_shape = lambda v: (v.shape[0], rows_k, v.shape[2])
    group = group_width
    groups = slot_count // group

    def tile_map(g, rows, cols, count):
        last = jnp.maximum(count[0] - 1, 0) // group
        return (jnp.minimum(g, last), 0, 0)

    def whole(g, rows, cols, count):
        return (0, 0, 0)

    grid_spec = pltpu.PrefetchScalarGridSpec(
        num_scalar_prefetch=3,
        grid=(groups,),
        in_specs=[
            pl.BlockSpec((group, tile, tile), tile_map),
            pl.BlockSpec(row_tiles.shape, whole),
            pl.BlockSpec(column_tiles.shape, whole),
        ],
        out_specs=[
            pl.BlockSpec(sums_shape(row_tiles), whole),
            pl.BlockSpec(sums_shape(column_tiles), whole),
        ],
    )
    return pl.pallas_call(
        functools.partial(_slots_kernel, group, rows_k),
        grid_spec=grid_spec,
        out_shape=(
            jax.ShapeDtypeStruct(sums_shape(row_tiles), jnp.float32),
            jax.ShapeDtypeStruct(sums_shape(column_tiles), jnp.float32),
        ),
        compiler_params=pltpu.CompilerParams(dimension_semantics=("arbitrary",)),
    )(rows_here, cols_here, live_count.reshape(1), blocks, row_tiles, column_tiles)


def to_tiles(vectors, tile):
    return vectors.reshape(vectors.shape[0], -1, tile).transpose(1, 0, 2)


def from_tiles(tiles):
    return tiles.transpose(1, 0, 2).reshape(tiles.shape[1], -1)


def tile_dot(left, right):
    return jnp.einsum("tki,tli->kl", left, right, precision=highest)


def dot_rows(left, right):
    return jnp.dot(left, right.T, precision=highest)


def local(n_row, n_col, tile_values, tile_row, tile_col, counts, diagonal, current, previous, previous_image):
    k = current.shape[0]
    tile = tile_values.shape[-1]
    slot_count = tile_values.shape[2]
    blocks = tile_values.reshape(slot_count, tile, tile)
    rows_here = tile_row.reshape(slot_count)
    cols_here = tile_col.reshape(slot_count)
    live_count = counts.reshape(())

    row_cp, col_cp = gather_tiles(to_tiles(jnp.concatenate([current, previous], 0), tile), n_row, n_col, 0)
    row_sum, col_sum = slot_products(blocks, rows_here, cols_here, live_count, row_cp, col_cp, k)
    row_cur, col_cur = row_cp[:, :k], col_cp[:, :k]
    scaled = diagonal[None, :] * current
    small_gram = dot_rows(current, current)
    proj_part = dot_rows(current, scaled) + tile_dot(row_cur, row_sum) + tile_dot(col_cur, col_sum)
    image_tiles, small, row_img, col_img = reduce_tiles(
        to_tiles(scaled, tile), row_sum, col_sum, pack_small((small_gram, proj_part)), n_row, n_col, 1,
        forward=True,
    )
    image = from_tiles(image_tiles)
    small_gram, small_proj = unpack_small(small, (small_gram, proj_part))

    factor = jnp.linalg.cholesky(small_gram)
    ritz_matrix = jax.scipy.linalg.cho_solve((factor, True), small_proj)
    residual = image - jnp.dot(ritz_matrix.T, current, precision=highest)

    def residual_of(img_tiles, cur_tiles):
        fitted = sum(ritz_matrix[l][None, :, None] * cur_tiles[:, l:l + 1, :] for l in range(k))
        return img_tiles - fitted

    row_res = residual_of(row_img, row_cur)
    col_res = residual_of(col_img, col_cur)
    row_sum, col_sum = slot_products(blocks, rows_here, cols_here, live_count, row_res, col_res, k)
    search_basis = jnp.concatenate([current, residual, previous], 0)
    row_basis = jnp.concatenate([row_cur, row_res, row_cp[:, k:]], 1)
    col_basis = jnp.concatenate([col_cur, col_res, col_cp[:, k:]], 1)
    scaled = diagonal[None, :] * residual
    correlation = dot_rows(search_basis, search_basis)
    residual_part = (
        dot_rows(search_basis, scaled) + tile_dot(row_basis, row_sum) + tile_dot(col_basis, col_sum)
    )
    mixed_part = jnp.concatenate(
        [dot_rows(search_basis, image), residual_part, dot_rows(search_basis, previous_image)], 1
    )
    image_tiles, small = reduce_tiles(
        to_tiles(scaled, tile), row_sum, col_sum, pack_small((correlation, mixed_part)), n_row, n_col, 2
    )
    residual_image = from_tiles(image_tiles)
    correlation, mixed_terms = unpack_small(small, (correlation, mixed_part))
    pencil = 0.5 * (mixed_terms + mixed_terms.T)
    lower_factor = jnp.linalg.cholesky(correlation)
    half_solve = jax.scipy.linalg.solve_triangular(lower_factor, pencil, lower=True)
    reduced = jax.scipy.linalg.solve_triangular(lower_factor, half_solve.T, lower=True)
    return (image, residual, residual_image, reduced)


def solution(mesh):
    n_row = mesh.shape["row"]
    n_col = mesh.shape["col"]
    return jax.shard_map(
        functools.partial(local, n_row, n_col),
        mesh=mesh,
        in_specs=(
            P("row", "col", None, None, None),
            P("row", "col", None),
            P("row", "col", None),
            P("row", "col"),
            P(("row", "col")),
            P(None, ("row", "col")),
            P(None, ("row", "col")),
            P(None, ("row", "col")),
        ),
        out_specs=(P(None, ("row", "col")), P(None, ("row", "col")), P(None, ("row", "col")), P()),
        check_vma=False,
    )
```

```python
import functools

import jax
import jax.numpy as jnp
from jax import lax
from jax.experimental import pallas as pl
from jax.experimental.pallas import tpu as pltpu
from jax.sharding import PartitionSpec as P

highest = lax.Precision.HIGHEST
group_width = 8
MESH = pl.DeviceIdType.MESH


def _barrier(n_row, n_col, r, c):
    barrier = pltpu.get_barrier_semaphore()

    def greet_col(k, carry):
        pl.semaphore_signal(barrier, 1, device_id=(r, lax.rem(c + k, n_col)), device_id_type=MESH)
        return carry

    def greet_row(k, carry):
        pl.semaphore_signal(barrier, 1, device_id=(lax.rem(r + k, n_row), c), device_id_type=MESH)
        return carry

    lax.fori_loop(1, n_col, greet_col, 0)
    lax.fori_loop(1, n_row, greet_row, 0)
    pl.semaphore_wait(barrier, n_row + n_col - 2)


def _gather_kernel(n_row, n_col, x_ref, rowv_ref, colv_ref, send_row, recv_row, send_col, recv_col, local_sem):
    vt = x_ref.shape[0]
    r = lax.axis_index("row")
    c = lax.axis_index("col")
    _barrier(n_row, n_col, r, c)

    def row_copy(j, src):
        return pltpu.make_async_remote_copy(
            src_ref=x_ref,
            dst_ref=rowv_ref.at[pl.ds(src * vt, vt)],
            send_sem=send_row.at[j],
            recv_sem=recv_row.at[src],
            device_id=(r, j),
            device_id_type=MESH,
        )

    def col_copy(i, src):
        return pltpu.make_async_remote_copy(
            src_ref=x_ref,
            dst_ref=colv_ref.at[pl.ds(src * vt, vt)],
            send_sem=send_col.at[i],
            recv_sem=recv_col.at[src],
            device_id=(i, c),
            device_id_type=MESH,
        )

    own_row = pltpu.make_async_copy(x_ref, rowv_ref.at[pl.ds(c * vt, vt)], local_sem.at[0])
    own_col = pltpu.make_async_copy(x_ref, colv_ref.at[pl.ds(r * vt, vt)], local_sem.at[1])
    own_row.start()
    own_col.start()

    def start_col(k, carry):
        row_copy(lax.rem(c + k, n_col), c).start()
        return carry

    def start_row(k, carry):
        col_copy(lax.rem(r + k, n_row), r).start()
        return carry

    lax.fori_loop(1, n_col, start_col, 0)
    lax.fori_loop(1, n_row, start_row, 0)

    def wait_col(k, carry):
        row_copy(lax.rem(c + k, n_col), c).wait_send()
        row_copy(c, lax.rem(c + n_col - k, n_col)).wait_recv()
        return carry

    def wait_row(k, carry):
        col_copy(lax.rem(r + k, n_row), r).wait_send()
        col_copy(r, lax.rem(r + n_row - k, n_row)).wait_recv()
        return carry

    lax.fori_loop(1, n_col, wait_col, 0)
    lax.fori_loop(1, n_row, wait_row, 0)
    own_row.wait()
    own_col.wait()


def gather_tiles(x_tiles, n_row, n_col, collective_id):
    vt, k, t = x_tiles.shape
    vmem = pl.BlockSpec(memory_space=pltpu.VMEM)
    return pl.pallas_call(
        functools.partial(_gather_kernel, n_row, n_col),
        out_shape=(
            jax.ShapeDtypeStruct((n_col * vt, k, t), x_tiles.dtype),
            jax.ShapeDtypeStruct((n_row * vt, k, t), x_tiles.dtype),
        ),
        in_specs=[vmem],
        out_specs=(vmem, vmem),
        scratch_shapes=[
            pltpu.SemaphoreType.DMA((n_col,)),
            pltpu.SemaphoreType.DMA((n_col,)),
            pltpu.SemaphoreType.DMA((n_row,)),
            pltpu.SemaphoreType.DMA((n_row,)),
            pltpu.SemaphoreType.DMA((2,)),
        ],
        compiler_params=pltpu.CompilerParams(collective_id=collective_id, has_side_effects=True),
    )(x_tiles)


def _reduce_kernel(n_row, n_col, forward, base_ref, rsum_ref, csum_ref, small_ref, out_ref, small_out, *rest):
    if forward:
        img_row, img_col = rest[:2]
        rest = rest[2:]
    (got_row, got_col, got_small_col, mid, got_small_row,
     send_row, recv_row, send_col, recv_col,
     send_small_col, recv_small_col, send_small_row, recv_small_row, local_sem) = rest[:14]
    vt = base_ref.shape[0]
    r = lax.axis_index("row")
    c = lax.axis_index("col")
    _barrier(n_row, n_col, r, c)

    def small_col_copy(j, src):
        return pltpu.make_async_remote_copy(
            src_ref=small_ref,
            dst_ref=got_small_col.at[src],
            send_sem=send_small_col.at[j],
            recv_sem=recv_small_col.at[src],
            device_id=(r, j),
            device_id_type=MESH,
        )

    def small_row_copy(i, src):
        return pltpu.make_async_remote_copy(
            src_ref=mid,
            dst_ref=got_small_row.at[src],
            send_sem=send_small_row.at[i],
            recv_sem=recv_small_row.at[src],
            device_id=(i, c),
            device_id_type=MESH,
        )

    def row_copy(j, src):
        return pltpu.make_async_remote_copy(
            src_ref=rsum_ref.at[pl.ds(j * vt, vt)],
            dst_ref=got_row.at[src],
            send_sem=send_row.at[j],
            recv_sem=recv_row.at[src],
            device_id=(r, j),
            device_id_type=MESH,
        )

    def col_copy(i, src):
        return pltpu.make_async_remote_copy(
            src_ref=csum_ref.at[pl.ds(i * vt, vt)],
            dst_ref=got_col.at[src],
            send_sem=send_col.at[i],
            recv_sem=recv_col.at[src],
            device_id=(i, c),
            device_id_type=MESH,
        )

    own_small = pltpu.make_async_copy(small_ref, got_small_col.at[c], local_sem.at[2])
    own_small.start()

    def start_small_col(k, carry):
        small_col_copy(lax.rem(c + k, n_col), c).start()
        return carry

    lax.fori_loop(1, n_col, start_small_col, 0)

    own_row = pltpu.make_async_copy(rsum_ref.at[pl.ds(c * vt, vt)], got_row.at[c], local_sem.at[0])
    own_col = pltpu.make_async_copy(csum_ref.at[pl.ds(r * vt, vt)], got_col.at[r], local_sem.at[1])
    own_row.start()
    own_col.start()

    def start_col(k, carry):
        row_copy(lax.rem(c + k, n_col), c).start()
        return carry

    def start_row(k, carry):
        col_copy(lax.rem(r + k, n_row), r).start()
        return carry

    lax.fori_loop(1, n_row, start_row, 0)
    lax.fori_loop(1, n_col, start_col, 0)

    def wait_small_col(k, carry):
        small_col_copy(lax.rem(c + k, n_col), c).wait_send()
        small_col_copy(c, lax.rem(c + n_col - k, n_col)).wait_recv()
        return carry

    lax.fori_loop(1, n_col, wait_small_col, 0)
    own_small.wait()
    mid[...] = jnp.sum(got_small_col[...], axis=0)

    own_mid = pltpu.make_async_copy(mid, got_small_row.at[r], local_sem.at[3])
    own_mid.start()

    def start_small_row(k, carry):
        small_row_copy(lax.rem(r + k, n_row), r).start()
        return carry

    lax.fori_loop(1, n_row, start_small_row, 0)

    def wait_col(k, carry):
        row_copy(lax.rem(c + k, n_col), c).wait_send()
        row_copy(c, lax.rem(c + n_col - k, n_col)).wait_recv()
        return carry

    def wait_row(k, carry):
        col_copy(lax.rem(r + k, n_row), r).wait_send()
        col_copy(r, lax.rem(r + n_row - k, n_row)).wait_recv()
        return carry

    lax.fori_loop(1, n_col, wait_col, 0)
    lax.fori_loop(1, n_row, wait_row, 0)
    own_row.wait()
    own_col.wait()
    out_ref[...] = base_ref[...] + jnp.sum(got_row[...], axis=0) + jnp.sum(got_col[...], axis=0)

    if forward:
        send_fr, recv_fr, send_fc, recv_fc = rest[14:]

        def fwd_row_copy(j, src):
            return pltpu.make_async_remote_copy(
                src_ref=out_ref,
                dst_ref=img_row.at[pl.ds(src * vt, vt)],
                send_sem=send_fr.at[j],
                recv_sem=recv_fr.at[src],
                device_id=(r, j),
                device_id_type=MESH,
            )

        def fwd_col_copy(i, src):
            return pltpu.make_async_remote_copy(
                src_ref=out_ref,
                dst_ref=img_col.at[pl.ds(src * vt, vt)],
                send_sem=send_fc.at[i],
                recv_sem=recv_fc.at[src],
                device_id=(i, c),
                device_id_type=MESH,
            )

        own_fr = pltpu.make_async_copy(out_ref, img_row.at[pl.ds(c * vt, vt)], local_sem.at[4])
        own_fc = pltpu.make_async_copy(out_ref, img_col.at[pl.ds(r * vt, vt)], local_sem.at[5])
        own_fr.start()
        own_fc.start()

        def start_fr(k, carry):
            fwd_row_copy(lax.rem(c + k, n_col), c).start()
            return carry

        def start_fc(k, carry):
            fwd_col_copy(lax.rem(r + k, n_row), r).start()
            return carry

        lax.fori_loop(1, n_row, start_fc, 0)
        lax.fori_loop(1, n_col, start_fr, 0)

    def wait_small_row(k, carry):
        small_row_copy(lax.rem(r + k, n_row), r).wait_send()
        small_row_copy(r, lax.rem(r + n_row - k, n_row)).wait_recv()
        return carry

    lax.fori_loop(1, n_row, wait_small_row, 0)
    own_mid.wait()
    small_out[...] = jnp.sum(got_small_row[...], axis=0)

    if forward:
        def wait_fr(k, carry):
            fwd_row_copy(lax.rem(c + k, n_col), c).wait_send()
            fwd_row_copy(c, lax.rem(c + n_col - k, n_col)).wait_recv()
            return carry

        def wait_fc(k, carry):
            fwd_col_copy(lax.rem(r + k, n_row), r).wait_send()
            fwd_col_copy(r, lax.rem(r + n_row - k, n_row)).wait_recv()
            return carry

        lax.fori_loop(1, n_col, wait_fr, 0)
        lax.fori_loop(1, n_row, wait_fc, 0)
        own_fr.wait()
        own_fc.wait()


def pack_small(values):
    flat = jnp.concatenate([v.reshape(-1) for v in values])
    tile = 8 * 128
    padded = -(-flat.shape[0] // tile) * tile
    return jnp.pad(flat, (0, padded - flat.shape[0])).reshape(-1, 128)


def unpack_small(total, values):
    total = total.reshape(-1)
    out, start = [], 0
    for v in values:
        out.append(total[start:start + v.size].reshape(v.shape))
        start += v.size
    return out


def reduce_tiles(base_tiles, row_sum, col_sum, small, n_row, n_col, collective_id, forward=False):
    vt, k, t = base_tiles.shape
    s = small.shape[0]
    vmem = pl.BlockSpec(memory_space=pltpu.VMEM)
    out_shape = [
        jax.ShapeDtypeStruct((vt, k, t), base_tiles.dtype),
        jax.ShapeDtypeStruct((s, 128), jnp.float32),
    ]
    extra_sems = []
    if forward:
        out_shape += [
            jax.ShapeDtypeStruct((n_col * vt, k, t), base_tiles.dtype),
            jax.ShapeDtypeStruct((n_row * vt, k, t), base_tiles.dtype),
        ]
        extra_sems = [
            pltpu.SemaphoreType.DMA((n_col,)),
            pltpu.SemaphoreType.DMA((n_col,)),
            pltpu.SemaphoreType.DMA((n_row,)),
            pltpu.SemaphoreType.DMA((n_row,)),
        ]
    return pl.pallas_call(
        functools.partial(_reduce_kernel, n_row, n_col, forward),
        out_shape=tuple(out_shape),
        in_specs=[vmem, vmem, vmem, vmem],
        out_specs=tuple(vmem for _ in out_shape),
        scratch_shapes=[
            pltpu.VMEM((n_col, vt, k, t), jnp.float32),
            pltpu.VMEM((n_row, vt, k, t), jnp.float32),
            pltpu.VMEM((n_col, s, 128), jnp.float32),
            pltpu.VMEM((s, 128), jnp.float32),
            pltpu.VMEM((n_row, s, 128), jnp.float32),
            pltpu.SemaphoreType.DMA((n_col,)),
            pltpu.SemaphoreType.DMA((n_col,)),
            pltpu.SemaphoreType.DMA((n_row,)),
            pltpu.SemaphoreType.DMA((n_row,)),
            pltpu.SemaphoreType.DMA((n_col,)),
            pltpu.SemaphoreType.DMA((n_col,)),
            pltpu.SemaphoreType.DMA((n_row,)),
            pltpu.SemaphoreType.DMA((n_row,)),
            pltpu.SemaphoreType.DMA((6,)),
        ] + extra_sems,
        compiler_params=pltpu.CompilerParams(collective_id=collective_id, has_side_effects=True),
    )(base_tiles, row_sum, col_sum, small)


def _slots_kernel(group, rows_k, rows_ref, cols_ref, count_ref, high_ref, low_ref, rowv_ref, colv_ref,
                  rsum_ref, csum_ref):
    g = pl.program_id(0)

    @pl.when(g == 0)
    def _():
        rsum_ref[...] = jnp.zeros_like(rsum_ref)
        csum_ref[...] = jnp.zeros_like(csum_ref)

    for s in range(group):
        slot = g * group + s

        @pl.when(slot < count_ref[0])
        def _():
            a = rows_ref[slot]
            b = cols_ref[slot]
            block = (high_ref[s], low_ref[s])
            direct = dot3(split_bf16(colv_ref[b, pl.ds(0, rows_k), :]), block, (((1,), (1,)), ((), ())))
            rsum_ref[a] += direct
            mirror = dot3(split_bf16(rowv_ref[a, pl.ds(0, rows_k), :]), block, (((1,), (0,)), ((), ())))
            csum_ref[b] += mirror


def split_bf16(x):
    high = x.astype(jnp.bfloat16)
    return high, (x - high.astype(jnp.float32)).astype(jnp.bfloat16)


def split_tiles(x):
    high = lax.reduce_precision(x, exponent_bits=8, mantissa_bits=7)
    return high.astype(jnp.bfloat16), (x - high).astype(jnp.bfloat16)


def dot3(left, right, dims):
    def one(x, y):
        return lax.dot_general(x, y, dims, preferred_element_type=jnp.float32)

    rows = left[0].shape[0]
    both = one(jnp.concatenate([left[0], left[1]], axis=0), right[0])
    return both[:rows] + (both[rows:] + one(left[0], right[1]))


def slot_products(blocks, rows_here, cols_here, live_count, row_tiles, column_tiles, rows_k):
    slot_count, tile, _ = blocks[0].shape
    sums_shape = lambda v: (v.shape[0], rows_k, v.shape[2])
    group = group_width
    groups = slot_count // group

    def tile_map(g, rows, cols, count):
        last = jnp.maximum(count[0] - 1, 0) // group
        return (jnp.minimum(g, last), 0, 0)

    def whole(g, rows, cols, count):
        return (0, 0, 0)

    grid_spec = pltpu.PrefetchScalarGridSpec(
        num_scalar_prefetch=3,
        grid=(groups,),
        in_specs=[
            pl.BlockSpec((group, tile, tile), tile_map),
            pl.BlockSpec((group, tile, tile), tile_map),
            pl.BlockSpec(row_tiles.shape, whole),
            pl.BlockSpec(column_tiles.shape, whole),
        ],
        out_specs=[
            pl.BlockSpec(sums_shape(row_tiles), whole),
            pl.BlockSpec(sums_shape(column_tiles), whole),
        ],
    )
    return pl.pallas_call(
        functools.partial(_slots_kernel, group, rows_k),
        grid_spec=grid_spec,
        out_shape=(
            jax.ShapeDtypeStruct(sums_shape(row_tiles), jnp.float32),
            jax.ShapeDtypeStruct(sums_shape(column_tiles), jnp.float32),
        ),
        compiler_params=pltpu.CompilerParams(dimension_semantics=("arbitrary",)),
    )(rows_here, cols_here, live_count.reshape(1), blocks[0], blocks[1], row_tiles, column_tiles)


def to_tiles(vectors, tile):
    return vectors.reshape(vectors.shape[0], -1, tile).transpose(1, 0, 2)


def from_tiles(tiles):
    return tiles.transpose(1, 0, 2).reshape(tiles.shape[1], -1)


def tile_dot(left, right):
    return jnp.einsum("tki,tli->kl", left, right, precision=highest)


def dot_rows(left, right):
    return jnp.dot(left, right.T, precision=highest)


def local(n_row, n_col, tile_values, tile_row, tile_col, counts, diagonal, current, previous, previous_image):
    k = current.shape[0]
    tile = tile_values.shape[-1]
    slot_count = tile_values.shape[2]
    blocks = split_tiles(tile_values.reshape(slot_count, tile, tile))
    rows_here = tile_row.reshape(slot_count)
    cols_here = tile_col.reshape(slot_count)
    live_count = counts.reshape(())

    row_cp, col_cp = gather_tiles(to_tiles(jnp.concatenate([current, previous], 0), tile), n_row, n_col, 0)
    row_sum, col_sum = slot_products(blocks, rows_here, cols_here, live_count, row_cp, col_cp, k)
    row_cur, col_cur = row_cp[:, :k], col_cp[:, :k]
    scaled = diagonal[None, :] * current
    small_gram = dot_rows(current, current)
    proj_part = dot_rows(current, scaled) + tile_dot(row_cur, row_sum) + tile_dot(col_cur, col_sum)
    image_tiles, small, row_img, col_img = reduce_tiles(
        to_tiles(scaled, tile), row_sum, col_sum, pack_small((small_gram, proj_part)), n_row, n_col, 1,
        forward=True,
    )
    image = from_tiles(image_tiles)
    small_gram, small_proj = unpack_small(small, (small_gram, proj_part))

    factor = jnp.linalg.cholesky(small_gram)
    ritz_matrix = jax.scipy.linalg.cho_solve((factor, True), small_proj)
    residual = image - jnp.dot(ritz_matrix.T, current, precision=highest)

    def residual_of(img_tiles, cur_tiles):
        fitted = sum(ritz_matrix[l][None, :, None] * cur_tiles[:, l:l + 1, :] for l in range(k))
        return img_tiles - fitted

    row_res = residual_of(row_img, row_cur)
    col_res = residual_of(col_img, col_cur)
    row_sum, col_sum = slot_products(blocks, rows_here, cols_here, live_count, row_res, col_res, k)
    search_basis = jnp.concatenate([current, residual, previous], 0)
    row_basis = jnp.concatenate([row_cur, row_res, row_cp[:, k:]], 1)
    col_basis = jnp.concatenate([col_cur, col_res, col_cp[:, k:]], 1)
    scaled = diagonal[None, :] * residual
    correlation = dot_rows(search_basis, search_basis)
    residual_part = (
        dot_rows(search_basis, scaled) + tile_dot(row_basis, row_sum) + tile_dot(col_basis, col_sum)
    )
    mixed_part = jnp.concatenate(
        [dot_rows(search_basis, image), residual_part, dot_rows(search_basis, previous_image)], 1
    )
    image_tiles, small = reduce_tiles(
        to_tiles(scaled, tile), row_sum, col_sum, pack_small((correlation, mixed_part)), n_row, n_col, 2
    )
    residual_image = from_tiles(image_tiles)
    correlation, mixed_terms = unpack_small(small, (correlation, mixed_part))
    pencil = 0.5 * (mixed_terms + mixed_terms.T)
    lower_factor = jnp.linalg.cholesky(correlation)
    half_solve = jax.scipy.linalg.solve_triangular(lower_factor, pencil, lower=True)
    reduced = jax.scipy.linalg.solve_triangular(lower_factor, half_solve.T, lower=True)
    return (image, residual, residual_image, reduced)


def solution(mesh):
    n_row = mesh.shape["row"]
    n_col = mesh.shape["col"]
    return jax.shard_map(
        functools.partial(local, n_row, n_col),
        mesh=mesh,
        in_specs=(
            P("row", "col", None, None, None),
            P("row", "col", None),
            P("row", "col", None),
            P("row", "col"),
            P(("row", "col")),
            P(None, ("row", "col")),
            P(None, ("row", "col")),
            P(None, ("row", "col")),
        ),
        out_specs=(P(None, ("row", "col")), P(None, ("row", "col")), P(None, ("row", "col")), P()),
        check_vma=False,
    )
```

```python
import functools

import jax
import jax.numpy as jnp
from jax import lax
from jax.experimental import pallas as pl
from jax.experimental.pallas import tpu as pltpu
from jax.sharding import PartitionSpec as P

highest = lax.Precision.HIGHEST
group_width = 8
MESH = pl.DeviceIdType.MESH


def _barrier(n_row, n_col, r, c):
    barrier = pltpu.get_barrier_semaphore()

    def greet_col(k, carry):
        pl.semaphore_signal(barrier, 1, device_id=(r, lax.rem(c + k, n_col)), device_id_type=MESH)
        return carry

    def greet_row(k, carry):
        pl.semaphore_signal(barrier, 1, device_id=(lax.rem(r + k, n_row), c), device_id_type=MESH)
        return carry

    lax.fori_loop(1, n_col, greet_col, 0)
    lax.fori_loop(1, n_row, greet_row, 0)
    pl.semaphore_wait(barrier, n_row + n_col - 2)


def _gather_kernel(n_row, n_col, x_ref, rowv_ref, colv_ref, send_row, recv_row, send_col, recv_col, local_sem):
    vt = x_ref.shape[0]
    r = lax.axis_index("row")
    c = lax.axis_index("col")
    _barrier(n_row, n_col, r, c)

    def row_copy(j, src):
        return pltpu.make_async_remote_copy(
            src_ref=x_ref,
            dst_ref=rowv_ref.at[pl.ds(src * vt, vt)],
            send_sem=send_row.at[j],
            recv_sem=recv_row.at[src],
            device_id=(r, j),
            device_id_type=MESH,
        )

    def col_copy(i, src):
        return pltpu.make_async_remote_copy(
            src_ref=x_ref,
            dst_ref=colv_ref.at[pl.ds(src * vt, vt)],
            send_sem=send_col.at[i],
            recv_sem=recv_col.at[src],
            device_id=(i, c),
            device_id_type=MESH,
        )

    own_row = pltpu.make_async_copy(x_ref, rowv_ref.at[pl.ds(c * vt, vt)], local_sem.at[0])
    own_col = pltpu.make_async_copy(x_ref, colv_ref.at[pl.ds(r * vt, vt)], local_sem.at[1])
    own_row.start()
    own_col.start()

    def start_col(k, carry):
        row_copy(lax.rem(c + k, n_col), c).start()
        return carry

    def start_row(k, carry):
        col_copy(lax.rem(r + k, n_row), r).start()
        return carry

    lax.fori_loop(1, n_col, start_col, 0)
    lax.fori_loop(1, n_row, start_row, 0)

    def wait_col(k, carry):
        row_copy(lax.rem(c + k, n_col), c).wait_send()
        row_copy(c, lax.rem(c + n_col - k, n_col)).wait_recv()
        return carry

    def wait_row(k, carry):
        col_copy(lax.rem(r + k, n_row), r).wait_send()
        col_copy(r, lax.rem(r + n_row - k, n_row)).wait_recv()
        return carry

    lax.fori_loop(1, n_col, wait_col, 0)
    lax.fori_loop(1, n_row, wait_row, 0)
    own_row.wait()
    own_col.wait()


def gather_tiles(x_tiles, n_row, n_col, collective_id):
    vt, k, t = x_tiles.shape
    vmem = pl.BlockSpec(memory_space=pltpu.VMEM)
    return pl.pallas_call(
        functools.partial(_gather_kernel, n_row, n_col),
        out_shape=(
            jax.ShapeDtypeStruct((n_col * vt, k, t), x_tiles.dtype),
            jax.ShapeDtypeStruct((n_row * vt, k, t), x_tiles.dtype),
        ),
        in_specs=[vmem],
        out_specs=(vmem, vmem),
        scratch_shapes=[
            pltpu.SemaphoreType.DMA((n_col,)),
            pltpu.SemaphoreType.DMA((n_col,)),
            pltpu.SemaphoreType.DMA((n_row,)),
            pltpu.SemaphoreType.DMA((n_row,)),
            pltpu.SemaphoreType.DMA((2,)),
        ],
        compiler_params=pltpu.CompilerParams(collective_id=collective_id, has_side_effects=True),
    )(x_tiles)


def _reduce_kernel(n_row, n_col, forward, base_ref, rsum_ref, csum_ref, small_ref, out_ref, small_out, *rest):
    if forward:
        img_row, img_col = rest[:2]
        rest = rest[2:]
    (got_row, got_col, got_small_col, mid, got_small_row,
     send_row, recv_row, send_col, recv_col,
     send_small_col, recv_small_col, send_small_row, recv_small_row, local_sem) = rest[:14]
    vt = base_ref.shape[0]
    r = lax.axis_index("row")
    c = lax.axis_index("col")
    _barrier(n_row, n_col, r, c)

    def small_col_copy(j, src):
        return pltpu.make_async_remote_copy(
            src_ref=small_ref,
            dst_ref=got_small_col.at[src],
            send_sem=send_small_col.at[j],
            recv_sem=recv_small_col.at[src],
            device_id=(r, j),
            device_id_type=MESH,
        )

    def small_row_copy(i, src):
        return pltpu.make_async_remote_copy(
            src_ref=mid,
            dst_ref=got_small_row.at[src],
            send_sem=send_small_row.at[i],
            recv_sem=recv_small_row.at[src],
            device_id=(i, c),
            device_id_type=MESH,
        )

    def row_copy(j, src):
        return pltpu.make_async_remote_copy(
            src_ref=rsum_ref.at[pl.ds(j * vt, vt)],
            dst_ref=got_row.at[src],
            send_sem=send_row.at[j],
            recv_sem=recv_row.at[src],
            device_id=(r, j),
            device_id_type=MESH,
        )

    def col_copy(i, src):
        return pltpu.make_async_remote_copy(
            src_ref=csum_ref.at[pl.ds(i * vt, vt)],
            dst_ref=got_col.at[src],
            send_sem=send_col.at[i],
            recv_sem=recv_col.at[src],
            device_id=(i, c),
            device_id_type=MESH,
        )

    own_small = pltpu.make_async_copy(small_ref, got_small_col.at[c], local_sem.at[2])
    own_small.start()

    def start_small_col(k, carry):
        small_col_copy(lax.rem(c + k, n_col), c).start()
        return carry

    lax.fori_loop(1, n_col, start_small_col, 0)

    own_row = pltpu.make_async_copy(rsum_ref.at[pl.ds(c * vt, vt)], got_row.at[c], local_sem.at[0])
    own_col = pltpu.make_async_copy(csum_ref.at[pl.ds(r * vt, vt)], got_col.at[r], local_sem.at[1])
    own_row.start()
    own_col.start()

    def start_col(k, carry):
        row_copy(lax.rem(c + k, n_col), c).start()
        return carry

    def start_row(k, carry):
        col_copy(lax.rem(r + k, n_row), r).start()
        return carry

    lax.fori_loop(1, n_row, start_row, 0)
    lax.fori_loop(1, n_col, start_col, 0)

    def wait_small_col(k, carry):
        small_col_copy(lax.rem(c + k, n_col), c).wait_send()
        small_col_copy(c, lax.rem(c + n_col - k, n_col)).wait_recv()
        return carry

    lax.fori_loop(1, n_col, wait_small_col, 0)
    own_small.wait()
    mid[...] = jnp.sum(got_small_col[...], axis=0)

    own_mid = pltpu.make_async_copy(mid, got_small_row.at[r], local_sem.at[3])
    own_mid.start()

    def start_small_row(k, carry):
        small_row_copy(lax.rem(r + k, n_row), r).start()
        return carry

    lax.fori_loop(1, n_row, start_small_row, 0)

    def wait_col(k, carry):
        row_copy(lax.rem(c + k, n_col), c).wait_send()
        row_copy(c, lax.rem(c + n_col - k, n_col)).wait_recv()
        return carry

    def wait_row(k, carry):
        col_copy(lax.rem(r + k, n_row), r).wait_send()
        col_copy(r, lax.rem(r + n_row - k, n_row)).wait_recv()
        return carry

    lax.fori_loop(1, n_col, wait_col, 0)
    lax.fori_loop(1, n_row, wait_row, 0)
    own_row.wait()
    own_col.wait()
    out_ref[...] = base_ref[...] + jnp.sum(got_row[...], axis=0) + jnp.sum(got_col[...], axis=0)

    if forward:
        send_fr, recv_fr, send_fc, recv_fc = rest[14:]

        def fwd_row_copy(j, src):
            return pltpu.make_async_remote_copy(
                src_ref=out_ref,
                dst_ref=img_row.at[pl.ds(src * vt, vt)],
                send_sem=send_fr.at[j],
                recv_sem=recv_fr.at[src],
                device_id=(r, j),
                device_id_type=MESH,
            )

        def fwd_col_copy(i, src):
            return pltpu.make_async_remote_copy(
                src_ref=out_ref,
                dst_ref=img_col.at[pl.ds(src * vt, vt)],
                send_sem=send_fc.at[i],
                recv_sem=recv_fc.at[src],
                device_id=(i, c),
                device_id_type=MESH,
            )

        own_fr = pltpu.make_async_copy(out_ref, img_row.at[pl.ds(c * vt, vt)], local_sem.at[4])
        own_fc = pltpu.make_async_copy(out_ref, img_col.at[pl.ds(r * vt, vt)], local_sem.at[5])
        own_fr.start()
        own_fc.start()

        def start_fr(k, carry):
            fwd_row_copy(lax.rem(c + k, n_col), c).start()
            return carry

        def start_fc(k, carry):
            fwd_col_copy(lax.rem(r + k, n_row), r).start()
            return carry

        lax.fori_loop(1, n_row, start_fc, 0)
        lax.fori_loop(1, n_col, start_fr, 0)

    def wait_small_row(k, carry):
        small_row_copy(lax.rem(r + k, n_row), r).wait_send()
        small_row_copy(r, lax.rem(r + n_row - k, n_row)).wait_recv()
        return carry

    lax.fori_loop(1, n_row, wait_small_row, 0)
    own_mid.wait()
    small_out[...] = jnp.sum(got_small_row[...], axis=0)

    if forward:
        def wait_fr(k, carry):
            fwd_row_copy(lax.rem(c + k, n_col), c).wait_send()
            fwd_row_copy(c, lax.rem(c + n_col - k, n_col)).wait_recv()
            return carry

        def wait_fc(k, carry):
            fwd_col_copy(lax.rem(r + k, n_row), r).wait_send()
            fwd_col_copy(r, lax.rem(r + n_row - k, n_row)).wait_recv()
            return carry

        lax.fori_loop(1, n_col, wait_fr, 0)
        lax.fori_loop(1, n_row, wait_fc, 0)
        own_fr.wait()
        own_fc.wait()


def pack_small(values):
    flat = jnp.concatenate([v.reshape(-1) for v in values])
    tile = 8 * 128
    padded = -(-flat.shape[0] // tile) * tile
    return jnp.pad(flat, (0, padded - flat.shape[0])).reshape(-1, 128)


def unpack_small(total, values):
    total = total.reshape(-1)
    out, start = [], 0
    for v in values:
        out.append(total[start:start + v.size].reshape(v.shape))
        start += v.size
    return out


def reduce_tiles(base_tiles, row_sum, col_sum, small, n_row, n_col, collective_id, forward=False):
    vt, k, t = base_tiles.shape
    s = small.shape[0]
    vmem = pl.BlockSpec(memory_space=pltpu.VMEM)
    out_shape = [
        jax.ShapeDtypeStruct((vt, k, t), base_tiles.dtype),
        jax.ShapeDtypeStruct((s, 128), jnp.float32),
    ]
    extra_sems = []
    if forward:
        out_shape += [
            jax.ShapeDtypeStruct((n_col * vt, k, t), base_tiles.dtype),
            jax.ShapeDtypeStruct((n_row * vt, k, t), base_tiles.dtype),
        ]
        extra_sems = [
            pltpu.SemaphoreType.DMA((n_col,)),
            pltpu.SemaphoreType.DMA((n_col,)),
            pltpu.SemaphoreType.DMA((n_row,)),
            pltpu.SemaphoreType.DMA((n_row,)),
        ]
    return pl.pallas_call(
        functools.partial(_reduce_kernel, n_row, n_col, forward),
        out_shape=tuple(out_shape),
        in_specs=[vmem, vmem, vmem, vmem],
        out_specs=tuple(vmem for _ in out_shape),
        scratch_shapes=[
            pltpu.VMEM((n_col, vt, k, t), jnp.float32),
            pltpu.VMEM((n_row, vt, k, t), jnp.float32),
            pltpu.VMEM((n_col, s, 128), jnp.float32),
            pltpu.VMEM((s, 128), jnp.float32),
            pltpu.VMEM((n_row, s, 128), jnp.float32),
            pltpu.SemaphoreType.DMA((n_col,)),
            pltpu.SemaphoreType.DMA((n_col,)),
            pltpu.SemaphoreType.DMA((n_row,)),
            pltpu.SemaphoreType.DMA((n_row,)),
            pltpu.SemaphoreType.DMA((n_col,)),
            pltpu.SemaphoreType.DMA((n_col,)),
            pltpu.SemaphoreType.DMA((n_row,)),
            pltpu.SemaphoreType.DMA((n_row,)),
            pltpu.SemaphoreType.DMA((6,)),
        ] + extra_sems,
        compiler_params=pltpu.CompilerParams(collective_id=collective_id, has_side_effects=True),
    )(base_tiles, row_sum, col_sum, small)


def _slots_kernel(group, rows_k, rows_ref, cols_ref, count_ref, tiles_ref, rowv_ref, colv_ref,
                  rsum_ref, csum_ref):
    g = pl.program_id(0)

    @pl.when(g == 0)
    def _():
        rsum_ref[...] = jnp.zeros_like(rsum_ref)
        csum_ref[...] = jnp.zeros_like(csum_ref)

    for s in range(group):
        slot = g * group + s

        @pl.when(slot < count_ref[0])
        def _():
            a = rows_ref[slot]
            b = cols_ref[slot]
            block = split_bf16(tiles_ref[s])
            direct = dot3(split_bf16(colv_ref[b, pl.ds(0, rows_k), :]), block, (((1,), (1,)), ((), ())))
            rsum_ref[a] += direct
            mirror = dot3(split_bf16(rowv_ref[a, pl.ds(0, rows_k), :]), block, (((1,), (0,)), ((), ())))
            csum_ref[b] += mirror


def split_bf16(x):
    high = x.astype(jnp.bfloat16)
    return high, (x - high.astype(jnp.float32)).astype(jnp.bfloat16)


def dot3(left, right, dims):
    def one(x, y):
        return lax.dot_general(x, y, dims, preferred_element_type=jnp.float32)

    rows = left[0].shape[0]
    both = one(jnp.concatenate([left[0], left[1]], axis=0), right[0])
    return both[:rows] + (both[rows:] + one(left[0], right[1]))


def slot_products(blocks, rows_here, cols_here, live_count, row_tiles, column_tiles, rows_k):
    slot_count, tile, _ = blocks.shape
    sums_shape = lambda v: (v.shape[0], rows_k, v.shape[2])
    group = group_width
    groups = slot_count // group

    def tile_map(g, rows, cols, count):
        last = jnp.maximum(count[0] - 1, 0) // group
        return (jnp.minimum(g, last), 0, 0)

    def whole(g, rows, cols, count):
        return (0, 0, 0)

    grid_spec = pltpu.PrefetchScalarGridSpec(
        num_scalar_prefetch=3,
        grid=(groups,),
        in_specs=[
            pl.BlockSpec((group, tile, tile), tile_map),
            pl.BlockSpec(row_tiles.shape, whole),
            pl.BlockSpec(column_tiles.shape, whole),
        ],
        out_specs=[
            pl.BlockSpec(sums_shape(row_tiles), whole),
            pl.BlockSpec(sums_shape(column_tiles), whole),
        ],
    )
    return pl.pallas_call(
        functools.partial(_slots_kernel, group, rows_k),
        grid_spec=grid_spec,
        out_shape=(
            jax.ShapeDtypeStruct(sums_shape(row_tiles), jnp.float32),
            jax.ShapeDtypeStruct(sums_shape(column_tiles), jnp.float32),
        ),
        compiler_params=pltpu.CompilerParams(dimension_semantics=("arbitrary",)),
    )(rows_here, cols_here, live_count.reshape(1), blocks, row_tiles, column_tiles)


def to_tiles(vectors, tile):
    return vectors.reshape(vectors.shape[0], -1, tile).transpose(1, 0, 2)


def from_tiles(tiles):
    return tiles.transpose(1, 0, 2).reshape(tiles.shape[1], -1)


def tile_dot(left, right):
    return jnp.sum(left[:, :, None, :] * right[:, None, :, :], axis=(0, 3))


def dot_rows(left, right):
    return jnp.dot(left, right.T, precision=highest)


def local(n_row, n_col, tile_values, tile_row, tile_col, counts, diagonal, current, previous, previous_image):
    k = current.shape[0]
    tile = tile_values.shape[-1]
    slot_count = tile_values.shape[2]
    blocks = tile_values.reshape(slot_count, tile, tile)
    rows_here = tile_row.reshape(slot_count)
    cols_here = tile_col.reshape(slot_count)
    live_count = counts.reshape(())

    row_cp, col_cp = gather_tiles(to_tiles(jnp.concatenate([current, previous], 0), tile), n_row, n_col, 0)
    row_sum, col_sum = slot_products(blocks, rows_here, cols_here, live_count, row_cp, col_cp, k)
    row_cur, col_cur = row_cp[:, :k], col_cp[:, :k]
    scaled = diagonal[None, :] * current
    small_gram = dot_rows(current, current)
    proj_part = dot_rows(current, scaled) + tile_dot(row_cur, row_sum) + tile_dot(col_cur, col_sum)
    image_tiles, small, row_img, col_img = reduce_tiles(
        to_tiles(scaled, tile), row_sum, col_sum, pack_small((small_gram, proj_part)), n_row, n_col, 1,
        forward=True,
    )
    image = from_tiles(image_tiles)
    small_gram, small_proj = unpack_small(small, (small_gram, proj_part))

    factor = jnp.linalg.cholesky(small_gram)
    ritz_matrix = jax.scipy.linalg.cho_solve((factor, True), small_proj)
    residual = image - jnp.dot(ritz_matrix.T, current, precision=highest)

    def residual_of(img_tiles, cur_tiles):
        fitted = sum(ritz_matrix[l][None, :, None] * cur_tiles[:, l:l + 1, :] for l in range(k))
        return img_tiles - fitted

    row_res = residual_of(row_img, row_cur)
    col_res = residual_of(col_img, col_cur)
    row_sum, col_sum = slot_products(blocks, rows_here, cols_here, live_count, row_res, col_res, k)
    search_basis = jnp.concatenate([current, residual, previous], 0)
    row_basis = jnp.concatenate([row_cur, row_res, row_cp[:, k:]], 1)
    col_basis = jnp.concatenate([col_cur, col_res, col_cp[:, k:]], 1)
    scaled = diagonal[None, :] * residual
    correlation = dot_rows(search_basis, search_basis)
    residual_part = (
        dot_rows(search_basis, scaled) + tile_dot(row_basis, row_sum) + tile_dot(col_basis, col_sum)
    )
    mixed_part = jnp.concatenate(
        [dot_rows(search_basis, image), residual_part, dot_rows(search_basis, previous_image)], 1
    )
    image_tiles, small = reduce_tiles(
        to_tiles(scaled, tile), row_sum, col_sum, pack_small((correlation, mixed_part)), n_row, n_col, 2
    )
    residual_image = from_tiles(image_tiles)
    correlation, mixed_terms = unpack_small(small, (correlation, mixed_part))
    pencil = 0.5 * (mixed_terms + mixed_terms.T)
    lower_factor = jnp.linalg.cholesky(correlation)
    half_solve = jax.scipy.linalg.solve_triangular(lower_factor, pencil, lower=True)
    reduced = jax.scipy.linalg.solve_triangular(lower_factor, half_solve.T, lower=True)
    return (image, residual, residual_image, reduced)


def solution(mesh):
    n_row = mesh.shape["row"]
    n_col = mesh.shape["col"]
    return jax.shard_map(
        functools.partial(local, n_row, n_col),
        mesh=mesh,
        in_specs=(
            P("row", "col", None, None, None),
            P("row", "col", None),
            P("row", "col", None),
            P("row", "col"),
            P(("row", "col")),
            P(None, ("row", "col")),
            P(None, ("row", "col")),
            P(None, ("row", "col")),
        ),
        out_specs=(P(None, ("row", "col")), P(None, ("row", "col")), P(None, ("row", "col")), P()),
        check_vma=False,
    )
```

```python
import functools

import jax
import jax.numpy as jnp
from jax import lax
from jax.experimental import pallas as pl
from jax.experimental.pallas import tpu as pltpu
from jax.sharding import PartitionSpec as P

highest = lax.Precision.HIGHEST
group_width = 8
MESH = pl.DeviceIdType.MESH


def _barrier(n_row, n_col, r, c):
    barrier = pltpu.get_barrier_semaphore()

    def greet_col(k, carry):
        pl.semaphore_signal(barrier, 1, device_id=(r, lax.rem(c + k, n_col)), device_id_type=MESH)
        return carry

    def greet_row(k, carry):
        pl.semaphore_signal(barrier, 1, device_id=(lax.rem(r + k, n_row), c), device_id_type=MESH)
        return carry

    lax.fori_loop(1, n_col, greet_col, 0)
    lax.fori_loop(1, n_row, greet_row, 0)
    pl.semaphore_wait(barrier, n_row + n_col - 2)


def _gather_kernel(n_row, n_col, x_ref, rowv_ref, colv_ref, send_row, recv_row, send_col, recv_col, local_sem):
    vt = x_ref.shape[0]
    r = lax.axis_index("row")
    c = lax.axis_index("col")
    _barrier(n_row, n_col, r, c)

    def row_copy(j, src):
        return pltpu.make_async_remote_copy(
            src_ref=x_ref,
            dst_ref=rowv_ref.at[pl.ds(src * vt, vt)],
            send_sem=send_row.at[j],
            recv_sem=recv_row.at[src],
            device_id=(r, j),
            device_id_type=MESH,
        )

    def col_copy(i, src):
        return pltpu.make_async_remote_copy(
            src_ref=x_ref,
            dst_ref=colv_ref.at[pl.ds(src * vt, vt)],
            send_sem=send_col.at[i],
            recv_sem=recv_col.at[src],
            device_id=(i, c),
            device_id_type=MESH,
        )

    own_row = pltpu.make_async_copy(x_ref, rowv_ref.at[pl.ds(c * vt, vt)], local_sem.at[0])
    own_col = pltpu.make_async_copy(x_ref, colv_ref.at[pl.ds(r * vt, vt)], local_sem.at[1])
    own_row.start()
    own_col.start()

    def start_col(k, carry):
        row_copy(lax.rem(c + k, n_col), c).start()
        return carry

    def start_row(k, carry):
        col_copy(lax.rem(r + k, n_row), r).start()
        return carry

    lax.fori_loop(1, n_col, start_col, 0)
    lax.fori_loop(1, n_row, start_row, 0)

    def wait_col(k, carry):
        row_copy(lax.rem(c + k, n_col), c).wait_send()
        row_copy(c, lax.rem(c + n_col - k, n_col)).wait_recv()
        return carry

    def wait_row(k, carry):
        col_copy(lax.rem(r + k, n_row), r).wait_send()
        col_copy(r, lax.rem(r + n_row - k, n_row)).wait_recv()
        return carry

    lax.fori_loop(1, n_col, wait_col, 0)
    lax.fori_loop(1, n_row, wait_row, 0)
    own_row.wait()
    own_col.wait()


def gather_tiles(x_tiles, n_row, n_col, collective_id):
    vt, k, t = x_tiles.shape
    vmem = pl.BlockSpec(memory_space=pltpu.VMEM)
    return pl.pallas_call(
        functools.partial(_gather_kernel, n_row, n_col),
        out_shape=(
            jax.ShapeDtypeStruct((n_col * vt, k, t), x_tiles.dtype),
            jax.ShapeDtypeStruct((n_row * vt, k, t), x_tiles.dtype),
        ),
        in_specs=[vmem],
        out_specs=(vmem, vmem),
        scratch_shapes=[
            pltpu.SemaphoreType.DMA((n_col,)),
            pltpu.SemaphoreType.DMA((n_col,)),
            pltpu.SemaphoreType.DMA((n_row,)),
            pltpu.SemaphoreType.DMA((n_row,)),
            pltpu.SemaphoreType.DMA((2,)),
        ],
        compiler_params=pltpu.CompilerParams(collective_id=collective_id, has_side_effects=True),
    )(x_tiles)


def _reduce_kernel(n_row, n_col, forward, base_ref, rsum_ref, csum_ref, small_ref, out_ref, small_out, *rest):
    if forward:
        img_row, img_col = rest[:2]
        rest = rest[2:]
    (got_row, got_col, got_small_col, mid, got_small_row,
     send_row, recv_row, send_col, recv_col,
     send_small_col, recv_small_col, send_small_row, recv_small_row, local_sem) = rest[:14]
    vt = base_ref.shape[0]
    r = lax.axis_index("row")
    c = lax.axis_index("col")
    _barrier(n_row, n_col, r, c)

    def small_col_copy(j, src):
        return pltpu.make_async_remote_copy(
            src_ref=small_ref,
            dst_ref=got_small_col.at[src],
            send_sem=send_small_col.at[j],
            recv_sem=recv_small_col.at[src],
            device_id=(r, j),
            device_id_type=MESH,
        )

    def small_row_copy(i, src):
        return pltpu.make_async_remote_copy(
            src_ref=mid,
            dst_ref=got_small_row.at[src],
            send_sem=send_small_row.at[i],
            recv_sem=recv_small_row.at[src],
            device_id=(i, c),
            device_id_type=MESH,
        )

    def row_copy(j, src):
        return pltpu.make_async_remote_copy(
            src_ref=rsum_ref.at[pl.ds(j * vt, vt)],
            dst_ref=got_row.at[src],
            send_sem=send_row.at[j],
            recv_sem=recv_row.at[src],
            device_id=(r, j),
            device_id_type=MESH,
        )

    def col_copy(i, src):
        return pltpu.make_async_remote_copy(
            src_ref=csum_ref.at[pl.ds(i * vt, vt)],
            dst_ref=got_col.at[src],
            send_sem=send_col.at[i],
            recv_sem=recv_col.at[src],
            device_id=(i, c),
            device_id_type=MESH,
        )

    own_small = pltpu.make_async_copy(small_ref, got_small_col.at[c], local_sem.at[2])
    own_small.start()

    def start_small_col(k, carry):
        small_col_copy(lax.rem(c + k, n_col), c).start()
        return carry

    lax.fori_loop(1, n_col, start_small_col, 0)

    own_row = pltpu.make_async_copy(rsum_ref.at[pl.ds(c * vt, vt)], got_row.at[c], local_sem.at[0])
    own_col = pltpu.make_async_copy(csum_ref.at[pl.ds(r * vt, vt)], got_col.at[r], local_sem.at[1])
    own_row.start()
    own_col.start()

    def start_col(k, carry):
        row_copy(lax.rem(c + k, n_col), c).start()
        return carry

    def start_row(k, carry):
        col_copy(lax.rem(r + k, n_row), r).start()
        return carry

    lax.fori_loop(1, n_row, start_row, 0)
    lax.fori_loop(1, n_col, start_col, 0)

    def wait_small_col(k, carry):
        small_col_copy(lax.rem(c + k, n_col), c).wait_send()
        small_col_copy(c, lax.rem(c + n_col - k, n_col)).wait_recv()
        return carry

    lax.fori_loop(1, n_col, wait_small_col, 0)
    own_small.wait()
    mid[...] = jnp.sum(got_small_col[...], axis=0)

    own_mid = pltpu.make_async_copy(mid, got_small_row.at[r], local_sem.at[3])
    own_mid.start()

    def start_small_row(k, carry):
        small_row_copy(lax.rem(r + k, n_row), r).start()
        return carry

    lax.fori_loop(1, n_row, start_small_row, 0)

    def wait_col(k, carry):
        row_copy(lax.rem(c + k, n_col), c).wait_send()
        row_copy(c, lax.rem(c + n_col - k, n_col)).wait_recv()
        return carry

    def wait_row(k, carry):
        col_copy(lax.rem(r + k, n_row), r).wait_send()
        col_copy(r, lax.rem(r + n_row - k, n_row)).wait_recv()
        return carry

    lax.fori_loop(1, n_col, wait_col, 0)
    lax.fori_loop(1, n_row, wait_row, 0)
    own_row.wait()
    own_col.wait()
    out_ref[...] = base_ref[...] + jnp.sum(got_row[...], axis=0) + jnp.sum(got_col[...], axis=0)

    if forward:
        send_fr, recv_fr, send_fc, recv_fc = rest[14:]

        def fwd_row_copy(j, src):
            return pltpu.make_async_remote_copy(
                src_ref=out_ref,
                dst_ref=img_row.at[pl.ds(src * vt, vt)],
                send_sem=send_fr.at[j],
                recv_sem=recv_fr.at[src],
                device_id=(r, j),
                device_id_type=MESH,
            )

        def fwd_col_copy(i, src):
            return pltpu.make_async_remote_copy(
                src_ref=out_ref,
                dst_ref=img_col.at[pl.ds(src * vt, vt)],
                send_sem=send_fc.at[i],
                recv_sem=recv_fc.at[src],
                device_id=(i, c),
                device_id_type=MESH,
            )

        own_fr = pltpu.make_async_copy(out_ref, img_row.at[pl.ds(c * vt, vt)], local_sem.at[4])
        own_fc = pltpu.make_async_copy(out_ref, img_col.at[pl.ds(r * vt, vt)], local_sem.at[5])
        own_fr.start()
        own_fc.start()

        def start_fr(k, carry):
            fwd_row_copy(lax.rem(c + k, n_col), c).start()
            return carry

        def start_fc(k, carry):
            fwd_col_copy(lax.rem(r + k, n_row), r).start()
            return carry

        lax.fori_loop(1, n_row, start_fc, 0)
        lax.fori_loop(1, n_col, start_fr, 0)

    def wait_small_row(k, carry):
        small_row_copy(lax.rem(r + k, n_row), r).wait_send()
        small_row_copy(r, lax.rem(r + n_row - k, n_row)).wait_recv()
        return carry

    lax.fori_loop(1, n_row, wait_small_row, 0)
    own_mid.wait()
    small_out[...] = jnp.sum(got_small_row[...], axis=0)

    if forward:
        def wait_fr(k, carry):
            fwd_row_copy(lax.rem(c + k, n_col), c).wait_send()
            fwd_row_copy(c, lax.rem(c + n_col - k, n_col)).wait_recv()
            return carry

        def wait_fc(k, carry):
            fwd_col_copy(lax.rem(r + k, n_row), r).wait_send()
            fwd_col_copy(r, lax.rem(r + n_row - k, n_row)).wait_recv()
            return carry

        lax.fori_loop(1, n_col, wait_fr, 0)
        lax.fori_loop(1, n_row, wait_fc, 0)
        own_fr.wait()
        own_fc.wait()


def pack_small(values):
    flat = jnp.concatenate([v.reshape(-1) for v in values])
    tile = 8 * 128
    padded = -(-flat.shape[0] // tile) * tile
    return jnp.pad(flat, (0, padded - flat.shape[0])).reshape(-1, 128)


def unpack_small(total, values):
    total = total.reshape(-1)
    out, start = [], 0
    for v in values:
        out.append(total[start:start + v.size].reshape(v.shape))
        start += v.size
    return out


def reduce_tiles(base_tiles, row_sum, col_sum, small, n_row, n_col, collective_id, forward=False):
    vt, k, t = base_tiles.shape
    s = small.shape[0]
    vmem = pl.BlockSpec(memory_space=pltpu.VMEM)
    out_shape = [
        jax.ShapeDtypeStruct((vt, k, t), base_tiles.dtype),
        jax.ShapeDtypeStruct((s, 128), jnp.float32),
    ]
    extra_sems = []
    if forward:
        out_shape += [
            jax.ShapeDtypeStruct((n_col * vt, k, t), base_tiles.dtype),
            jax.ShapeDtypeStruct((n_row * vt, k, t), base_tiles.dtype),
        ]
        extra_sems = [
            pltpu.SemaphoreType.DMA((n_col,)),
            pltpu.SemaphoreType.DMA((n_col,)),
            pltpu.SemaphoreType.DMA((n_row,)),
            pltpu.SemaphoreType.DMA((n_row,)),
        ]
    return pl.pallas_call(
        functools.partial(_reduce_kernel, n_row, n_col, forward),
        out_shape=tuple(out_shape),
        in_specs=[vmem, vmem, vmem, vmem],
        out_specs=tuple(vmem for _ in out_shape),
        scratch_shapes=[
            pltpu.VMEM((n_col, vt, k, t), jnp.float32),
            pltpu.VMEM((n_row, vt, k, t), jnp.float32),
            pltpu.VMEM((n_col, s, 128), jnp.float32),
            pltpu.VMEM((s, 128), jnp.float32),
            pltpu.VMEM((n_row, s, 128), jnp.float32),
            pltpu.SemaphoreType.DMA((n_col,)),
            pltpu.SemaphoreType.DMA((n_col,)),
            pltpu.SemaphoreType.DMA((n_row,)),
            pltpu.SemaphoreType.DMA((n_row,)),
            pltpu.SemaphoreType.DMA((n_col,)),
            pltpu.SemaphoreType.DMA((n_col,)),
            pltpu.SemaphoreType.DMA((n_row,)),
            pltpu.SemaphoreType.DMA((n_row,)),
            pltpu.SemaphoreType.DMA((6,)),
        ] + extra_sems,
        compiler_params=pltpu.CompilerParams(collective_id=collective_id, has_side_effects=True),
    )(base_tiles, row_sum, col_sum, small)


def _slots_kernel(group, rows_k, rows_ref, cols_ref, count_ref, tiles_ref, rowv_ref, colv_ref,
                  rsum_ref, csum_ref):
    g = pl.program_id(0)

    @pl.when(g == 0)
    def _():
        rsum_ref[...] = jnp.zeros_like(rsum_ref)
        csum_ref[...] = jnp.zeros_like(csum_ref)

    for s in range(group):
        slot = g * group + s

        @pl.when(slot < count_ref[0])
        def _():
            a = rows_ref[slot]
            b = cols_ref[slot]
            high, low = split_bf16(tiles_ref[s])
            rsum_ref[a] += dot3(
                split_bf16(colv_ref[b, pl.ds(0, rows_k), :]),
                jnp.concatenate([high, low], axis=0), (((1,), (1,)), ((), ())),
            )
            csum_ref[b] += dot3(
                split_bf16(rowv_ref[a, pl.ds(0, rows_k), :]),
                jnp.concatenate([high, low], axis=1), (((1,), (0,)), ((), ())),
            )


def split_bf16(x):
    high = x.astype(jnp.bfloat16)
    return high, (x - high.astype(jnp.float32)).astype(jnp.bfloat16)


def dot3(left, right, dims):
    rows = left[0].shape[0]
    both = lax.dot_general(
        jnp.concatenate([left[0], left[1]], axis=0), right, dims, preferred_element_type=jnp.float32
    )
    width = both.shape[1] // 2
    return both[:rows, :width] + (both[rows:, :width] + both[:rows, width:])


def slot_products(blocks, rows_here, cols_here, live_count, row_tiles, column_tiles, rows_k):
    slot_count, tile, _ = blocks.shape
    sums_shape = lambda v: (v.shape[0], rows_k, v.shape[2])
    group = group_width
    groups = slot_count // group

    def tile_map(g, rows, cols, count):
        last = jnp.maximum(count[0] - 1, 0) // group
        return (jnp.minimum(g, last), 0, 0)

    def whole(g, rows, cols, count):
        return (0, 0, 0)

    grid_spec = pltpu.PrefetchScalarGridSpec(
        num_scalar_prefetch=3,
        grid=(groups,),
        in_specs=[
            pl.BlockSpec((group, tile, tile), tile_map),
            pl.BlockSpec(row_tiles.shape, whole),
            pl.BlockSpec(column_tiles.shape, whole),
        ],
        out_specs=[
            pl.BlockSpec(sums_shape(row_tiles), whole),
            pl.BlockSpec(sums_shape(column_tiles), whole),
        ],
    )
    return pl.pallas_call(
        functools.partial(_slots_kernel, group, rows_k),
        grid_spec=grid_spec,
        out_shape=(
            jax.ShapeDtypeStruct(sums_shape(row_tiles), jnp.float32),
            jax.ShapeDtypeStruct(sums_shape(column_tiles), jnp.float32),
        ),
        compiler_params=pltpu.CompilerParams(dimension_semantics=("arbitrary",)),
    )(rows_here, cols_here, live_count.reshape(1), blocks, row_tiles, column_tiles)


def to_tiles(vectors, tile):
    return vectors.reshape(vectors.shape[0], -1, tile).transpose(1, 0, 2)


def from_tiles(tiles):
    return tiles.transpose(1, 0, 2).reshape(tiles.shape[1], -1)


def tile_dot(left, right):
    return jnp.einsum("tki,tli->kl", left, right, precision=highest)


def dot_rows(left, right):
    return jnp.dot(left, right.T, precision=highest)


def local(n_row, n_col, tile_values, tile_row, tile_col, counts, diagonal, current, previous, previous_image):
    k = current.shape[0]
    tile = tile_values.shape[-1]
    slot_count = tile_values.shape[2]
    blocks = tile_values.reshape(slot_count, tile, tile)
    rows_here = tile_row.reshape(slot_count)
    cols_here = tile_col.reshape(slot_count)
    live_count = counts.reshape(())

    row_cp, col_cp = gather_tiles(to_tiles(jnp.concatenate([current, previous], 0), tile), n_row, n_col, 0)
    row_sum, col_sum = slot_products(blocks, rows_here, cols_here, live_count, row_cp, col_cp, k)
    row_cur, col_cur = row_cp[:, :k], col_cp[:, :k]
    scaled = diagonal[None, :] * current
    small_gram = dot_rows(current, current)
    proj_part = dot_rows(current, scaled) + tile_dot(row_cur, row_sum) + tile_dot(col_cur, col_sum)
    image_tiles, small, row_img, col_img = reduce_tiles(
        to_tiles(scaled, tile), row_sum, col_sum, pack_small((small_gram, proj_part)), n_row, n_col, 1,
        forward=True,
    )
    image = from_tiles(image_tiles)
    small_gram, small_proj = unpack_small(small, (small_gram, proj_part))

    factor = jnp.linalg.cholesky(small_gram)
    ritz_matrix = jax.scipy.linalg.cho_solve((factor, True), small_proj)
    residual = image - jnp.dot(ritz_matrix.T, current, precision=highest)

    def residual_of(img_tiles, cur_tiles):
        fitted = sum(ritz_matrix[l][None, :, None] * cur_tiles[:, l:l + 1, :] for l in range(k))
        return img_tiles - fitted

    row_res = residual_of(row_img, row_cur)
    col_res = residual_of(col_img, col_cur)
    row_sum, col_sum = slot_products(blocks, rows_here, cols_here, live_count, row_res, col_res, k)
    search_basis = jnp.concatenate([current, residual, previous], 0)
    row_basis = jnp.concatenate([row_cur, row_res, row_cp[:, k:]], 1)
    col_basis = jnp.concatenate([col_cur, col_res, col_cp[:, k:]], 1)
    scaled = diagonal[None, :] * residual
    correlation = dot_rows(search_basis, search_basis)
    residual_part = (
        dot_rows(search_basis, scaled) + tile_dot(row_basis, row_sum) + tile_dot(col_basis, col_sum)
    )
    mixed_part = jnp.concatenate(
        [dot_rows(search_basis, image), residual_part, dot_rows(search_basis, previous_image)], 1
    )
    image_tiles, small = reduce_tiles(
        to_tiles(scaled, tile), row_sum, col_sum, pack_small((correlation, mixed_part)), n_row, n_col, 2
    )
    residual_image = from_tiles(image_tiles)
    correlation, mixed_terms = unpack_small(small, (correlation, mixed_part))
    pencil = 0.5 * (mixed_terms + mixed_terms.T)
    lower_factor = jnp.linalg.cholesky(correlation)
    half_solve = jax.scipy.linalg.solve_triangular(lower_factor, pencil, lower=True)
    reduced = jax.scipy.linalg.solve_triangular(lower_factor, half_solve.T, lower=True)
    return (image, residual, residual_image, reduced)


def solution(mesh):
    n_row = mesh.shape["row"]
    n_col = mesh.shape["col"]
    return jax.shard_map(
        functools.partial(local, n_row, n_col),
        mesh=mesh,
        in_specs=(
            P("row", "col", None, None, None),
            P("row", "col", None),
            P("row", "col", None),
            P("row", "col"),
            P(("row", "col")),
            P(None, ("row", "col")),
            P(None, ("row", "col")),
            P(None, ("row", "col")),
        ),
        out_specs=(P(None, ("row", "col")), P(None, ("row", "col")), P(None, ("row", "col")), P()),
        check_vma=False,
    )
```

```python
import functools

import jax
import jax.numpy as jnp
from jax import lax
from jax.experimental import pallas as pl
from jax.experimental.pallas import tpu as pltpu
from jax.sharding import PartitionSpec as P

highest = lax.Precision.HIGHEST
group_width = 8
MESH = pl.DeviceIdType.MESH


def _barrier(n_row, n_col, r, c):
    barrier = pltpu.get_barrier_semaphore()

    def greet_col(k, carry):
        pl.semaphore_signal(barrier, 1, device_id=(r, lax.rem(c + k, n_col)), device_id_type=MESH)
        return carry

    def greet_row(k, carry):
        pl.semaphore_signal(barrier, 1, device_id=(lax.rem(r + k, n_row), c), device_id_type=MESH)
        return carry

    lax.fori_loop(1, n_col, greet_col, 0)
    lax.fori_loop(1, n_row, greet_row, 0)
    pl.semaphore_wait(barrier, n_row + n_col - 2)


def _gather_kernel(n_row, n_col, x_ref, rowv_ref, colv_ref, send_row, recv_row, send_col, recv_col, local_sem):
    vt = x_ref.shape[1]
    r = lax.axis_index("row")
    c = lax.axis_index("col")
    _barrier(n_row, n_col, r, c)

    def row_copy(j, src):
        return pltpu.make_async_remote_copy(
            src_ref=x_ref,
            dst_ref=rowv_ref.at[:, pl.ds(src * vt, vt)],
            send_sem=send_row.at[j],
            recv_sem=recv_row.at[src],
            device_id=(r, j),
            device_id_type=MESH,
        )

    def col_copy(i, src):
        return pltpu.make_async_remote_copy(
            src_ref=x_ref,
            dst_ref=colv_ref.at[:, pl.ds(src * vt, vt)],
            send_sem=send_col.at[i],
            recv_sem=recv_col.at[src],
            device_id=(i, c),
            device_id_type=MESH,
        )

    own_row = pltpu.make_async_copy(x_ref, rowv_ref.at[:, pl.ds(c * vt, vt)], local_sem.at[0])
    own_col = pltpu.make_async_copy(x_ref, colv_ref.at[:, pl.ds(r * vt, vt)], local_sem.at[1])
    own_row.start()
    own_col.start()

    def start_col(k, carry):
        row_copy(lax.rem(c + k, n_col), c).start()
        return carry

    def start_row(k, carry):
        col_copy(lax.rem(r + k, n_row), r).start()
        return carry

    lax.fori_loop(1, n_col, start_col, 0)
    lax.fori_loop(1, n_row, start_row, 0)

    def wait_col(k, carry):
        row_copy(lax.rem(c + k, n_col), c).wait_send()
        row_copy(c, lax.rem(c + n_col - k, n_col)).wait_recv()
        return carry

    def wait_row(k, carry):
        col_copy(lax.rem(r + k, n_row), r).wait_send()
        col_copy(r, lax.rem(r + n_row - k, n_row)).wait_recv()
        return carry

    lax.fori_loop(1, n_col, wait_col, 0)
    lax.fori_loop(1, n_row, wait_row, 0)
    own_row.wait()
    own_col.wait()


def gather_tiles(x_tiles, n_row, n_col, collective_id):
    k, vt = x_tiles.shape
    vmem = pl.BlockSpec(memory_space=pltpu.VMEM)
    return pl.pallas_call(
        functools.partial(_gather_kernel, n_row, n_col),
        out_shape=(
            jax.ShapeDtypeStruct((k, n_col * vt), x_tiles.dtype),
            jax.ShapeDtypeStruct((k, n_row * vt), x_tiles.dtype),
        ),
        in_specs=[vmem],
        out_specs=(vmem, vmem),
        scratch_shapes=[
            pltpu.SemaphoreType.DMA((n_col,)),
            pltpu.SemaphoreType.DMA((n_col,)),
            pltpu.SemaphoreType.DMA((n_row,)),
            pltpu.SemaphoreType.DMA((n_row,)),
            pltpu.SemaphoreType.DMA((2,)),
        ],
        compiler_params=pltpu.CompilerParams(collective_id=collective_id, has_side_effects=True),
    )(x_tiles)


def _reduce_kernel(n_row, n_col, forward, base_ref, rsum_ref, csum_ref, small_ref, out_ref, small_out, *rest):
    if forward:
        img_row, img_col = rest[:2]
        rest = rest[2:]
    (got_row, got_col, got_small_col, mid, got_small_row,
     send_row, recv_row, send_col, recv_col,
     send_small_col, recv_small_col, send_small_row, recv_small_row, local_sem) = rest[:14]
    vt = base_ref.shape[1]
    r = lax.axis_index("row")
    c = lax.axis_index("col")
    _barrier(n_row, n_col, r, c)

    def small_col_copy(j, src):
        return pltpu.make_async_remote_copy(
            src_ref=small_ref,
            dst_ref=got_small_col.at[src],
            send_sem=send_small_col.at[j],
            recv_sem=recv_small_col.at[src],
            device_id=(r, j),
            device_id_type=MESH,
        )

    def small_row_copy(i, src):
        return pltpu.make_async_remote_copy(
            src_ref=mid,
            dst_ref=got_small_row.at[src],
            send_sem=send_small_row.at[i],
            recv_sem=recv_small_row.at[src],
            device_id=(i, c),
            device_id_type=MESH,
        )

    def row_copy(j, src):
        return pltpu.make_async_remote_copy(
            src_ref=rsum_ref.at[:, pl.ds(j * vt, vt)],
            dst_ref=got_row.at[src],
            send_sem=send_row.at[j],
            recv_sem=recv_row.at[src],
            device_id=(r, j),
            device_id_type=MESH,
        )

    def col_copy(i, src):
        return pltpu.make_async_remote_copy(
            src_ref=csum_ref.at[:, pl.ds(i * vt, vt)],
            dst_ref=got_col.at[src],
            send_sem=send_col.at[i],
            recv_sem=recv_col.at[src],
            device_id=(i, c),
            device_id_type=MESH,
        )

    own_small = pltpu.make_async_copy(small_ref, got_small_col.at[c], local_sem.at[2])
    own_small.start()

    def start_small_col(k, carry):
        small_col_copy(lax.rem(c + k, n_col), c).start()
        return carry

    lax.fori_loop(1, n_col, start_small_col, 0)

    own_row = pltpu.make_async_copy(rsum_ref.at[:, pl.ds(c * vt, vt)], got_row.at[c], local_sem.at[0])
    own_col = pltpu.make_async_copy(csum_ref.at[:, pl.ds(r * vt, vt)], got_col.at[r], local_sem.at[1])
    own_row.start()
    own_col.start()

    def start_col(k, carry):
        row_copy(lax.rem(c + k, n_col), c).start()
        return carry

    def start_row(k, carry):
        col_copy(lax.rem(r + k, n_row), r).start()
        return carry

    lax.fori_loop(1, n_row, start_row, 0)
    lax.fori_loop(1, n_col, start_col, 0)

    def wait_small_col(k, carry):
        small_col_copy(lax.rem(c + k, n_col), c).wait_send()
        small_col_copy(c, lax.rem(c + n_col - k, n_col)).wait_recv()
        return carry

    lax.fori_loop(1, n_col, wait_small_col, 0)
    own_small.wait()
    mid[...] = jnp.sum(got_small_col[...], axis=0)

    own_mid = pltpu.make_async_copy(mid, got_small_row.at[r], local_sem.at[3])
    own_mid.start()

    def start_small_row(k, carry):
        small_row_copy(lax.rem(r + k, n_row), r).start()
        return carry

    lax.fori_loop(1, n_row, start_small_row, 0)

    def wait_col(k, carry):
        row_copy(lax.rem(c + k, n_col), c).wait_send()
        row_copy(c, lax.rem(c + n_col - k, n_col)).wait_recv()
        return carry

    def wait_row(k, carry):
        col_copy(lax.rem(r + k, n_row), r).wait_send()
        col_copy(r, lax.rem(r + n_row - k, n_row)).wait_recv()
        return carry

    lax.fori_loop(1, n_col, wait_col, 0)
    lax.fori_loop(1, n_row, wait_row, 0)
    own_row.wait()
    own_col.wait()
    out_ref[...] = base_ref[...] + jnp.sum(got_row[...], axis=0) + jnp.sum(got_col[...], axis=0)

    if forward:
        send_fr, recv_fr, send_fc, recv_fc = rest[14:]

        def fwd_row_copy(j, src):
            return pltpu.make_async_remote_copy(
                src_ref=out_ref,
                dst_ref=img_row.at[:, pl.ds(src * vt, vt)],
                send_sem=send_fr.at[j],
                recv_sem=recv_fr.at[src],
                device_id=(r, j),
                device_id_type=MESH,
            )

        def fwd_col_copy(i, src):
            return pltpu.make_async_remote_copy(
                src_ref=out_ref,
                dst_ref=img_col.at[:, pl.ds(src * vt, vt)],
                send_sem=send_fc.at[i],
                recv_sem=recv_fc.at[src],
                device_id=(i, c),
                device_id_type=MESH,
            )

        own_fr = pltpu.make_async_copy(out_ref, img_row.at[:, pl.ds(c * vt, vt)], local_sem.at[4])
        own_fc = pltpu.make_async_copy(out_ref, img_col.at[:, pl.ds(r * vt, vt)], local_sem.at[5])
        own_fr.start()
        own_fc.start()

        def start_fr(k, carry):
            fwd_row_copy(lax.rem(c + k, n_col), c).start()
            return carry

        def start_fc(k, carry):
            fwd_col_copy(lax.rem(r + k, n_row), r).start()
            return carry

        lax.fori_loop(1, n_row, start_fc, 0)
        lax.fori_loop(1, n_col, start_fr, 0)

    def wait_small_row(k, carry):
        small_row_copy(lax.rem(r + k, n_row), r).wait_send()
        small_row_copy(r, lax.rem(r + n_row - k, n_row)).wait_recv()
        return carry

    lax.fori_loop(1, n_row, wait_small_row, 0)
    own_mid.wait()
    small_out[...] = jnp.sum(got_small_row[...], axis=0)

    if forward:
        def wait_fr(k, carry):
            fwd_row_copy(lax.rem(c + k, n_col), c).wait_send()
            fwd_row_copy(c, lax.rem(c + n_col - k, n_col)).wait_recv()
            return carry

        def wait_fc(k, carry):
            fwd_col_copy(lax.rem(r + k, n_row), r).wait_send()
            fwd_col_copy(r, lax.rem(r + n_row - k, n_row)).wait_recv()
            return carry

        lax.fori_loop(1, n_col, wait_fr, 0)
        lax.fori_loop(1, n_row, wait_fc, 0)
        own_fr.wait()
        own_fc.wait()


def pack_small(values):
    flat = jnp.concatenate([v.reshape(-1) for v in values])
    tile = 8 * 128
    padded = -(-flat.shape[0] // tile) * tile
    return jnp.pad(flat, (0, padded - flat.shape[0])).reshape(-1, 128)


def unpack_small(total, values):
    total = total.reshape(-1)
    out, start = [], 0
    for v in values:
        out.append(total[start:start + v.size].reshape(v.shape))
        start += v.size
    return out


def reduce_tiles(base_tiles, row_sum, col_sum, small, n_row, n_col, collective_id, forward=False):
    k, vt = base_tiles.shape
    s = small.shape[0]
    vmem = pl.BlockSpec(memory_space=pltpu.VMEM)
    out_shape = [
        jax.ShapeDtypeStruct((k, vt), base_tiles.dtype),
        jax.ShapeDtypeStruct((s, 128), jnp.float32),
    ]
    extra_sems = []
    if forward:
        out_shape += [
            jax.ShapeDtypeStruct((k, n_col * vt), base_tiles.dtype),
            jax.ShapeDtypeStruct((k, n_row * vt), base_tiles.dtype),
        ]
        extra_sems = [
            pltpu.SemaphoreType.DMA((n_col,)),
            pltpu.SemaphoreType.DMA((n_col,)),
            pltpu.SemaphoreType.DMA((n_row,)),
            pltpu.SemaphoreType.DMA((n_row,)),
        ]
    return pl.pallas_call(
        functools.partial(_reduce_kernel, n_row, n_col, forward),
        out_shape=tuple(out_shape),
        in_specs=[vmem, vmem, vmem, vmem],
        out_specs=tuple(vmem for _ in out_shape),
        scratch_shapes=[
            pltpu.VMEM((n_col, k, vt), jnp.float32),
            pltpu.VMEM((n_row, k, vt), jnp.float32),
            pltpu.VMEM((n_col, s, 128), jnp.float32),
            pltpu.VMEM((s, 128), jnp.float32),
            pltpu.VMEM((n_row, s, 128), jnp.float32),
            pltpu.SemaphoreType.DMA((n_col,)),
            pltpu.SemaphoreType.DMA((n_col,)),
            pltpu.SemaphoreType.DMA((n_row,)),
            pltpu.SemaphoreType.DMA((n_row,)),
            pltpu.SemaphoreType.DMA((n_col,)),
            pltpu.SemaphoreType.DMA((n_col,)),
            pltpu.SemaphoreType.DMA((n_row,)),
            pltpu.SemaphoreType.DMA((n_row,)),
            pltpu.SemaphoreType.DMA((6,)),
        ] + extra_sems,
        compiler_params=pltpu.CompilerParams(collective_id=collective_id, has_side_effects=True),
    )(base_tiles, row_sum, col_sum, small)


def _slots_kernel(group, rows_k, tile, rows_ref, cols_ref, count_ref, tiles_ref, rowv_ref, colv_ref,
                  rsum_ref, csum_ref):
    g = pl.program_id(0)

    @pl.when(g == 0)
    def _():
        rsum_ref[...] = jnp.zeros_like(rsum_ref)
        csum_ref[...] = jnp.zeros_like(csum_ref)

    for s in range(group):
        slot = g * group + s

        @pl.when(slot < count_ref[0])
        def _():
            a = pl.multiple_of(rows_ref[slot] * tile, tile)
            b = pl.multiple_of(cols_ref[slot] * tile, tile)
            high, low = split_bf16(tiles_ref[s])
            rsum_ref[:, pl.ds(a, tile)] += dot3(
                split_bf16(colv_ref[pl.ds(0, rows_k), pl.ds(b, tile)]),
                jnp.concatenate([high, low], axis=0), (((1,), (1,)), ((), ())),
            )
            csum_ref[:, pl.ds(b, tile)] += dot3(
                split_bf16(rowv_ref[pl.ds(0, rows_k), pl.ds(a, tile)]),
                jnp.concatenate([high, low], axis=1), (((1,), (0,)), ((), ())),
            )


def split_bf16(x):
    high = x.astype(jnp.bfloat16)
    return high, (x - high.astype(jnp.float32)).astype(jnp.bfloat16)


def dot3(left, right, dims):
    rows = left[0].shape[0]
    both = lax.dot_general(
        jnp.concatenate([left[0], left[1]], axis=0), right, dims, preferred_element_type=jnp.float32
    )
    width = both.shape[1] // 2
    return both[:rows, :width] + (both[rows:, :width] + both[:rows, width:])


def slot_products(blocks, rows_here, cols_here, live_count, row_tiles, column_tiles, rows_k):
    slot_count, tile, _ = blocks.shape
    sums_shape = lambda v: (rows_k, v.shape[1])
    group = group_width
    groups = slot_count // group

    def tile_map(g, rows, cols, count):
        last = jnp.maximum(count[0] - 1, 0) // group
        return (jnp.minimum(g, last), 0, 0)

    def whole(g, rows, cols, count):
        return (0, 0)

    grid_spec = pltpu.PrefetchScalarGridSpec(
        num_scalar_prefetch=3,
        grid=(groups,),
        in_specs=[
            pl.BlockSpec((group, tile, tile), tile_map),
            pl.BlockSpec(row_tiles.shape, whole),
            pl.BlockSpec(column_tiles.shape, whole),
        ],
        out_specs=[
            pl.BlockSpec(sums_shape(row_tiles), whole),
            pl.BlockSpec(sums_shape(column_tiles), whole),
        ],
    )
    return pl.pallas_call(
        functools.partial(_slots_kernel, group, rows_k, tile),
        grid_spec=grid_spec,
        out_shape=(
            jax.ShapeDtypeStruct(sums_shape(row_tiles), jnp.float32),
            jax.ShapeDtypeStruct(sums_shape(column_tiles), jnp.float32),
        ),
        compiler_params=pltpu.CompilerParams(dimension_semantics=("arbitrary",)),
    )(rows_here, cols_here, live_count.reshape(1), blocks, row_tiles, column_tiles)


def tile_dot(left, right):
    return jnp.dot(left, right.T, precision=highest)


def dot_rows(left, right):
    return jnp.dot(left, right.T, precision=highest)


def local(n_row, n_col, tile_values, tile_row, tile_col, counts, diagonal, current, previous, previous_image):
    k = current.shape[0]
    tile = tile_values.shape[-1]
    slot_count = tile_values.shape[2]
    blocks = tile_values.reshape(slot_count, tile, tile)
    rows_here = tile_row.reshape(slot_count)
    cols_here = tile_col.reshape(slot_count)
    live_count = counts.reshape(())

    row_cp, col_cp = gather_tiles(jnp.concatenate([current, previous], 0), n_row, n_col, 0)
    row_sum, col_sum = slot_products(blocks, rows_here, cols_here, live_count, row_cp, col_cp, k)
    row_cur, col_cur = row_cp[:k], col_cp[:k]
    scaled = diagonal[None, :] * current
    small_gram = dot_rows(current, current)
    proj_part = dot_rows(current, scaled) + tile_dot(row_cur, row_sum) + tile_dot(col_cur, col_sum)
    image_tiles, small, row_img, col_img = reduce_tiles(
        scaled, row_sum, col_sum, pack_small((small_gram, proj_part)), n_row, n_col, 1,
        forward=True,
    )
    image = image_tiles
    small_gram, small_proj = unpack_small(small, (small_gram, proj_part))

    factor = jnp.linalg.cholesky(small_gram)
    ritz_matrix = jax.scipy.linalg.cho_solve((factor, True), small_proj)
    residual = image - jnp.dot(ritz_matrix.T, current, precision=highest)

    def residual_of(img_tiles, cur_tiles):
        fitted = sum(ritz_matrix[l][:, None] * cur_tiles[l:l + 1, :] for l in range(k))
        return img_tiles - fitted

    row_res = residual_of(row_img, row_cur)
    col_res = residual_of(col_img, col_cur)
    row_sum, col_sum = slot_products(blocks, rows_here, cols_here, live_count, row_res, col_res, k)
    search_basis = jnp.concatenate([current, residual, previous], 0)
    row_basis = jnp.concatenate([row_cur, row_res, row_cp[k:]], 0)
    col_basis = jnp.concatenate([col_cur, col_res, col_cp[k:]], 0)
    scaled = diagonal[None, :] * residual
    correlation = dot_rows(search_basis, search_basis)
    residual_part = (
        dot_rows(search_basis, scaled) + tile_dot(row_basis, row_sum) + tile_dot(col_basis, col_sum)
    )
    mixed_part = jnp.concatenate(
        [dot_rows(search_basis, image), residual_part, dot_rows(search_basis, previous_image)], 1
    )
    image_tiles, small = reduce_tiles(
        scaled, row_sum, col_sum, pack_small((correlation, mixed_part)), n_row, n_col, 2
    )
    residual_image = image_tiles
    correlation, mixed_terms = unpack_small(small, (correlation, mixed_part))
    pencil = 0.5 * (mixed_terms + mixed_terms.T)
    lower_factor = jnp.linalg.cholesky(correlation)
    half_solve = jax.scipy.linalg.solve_triangular(lower_factor, pencil, lower=True)
    reduced = jax.scipy.linalg.solve_triangular(lower_factor, half_solve.T, lower=True)
    return (image, residual, residual_image, reduced)


def solution(mesh):
    n_row = mesh.shape["row"]
    n_col = mesh.shape["col"]
    return jax.shard_map(
        functools.partial(local, n_row, n_col),
        mesh=mesh,
        in_specs=(
            P("row", "col", None, None, None),
            P("row", "col", None),
            P("row", "col", None),
            P("row", "col"),
            P(("row", "col")),
            P(None, ("row", "col")),
            P(None, ("row", "col")),
            P(None, ("row", "col")),
        ),
        out_specs=(P(None, ("row", "col")), P(None, ("row", "col")), P(None, ("row", "col")), P()),
        check_vma=False,
    )
```

```python
import functools

import jax
import jax.numpy as jnp
from jax import lax
from jax.experimental import pallas as pl
from jax.experimental.pallas import tpu as pltpu
from jax.sharding import PartitionSpec as P

highest = lax.Precision.HIGHEST
group_width = 8
MESH = pl.DeviceIdType.MESH


def _barrier(n_row, n_col, r, c):
    barrier = pltpu.get_barrier_semaphore()

    def greet_col(k, carry):
        pl.semaphore_signal(barrier, 1, device_id=(r, lax.rem(c + k, n_col)), device_id_type=MESH)
        return carry

    def greet_row(k, carry):
        pl.semaphore_signal(barrier, 1, device_id=(lax.rem(r + k, n_row), c), device_id_type=MESH)
        return carry

    lax.fori_loop(1, n_col, greet_col, 0)
    lax.fori_loop(1, n_row, greet_row, 0)
    pl.semaphore_wait(barrier, n_row + n_col - 2)


def _gather_kernel(n_row, n_col, x_ref, rowv_ref, colv_ref, send_row, recv_row, send_col, recv_col, local_sem):
    vt = x_ref.shape[1]
    r = lax.axis_index("row")
    c = lax.axis_index("col")
    _barrier(n_row, n_col, r, c)

    def row_copy(j, src):
        return pltpu.make_async_remote_copy(
            src_ref=x_ref,
            dst_ref=rowv_ref.at[:, pl.ds(src * vt, vt)],
            send_sem=send_row.at[j],
            recv_sem=recv_row.at[src],
            device_id=(r, j),
            device_id_type=MESH,
        )

    def col_copy(i, src):
        return pltpu.make_async_remote_copy(
            src_ref=x_ref,
            dst_ref=colv_ref.at[:, pl.ds(src * vt, vt)],
            send_sem=send_col.at[i],
            recv_sem=recv_col.at[src],
            device_id=(i, c),
            device_id_type=MESH,
        )

    own_row = pltpu.make_async_copy(x_ref, rowv_ref.at[:, pl.ds(c * vt, vt)], local_sem.at[0])
    own_col = pltpu.make_async_copy(x_ref, colv_ref.at[:, pl.ds(r * vt, vt)], local_sem.at[1])
    own_row.start()
    own_col.start()

    def start_col(k, carry):
        row_copy(lax.rem(c + k, n_col), c).start()
        return carry

    def start_row(k, carry):
        col_copy(lax.rem(r + k, n_row), r).start()
        return carry

    lax.fori_loop(1, n_col, start_col, 0)
    lax.fori_loop(1, n_row, start_row, 0)

    def wait_col(k, carry):
        row_copy(lax.rem(c + k, n_col), c).wait_send()
        row_copy(c, lax.rem(c + n_col - k, n_col)).wait_recv()
        return carry

    def wait_row(k, carry):
        col_copy(lax.rem(r + k, n_row), r).wait_send()
        col_copy(r, lax.rem(r + n_row - k, n_row)).wait_recv()
        return carry

    lax.fori_loop(1, n_col, wait_col, 0)
    lax.fori_loop(1, n_row, wait_row, 0)
    own_row.wait()
    own_col.wait()


def gather_tiles(x_tiles, n_row, n_col, collective_id):
    k, vt = x_tiles.shape
    vmem = pl.BlockSpec(memory_space=pltpu.VMEM)
    return pl.pallas_call(
        functools.partial(_gather_kernel, n_row, n_col),
        out_shape=(
            jax.ShapeDtypeStruct((k, n_col * vt), x_tiles.dtype),
            jax.ShapeDtypeStruct((k, n_row * vt), x_tiles.dtype),
        ),
        in_specs=[vmem],
        out_specs=(vmem, vmem),
        scratch_shapes=[
            pltpu.SemaphoreType.DMA((n_col,)),
            pltpu.SemaphoreType.DMA((n_col,)),
            pltpu.SemaphoreType.DMA((n_row,)),
            pltpu.SemaphoreType.DMA((n_row,)),
            pltpu.SemaphoreType.DMA((2,)),
        ],
        compiler_params=pltpu.CompilerParams(collective_id=collective_id, has_side_effects=True),
    )(x_tiles)


def _reduce_kernel(n_row, n_col, forward, base_ref, rsum_ref, csum_ref, small_ref, out_ref, small_out, *rest):
    if forward:
        img_row, img_col = rest[:2]
        rest = rest[2:]
    (got_row, got_col, got_small_col, mid, got_small_row,
     send_row, recv_row, send_col, recv_col,
     send_small_col, recv_small_col, send_small_row, recv_small_row, local_sem) = rest[:14]
    vt = base_ref.shape[1]
    r = lax.axis_index("row")
    c = lax.axis_index("col")
    _barrier(n_row, n_col, r, c)

    def small_col_copy(j, src):
        return pltpu.make_async_remote_copy(
            src_ref=small_ref,
            dst_ref=got_small_col.at[src],
            send_sem=send_small_col.at[j],
            recv_sem=recv_small_col.at[src],
            device_id=(r, j),
            device_id_type=MESH,
        )

    def small_row_copy(i, src):
        return pltpu.make_async_remote_copy(
            src_ref=mid,
            dst_ref=got_small_row.at[src],
            send_sem=send_small_row.at[i],
            recv_sem=recv_small_row.at[src],
            device_id=(i, c),
            device_id_type=MESH,
        )

    def row_copy(j, src):
        return pltpu.make_async_remote_copy(
            src_ref=rsum_ref.at[:, pl.ds(j * vt, vt)],
            dst_ref=got_row.at[src],
            send_sem=send_row.at[j],
            recv_sem=recv_row.at[src],
            device_id=(r, j),
            device_id_type=MESH,
        )

    def col_copy(i, src):
        return pltpu.make_async_remote_copy(
            src_ref=csum_ref.at[:, pl.ds(i * vt, vt)],
            dst_ref=got_col.at[src],
            send_sem=send_col.at[i],
            recv_sem=recv_col.at[src],
            device_id=(i, c),
            device_id_type=MESH,
        )

    own_small = pltpu.make_async_copy(small_ref, got_small_col.at[c], local_sem.at[2])
    own_small.start()

    def start_small_col(k, carry):
        small_col_copy(lax.rem(c + k, n_col), c).start()
        return carry

    lax.fori_loop(1, n_col, start_small_col, 0)


    def wait_small_col(k, carry):
        small_col_copy(lax.rem(c + k, n_col), c).wait_send()
        small_col_copy(c, lax.rem(c + n_col - k, n_col)).wait_recv()
        return carry

    lax.fori_loop(1, n_col, wait_small_col, 0)
    own_small.wait()
    mid[...] = jnp.sum(got_small_col[...], axis=0)

    own_mid = pltpu.make_async_copy(mid, got_small_row.at[r], local_sem.at[3])
    own_mid.start()

    def start_small_row(k, carry):
        small_row_copy(lax.rem(r + k, n_row), r).start()
        return carry

    lax.fori_loop(1, n_row, start_small_row, 0)

    own_row = pltpu.make_async_copy(rsum_ref.at[:, pl.ds(c * vt, vt)], got_row.at[c], local_sem.at[0])
    own_col = pltpu.make_async_copy(csum_ref.at[:, pl.ds(r * vt, vt)], got_col.at[r], local_sem.at[1])
    own_row.start()
    own_col.start()

    def start_col(k, carry):
        row_copy(lax.rem(c + k, n_col), c).start()
        return carry

    def start_row(k, carry):
        col_copy(lax.rem(r + k, n_row), r).start()
        return carry

    lax.fori_loop(1, n_row, start_row, 0)
    lax.fori_loop(1, n_col, start_col, 0)

    def wait_col(k, carry):
        row_copy(lax.rem(c + k, n_col), c).wait_send()
        row_copy(c, lax.rem(c + n_col - k, n_col)).wait_recv()
        return carry

    def wait_row(k, carry):
        col_copy(lax.rem(r + k, n_row), r).wait_send()
        col_copy(r, lax.rem(r + n_row - k, n_row)).wait_recv()
        return carry

    lax.fori_loop(1, n_col, wait_col, 0)
    lax.fori_loop(1, n_row, wait_row, 0)
    own_row.wait()
    own_col.wait()
    out_ref[...] = base_ref[...] + jnp.sum(got_row[...], axis=0) + jnp.sum(got_col[...], axis=0)

    if forward:
        send_fr, recv_fr, send_fc, recv_fc = rest[14:]

        def fwd_row_copy(j, src):
            return pltpu.make_async_remote_copy(
                src_ref=out_ref,
                dst_ref=img_row.at[:, pl.ds(src * vt, vt)],
                send_sem=send_fr.at[j],
                recv_sem=recv_fr.at[src],
                device_id=(r, j),
                device_id_type=MESH,
            )

        def fwd_col_copy(i, src):
            return pltpu.make_async_remote_copy(
                src_ref=out_ref,
                dst_ref=img_col.at[:, pl.ds(src * vt, vt)],
                send_sem=send_fc.at[i],
                recv_sem=recv_fc.at[src],
                device_id=(i, c),
                device_id_type=MESH,
            )

        own_fr = pltpu.make_async_copy(out_ref, img_row.at[:, pl.ds(c * vt, vt)], local_sem.at[4])
        own_fc = pltpu.make_async_copy(out_ref, img_col.at[:, pl.ds(r * vt, vt)], local_sem.at[5])
        own_fr.start()
        own_fc.start()

        def start_fr(k, carry):
            fwd_row_copy(lax.rem(c + k, n_col), c).start()
            return carry

        def start_fc(k, carry):
            fwd_col_copy(lax.rem(r + k, n_row), r).start()
            return carry

        lax.fori_loop(1, n_row, start_fc, 0)
        lax.fori_loop(1, n_col, start_fr, 0)

    def wait_small_row(k, carry):
        small_row_copy(lax.rem(r + k, n_row), r).wait_send()
        small_row_copy(r, lax.rem(r + n_row - k, n_row)).wait_recv()
        return carry

    lax.fori_loop(1, n_row, wait_small_row, 0)
    own_mid.wait()
    small_out[...] = jnp.sum(got_small_row[...], axis=0)

    if forward:
        def wait_fr(k, carry):
            fwd_row_copy(lax.rem(c + k, n_col), c).wait_send()
            fwd_row_copy(c, lax.rem(c + n_col - k, n_col)).wait_recv()
            return carry

        def wait_fc(k, carry):
            fwd_col_copy(lax.rem(r + k, n_row), r).wait_send()
            fwd_col_copy(r, lax.rem(r + n_row - k, n_row)).wait_recv()
            return carry

        lax.fori_loop(1, n_col, wait_fr, 0)
        lax.fori_loop(1, n_row, wait_fc, 0)
        own_fr.wait()
        own_fc.wait()


def pack_small(values):
    flat = jnp.concatenate([v.reshape(-1) for v in values])
    tile = 8 * 128
    padded = -(-flat.shape[0] // tile) * tile
    return jnp.pad(flat, (0, padded - flat.shape[0])).reshape(-1, 128)


def unpack_small(total, values):
    total = total.reshape(-1)
    out, start = [], 0
    for v in values:
        out.append(total[start:start + v.size].reshape(v.shape))
        start += v.size
    return out


def reduce_tiles(base_tiles, row_sum, col_sum, small, n_row, n_col, collective_id, forward=False):
    k, vt = base_tiles.shape
    s = small.shape[0]
    vmem = pl.BlockSpec(memory_space=pltpu.VMEM)
    out_shape = [
        jax.ShapeDtypeStruct((k, vt), base_tiles.dtype),
        jax.ShapeDtypeStruct((s, 128), jnp.float32),
    ]
    extra_sems = []
    if forward:
        out_shape += [
            jax.ShapeDtypeStruct((k, n_col * vt), base_tiles.dtype),
            jax.ShapeDtypeStruct((k, n_row * vt), base_tiles.dtype),
        ]
        extra_sems = [
            pltpu.SemaphoreType.DMA((n_col,)),
            pltpu.SemaphoreType.DMA((n_col,)),
            pltpu.SemaphoreType.DMA((n_row,)),
            pltpu.SemaphoreType.DMA((n_row,)),
        ]
    return pl.pallas_call(
        functools.partial(_reduce_kernel, n_row, n_col, forward),
        out_shape=tuple(out_shape),
        in_specs=[vmem, vmem, vmem, vmem],
        out_specs=tuple(vmem for _ in out_shape),
        scratch_shapes=[
            pltpu.VMEM((n_col, k, vt), jnp.float32),
            pltpu.VMEM((n_row, k, vt), jnp.float32),
            pltpu.VMEM((n_col, s, 128), jnp.float32),
            pltpu.VMEM((s, 128), jnp.float32),
            pltpu.VMEM((n_row, s, 128), jnp.float32),
            pltpu.SemaphoreType.DMA((n_col,)),
            pltpu.SemaphoreType.DMA((n_col,)),
            pltpu.SemaphoreType.DMA((n_row,)),
            pltpu.SemaphoreType.DMA((n_row,)),
            pltpu.SemaphoreType.DMA((n_col,)),
            pltpu.SemaphoreType.DMA((n_col,)),
            pltpu.SemaphoreType.DMA((n_row,)),
            pltpu.SemaphoreType.DMA((n_row,)),
            pltpu.SemaphoreType.DMA((6,)),
        ] + extra_sems,
        compiler_params=pltpu.CompilerParams(collective_id=collective_id, has_side_effects=True),
    )(base_tiles, row_sum, col_sum, small)


def _slots_kernel(group, rows_k, tile, rows_ref, cols_ref, count_ref, tiles_ref, rowv_ref, colv_ref,
                  rsum_ref, csum_ref):
    g = pl.program_id(0)

    @pl.when(g == 0)
    def _():
        rsum_ref[...] = jnp.zeros_like(rsum_ref)
        csum_ref[...] = jnp.zeros_like(csum_ref)

    for s in range(group):
        slot = g * group + s

        @pl.when(slot < count_ref[0])
        def _():
            a = pl.multiple_of(rows_ref[slot] * tile, tile)
            b = pl.multiple_of(cols_ref[slot] * tile, tile)
            high, low = split_bf16(tiles_ref[s])
            rsum_ref[:, pl.ds(a, tile)] += dot3(
                split_bf16(colv_ref[pl.ds(0, rows_k), pl.ds(b, tile)]),
                jnp.concatenate([high, low], axis=0), (((1,), (1,)), ((), ())),
            )
            csum_ref[:, pl.ds(b, tile)] += dot3(
                split_bf16(rowv_ref[pl.ds(0, rows_k), pl.ds(a, tile)]),
                jnp.concatenate([high, low], axis=1), (((1,), (0,)), ((), ())),
            )


def split_bf16(x):
    high = x.astype(jnp.bfloat16)
    return high, (x - high.astype(jnp.float32)).astype(jnp.bfloat16)


def dot3(left, right, dims):
    rows = left[0].shape[0]
    both = lax.dot_general(
        jnp.concatenate([left[0], left[1]], axis=0), right, dims, preferred_element_type=jnp.float32
    )
    width = both.shape[1] // 2
    return both[:rows, :width] + (both[rows:, :width] + both[:rows, width:])


def slot_products(blocks, rows_here, cols_here, live_count, row_tiles, column_tiles, rows_k):
    slot_count, tile, _ = blocks.shape
    sums_shape = lambda v: (rows_k, v.shape[1])
    group = group_width
    groups = slot_count // group

    def tile_map(g, rows, cols, count):
        last = jnp.maximum(count[0] - 1, 0) // group
        return (jnp.minimum(g, last), 0, 0)

    def whole(g, rows, cols, count):
        return (0, 0)

    grid_spec = pltpu.PrefetchScalarGridSpec(
        num_scalar_prefetch=3,
        grid=(groups,),
        in_specs=[
            pl.BlockSpec((group, tile, tile), tile_map),
            pl.BlockSpec(row_tiles.shape, whole),
            pl.BlockSpec(column_tiles.shape, whole),
        ],
        out_specs=[
            pl.BlockSpec(sums_shape(row_tiles), whole),
            pl.BlockSpec(sums_shape(column_tiles), whole),
        ],
    )
    return pl.pallas_call(
        functools.partial(_slots_kernel, group, rows_k, tile),
        grid_spec=grid_spec,
        out_shape=(
            jax.ShapeDtypeStruct(sums_shape(row_tiles), jnp.float32),
            jax.ShapeDtypeStruct(sums_shape(column_tiles), jnp.float32),
        ),
        compiler_params=pltpu.CompilerParams(dimension_semantics=("arbitrary",)),
    )(rows_here, cols_here, live_count.reshape(1), blocks, row_tiles, column_tiles)


def tile_dot(left, right):
    return jnp.dot(left, right.T, precision=highest)


def dot_rows(left, right):
    return jnp.dot(left, right.T, precision=highest)


def local(n_row, n_col, tile_values, tile_row, tile_col, counts, diagonal, current, previous, previous_image):
    k = current.shape[0]
    tile = tile_values.shape[-1]
    slot_count = tile_values.shape[2]
    blocks = tile_values.reshape(slot_count, tile, tile)
    rows_here = tile_row.reshape(slot_count)
    cols_here = tile_col.reshape(slot_count)
    live_count = counts.reshape(())

    row_cp, col_cp = gather_tiles(jnp.concatenate([current, previous], 0), n_row, n_col, 0)
    row_sum, col_sum = slot_products(blocks, rows_here, cols_here, live_count, row_cp, col_cp, k)
    row_cur, col_cur = row_cp[:k], col_cp[:k]
    scaled = diagonal[None, :] * current
    small_gram = dot_rows(current, current)
    proj_part = dot_rows(current, scaled) + tile_dot(row_cur, row_sum) + tile_dot(col_cur, col_sum)
    image_tiles, small, row_img, col_img = reduce_tiles(
        scaled, row_sum, col_sum, pack_small((small_gram, proj_part)), n_row, n_col, 1,
        forward=True,
    )
    image = image_tiles
    small_gram, small_proj = unpack_small(small, (small_gram, proj_part))

    factor = jnp.linalg.cholesky(small_gram)
    ritz_matrix = jax.scipy.linalg.cho_solve((factor, True), small_proj)
    residual = image - jnp.dot(ritz_matrix.T, current, precision=highest)

    def residual_of(img_tiles, cur_tiles):
        fitted = sum(ritz_matrix[l][:, None] * cur_tiles[l:l + 1, :] for l in range(k))
        return img_tiles - fitted

    row_res = residual_of(row_img, row_cur)
    col_res = residual_of(col_img, col_cur)
    row_sum, col_sum = slot_products(blocks, rows_here, cols_here, live_count, row_res, col_res, k)
    search_basis = jnp.concatenate([current, residual, previous], 0)
    row_basis = jnp.concatenate([row_cur, row_res, row_cp[k:]], 0)
    col_basis = jnp.concatenate([col_cur, col_res, col_cp[k:]], 0)
    scaled = diagonal[None, :] * residual
    correlation = dot_rows(search_basis, search_basis)
    residual_part = (
        dot_rows(search_basis, scaled) + tile_dot(row_basis, row_sum) + tile_dot(col_basis, col_sum)
    )
    mixed_part = jnp.concatenate(
        [dot_rows(search_basis, image), residual_part, dot_rows(search_basis, previous_image)], 1
    )
    image_tiles, small = reduce_tiles(
        scaled, row_sum, col_sum, pack_small((correlation, mixed_part)), n_row, n_col, 2
    )
    residual_image = image_tiles
    correlation, mixed_terms = unpack_small(small, (correlation, mixed_part))
    pencil = 0.5 * (mixed_terms + mixed_terms.T)
    lower_factor = jnp.linalg.cholesky(correlation)
    half_solve = jax.scipy.linalg.solve_triangular(lower_factor, pencil, lower=True)
    reduced = jax.scipy.linalg.solve_triangular(lower_factor, half_solve.T, lower=True)
    return (image, residual, residual_image, reduced)


def solution(mesh):
    n_row = mesh.shape["row"]
    n_col = mesh.shape["col"]
    return jax.shard_map(
        functools.partial(local, n_row, n_col),
        mesh=mesh,
        in_specs=(
            P("row", "col", None, None, None),
            P("row", "col", None),
            P("row", "col", None),
            P("row", "col"),
            P(("row", "col")),
            P(None, ("row", "col")),
            P(None, ("row", "col")),
            P(None, ("row", "col")),
        ),
        out_specs=(P(None, ("row", "col")), P(None, ("row", "col")), P(None, ("row", "col")), P()),
        check_vma=False,
    )
```

```python
import functools

import jax
import jax.numpy as jnp
from jax import lax
from jax.experimental import pallas as pl
from jax.experimental.pallas import tpu as pltpu
from jax.sharding import PartitionSpec as P

highest = lax.Precision.HIGHEST
group_width = 8
MESH = pl.DeviceIdType.MESH


def _barrier(n_row, n_col, r, c):
    barrier = pltpu.get_barrier_semaphore()

    def greet_col(k, carry):
        pl.semaphore_signal(barrier, 1, device_id=(r, lax.rem(c + k, n_col)), device_id_type=MESH)
        return carry

    def greet_row(k, carry):
        pl.semaphore_signal(barrier, 1, device_id=(lax.rem(r + k, n_row), c), device_id_type=MESH)
        return carry

    lax.fori_loop(1, n_col, greet_col, 0)
    lax.fori_loop(1, n_row, greet_row, 0)
    pl.semaphore_wait(barrier, n_row + n_col - 2)


def _gather_kernel(n_row, n_col, x_ref, rowv_ref, colv_ref, send_row, recv_row, send_col, recv_col, local_sem):
    vt = x_ref.shape[1]
    r = lax.axis_index("row")
    c = lax.axis_index("col")
    _barrier(n_row, n_col, r, c)

    def row_copy(j, src):
        return pltpu.make_async_remote_copy(
            src_ref=x_ref,
            dst_ref=rowv_ref.at[:, pl.ds(src * vt, vt)],
            send_sem=send_row.at[j],
            recv_sem=recv_row.at[src],
            device_id=(r, j),
            device_id_type=MESH,
        )

    def col_copy(i, src):
        return pltpu.make_async_remote_copy(
            src_ref=x_ref,
            dst_ref=colv_ref.at[:, pl.ds(src * vt, vt)],
            send_sem=send_col.at[i],
            recv_sem=recv_col.at[src],
            device_id=(i, c),
            device_id_type=MESH,
        )

    own_row = pltpu.make_async_copy(x_ref, rowv_ref.at[:, pl.ds(c * vt, vt)], local_sem.at[0])
    own_col = pltpu.make_async_copy(x_ref, colv_ref.at[:, pl.ds(r * vt, vt)], local_sem.at[1])
    own_row.start()
    own_col.start()

    def start_col(k, carry):
        row_copy(lax.rem(c + k, n_col), c).start()
        return carry

    def start_row(k, carry):
        col_copy(lax.rem(r + k, n_row), r).start()
        return carry

    lax.fori_loop(1, n_col, start_col, 0)
    lax.fori_loop(1, n_row, start_row, 0)

    def wait_col(k, carry):
        row_copy(lax.rem(c + k, n_col), c).wait_send()
        row_copy(c, lax.rem(c + n_col - k, n_col)).wait_recv()
        return carry

    def wait_row(k, carry):
        col_copy(lax.rem(r + k, n_row), r).wait_send()
        col_copy(r, lax.rem(r + n_row - k, n_row)).wait_recv()
        return carry

    lax.fori_loop(1, n_col, wait_col, 0)
    lax.fori_loop(1, n_row, wait_row, 0)
    own_row.wait()
    own_col.wait()


def gather_tiles(x_tiles, n_row, n_col, collective_id):
    k, vt = x_tiles.shape
    vmem = pl.BlockSpec(memory_space=pltpu.VMEM)
    return pl.pallas_call(
        functools.partial(_gather_kernel, n_row, n_col),
        out_shape=(
            jax.ShapeDtypeStruct((k, n_col * vt), x_tiles.dtype),
            jax.ShapeDtypeStruct((k, n_row * vt), x_tiles.dtype),
        ),
        in_specs=[vmem],
        out_specs=(vmem, vmem),
        scratch_shapes=[
            pltpu.SemaphoreType.DMA((n_col,)),
            pltpu.SemaphoreType.DMA((n_col,)),
            pltpu.SemaphoreType.DMA((n_row,)),
            pltpu.SemaphoreType.DMA((n_row,)),
            pltpu.SemaphoreType.DMA((2,)),
        ],
        compiler_params=pltpu.CompilerParams(collective_id=collective_id, has_side_effects=True),
    )(x_tiles)


def _reduce_kernel(n_row, n_col, forward, base_ref, rsum_ref, csum_ref, small_ref, out_ref, small_out, *rest):
    if forward:
        img_row, img_col = rest[:2]
        rest = rest[2:]
    (got_row, got_col, got_small_col, mid, got_small_row,
     send_row, recv_row, send_col, recv_col,
     send_small_col, recv_small_col, send_small_row, recv_small_row, local_sem) = rest[:14]
    vt = base_ref.shape[1]
    r = lax.axis_index("row")
    c = lax.axis_index("col")
    _barrier(n_row, n_col, r, c)

    def small_col_copy(j, src):
        return pltpu.make_async_remote_copy(
            src_ref=small_ref,
            dst_ref=got_small_col.at[src],
            send_sem=send_small_col.at[j],
            recv_sem=recv_small_col.at[src],
            device_id=(r, j),
            device_id_type=MESH,
        )

    def small_row_copy(i, src):
        return pltpu.make_async_remote_copy(
            src_ref=mid,
            dst_ref=got_small_row.at[src],
            send_sem=send_small_row.at[i],
            recv_sem=recv_small_row.at[src],
            device_id=(i, c),
            device_id_type=MESH,
        )

    def row_copy(j, src):
        return pltpu.make_async_remote_copy(
            src_ref=rsum_ref.at[:, pl.ds(j * vt, vt)],
            dst_ref=got_row.at[src],
            send_sem=send_row.at[j],
            recv_sem=recv_row.at[src],
            device_id=(r, j),
            device_id_type=MESH,
        )

    def col_copy(i, src):
        return pltpu.make_async_remote_copy(
            src_ref=csum_ref.at[:, pl.ds(i * vt, vt)],
            dst_ref=got_col.at[src],
            send_sem=send_col.at[i],
            recv_sem=recv_col.at[src],
            device_id=(i, c),
            device_id_type=MESH,
        )

    own_small = pltpu.make_async_copy(small_ref, got_small_col.at[c], local_sem.at[2])
    own_small.start()

    def start_small_col(k, carry):
        small_col_copy(lax.rem(c + k, n_col), c).start()
        return carry

    lax.fori_loop(1, n_col, start_small_col, 0)

    own_row = pltpu.make_async_copy(rsum_ref.at[:, pl.ds(c * vt, vt)], got_row.at[c], local_sem.at[0])
    own_col = pltpu.make_async_copy(csum_ref.at[:, pl.ds(r * vt, vt)], got_col.at[r], local_sem.at[1])
    own_row.start()
    own_col.start()

    def start_col(k, carry):
        row_copy(lax.rem(c + k, n_col), c).start()
        return carry

    def start_row(k, carry):
        col_copy(lax.rem(r + k, n_row), r).start()
        return carry

    lax.fori_loop(1, n_row, start_row, 0)
    lax.fori_loop(1, n_col, start_col, 0)

    def wait_small_col(k, carry):
        small_col_copy(lax.rem(c + k, n_col), c).wait_send()
        small_col_copy(c, lax.rem(c + n_col - k, n_col)).wait_recv()
        return carry

    lax.fori_loop(1, n_col, wait_small_col, 0)
    own_small.wait()
    mid[...] = jnp.sum(got_small_col[...], axis=0)

    own_mid = pltpu.make_async_copy(mid, got_small_row.at[r], local_sem.at[3])
    own_mid.start()

    def start_small_row(k, carry):
        small_row_copy(lax.rem(r + k, n_row), r).start()
        return carry

    lax.fori_loop(1, n_row, start_small_row, 0)

    def wait_col(k, carry):
        row_copy(lax.rem(c + k, n_col), c).wait_send()
        row_copy(c, lax.rem(c + n_col - k, n_col)).wait_recv()
        return carry

    def wait_row(k, carry):
        col_copy(lax.rem(r + k, n_row), r).wait_send()
        col_copy(r, lax.rem(r + n_row - k, n_row)).wait_recv()
        return carry

    lax.fori_loop(1, n_col, wait_col, 0)
    lax.fori_loop(1, n_row, wait_row, 0)
    own_row.wait()
    own_col.wait()
    out_ref[...] = base_ref[...] + jnp.sum(got_row[...], axis=0) + jnp.sum(got_col[...], axis=0)

    if forward:
        send_fr, recv_fr, send_fc, recv_fc = rest[14:]

        def fwd_row_copy(j, src):
            return pltpu.make_async_remote_copy(
                src_ref=out_ref,
                dst_ref=img_row.at[:, pl.ds(src * vt, vt)],
                send_sem=send_fr.at[j],
                recv_sem=recv_fr.at[src],
                device_id=(r, j),
                device_id_type=MESH,
            )

        def fwd_col_copy(i, src):
            return pltpu.make_async_remote_copy(
                src_ref=out_ref,
                dst_ref=img_col.at[:, pl.ds(src * vt, vt)],
                send_sem=send_fc.at[i],
                recv_sem=recv_fc.at[src],
                device_id=(i, c),
                device_id_type=MESH,
            )

        own_fr = pltpu.make_async_copy(out_ref, img_row.at[:, pl.ds(c * vt, vt)], local_sem.at[4])
        own_fc = pltpu.make_async_copy(out_ref, img_col.at[:, pl.ds(r * vt, vt)], local_sem.at[5])
        own_fr.start()
        own_fc.start()

        def start_fr(k, carry):
            fwd_row_copy(lax.rem(c + k, n_col), c).start()
            return carry

        def start_fc(k, carry):
            fwd_col_copy(lax.rem(r + k, n_row), r).start()
            return carry

        lax.fori_loop(1, n_row, start_fc, 0)
        lax.fori_loop(1, n_col, start_fr, 0)

    def wait_small_row(k, carry):
        small_row_copy(lax.rem(r + k, n_row), r).wait_send()
        small_row_copy(r, lax.rem(r + n_row - k, n_row)).wait_recv()
        return carry

    lax.fori_loop(1, n_row, wait_small_row, 0)
    own_mid.wait()
    small_out[...] = jnp.sum(got_small_row[...], axis=0)

    if forward:
        def wait_fr(k, carry):
            fwd_row_copy(lax.rem(c + k, n_col), c).wait_send()
            fwd_row_copy(c, lax.rem(c + n_col - k, n_col)).wait_recv()
            return carry

        def wait_fc(k, carry):
            fwd_col_copy(lax.rem(r + k, n_row), r).wait_send()
            fwd_col_copy(r, lax.rem(r + n_row - k, n_row)).wait_recv()
            return carry

        lax.fori_loop(1, n_col, wait_fr, 0)
        lax.fori_loop(1, n_row, wait_fc, 0)
        own_fr.wait()
        own_fc.wait()


def pack_small(values):
    flat = jnp.concatenate([v.reshape(-1) for v in values])
    tile = 8 * 128
    padded = -(-flat.shape[0] // tile) * tile
    return jnp.pad(flat, (0, padded - flat.shape[0])).reshape(-1, 128)


def unpack_small(total, values):
    total = total.reshape(-1)
    out, start = [], 0
    for v in values:
        out.append(total[start:start + v.size].reshape(v.shape))
        start += v.size
    return out


def reduce_tiles(base_tiles, row_sum, col_sum, small, n_row, n_col, collective_id, forward=False):
    k, vt = base_tiles.shape
    s = small.shape[0]
    vmem = pl.BlockSpec(memory_space=pltpu.VMEM)
    out_shape = [
        jax.ShapeDtypeStruct((k, vt), base_tiles.dtype),
        jax.ShapeDtypeStruct((s, 128), jnp.float32),
    ]
    extra_sems = []
    if forward:
        out_shape += [
            jax.ShapeDtypeStruct((k, n_col * vt), base_tiles.dtype),
            jax.ShapeDtypeStruct((k, n_row * vt), base_tiles.dtype),
        ]
        extra_sems = [
            pltpu.SemaphoreType.DMA((n_col,)),
            pltpu.SemaphoreType.DMA((n_col,)),
            pltpu.SemaphoreType.DMA((n_row,)),
            pltpu.SemaphoreType.DMA((n_row,)),
        ]
    return pl.pallas_call(
        functools.partial(_reduce_kernel, n_row, n_col, forward),
        out_shape=tuple(out_shape),
        in_specs=[vmem, vmem, vmem, vmem],
        out_specs=tuple(vmem for _ in out_shape),
        scratch_shapes=[
            pltpu.VMEM((n_col, k, vt), jnp.float32),
            pltpu.VMEM((n_row, k, vt), jnp.float32),
            pltpu.VMEM((n_col, s, 128), jnp.float32),
            pltpu.VMEM((s, 128), jnp.float32),
            pltpu.VMEM((n_row, s, 128), jnp.float32),
            pltpu.SemaphoreType.DMA((n_col,)),
            pltpu.SemaphoreType.DMA((n_col,)),
            pltpu.SemaphoreType.DMA((n_row,)),
            pltpu.SemaphoreType.DMA((n_row,)),
            pltpu.SemaphoreType.DMA((n_col,)),
            pltpu.SemaphoreType.DMA((n_col,)),
            pltpu.SemaphoreType.DMA((n_row,)),
            pltpu.SemaphoreType.DMA((n_row,)),
            pltpu.SemaphoreType.DMA((6,)),
        ] + extra_sems,
        compiler_params=pltpu.CompilerParams(collective_id=collective_id, has_side_effects=True),
    )(base_tiles, row_sum, col_sum, small)


def _slots_kernel(group, rows_k, tile, rows_ref, cols_ref, count_ref, tiles_ref, rowv_ref, colv_ref,
                  rsum_ref, csum_ref):
    g = pl.program_id(0)

    @pl.when(g == 0)
    def _():
        rsum_ref[...] = jnp.zeros_like(rsum_ref)
        csum_ref[...] = jnp.zeros_like(csum_ref)

    for s in range(group):
        slot = g * group + s

        @pl.when(slot < count_ref[0])
        def _():
            a = pl.multiple_of(rows_ref[slot] * tile, tile)
            b = pl.multiple_of(cols_ref[slot] * tile, tile)
            high, low = split_bf16(tiles_ref[s])
            col_high, col_low = split_bf16(colv_ref[pl.ds(0, rows_k), pl.ds(b, tile)].T)
            both = jnp.dot(
                jnp.concatenate([high, low], axis=0), jnp.concatenate([col_high, col_low], axis=1),
                preferred_element_type=jnp.float32,
            )
            rsum_ref[:, pl.ds(a, tile)] += (
                both[:tile, :rows_k] + (both[:tile, rows_k:] + both[tile:, :rows_k])
            ).T
            csum_ref[:, pl.ds(b, tile)] += dot3(
                split_bf16(rowv_ref[pl.ds(0, rows_k), pl.ds(a, tile)]),
                jnp.concatenate([high, low], axis=1), (((1,), (0,)), ((), ())),
            )


def split_bf16(x):
    high = x.astype(jnp.bfloat16)
    return high, (x - high.astype(jnp.float32)).astype(jnp.bfloat16)


def dot3(left, right, dims):
    rows = left[0].shape[0]
    both = lax.dot_general(
        jnp.concatenate([left[0], left[1]], axis=0), right, dims, preferred_element_type=jnp.float32
    )
    width = both.shape[1] // 2
    return both[:rows, :width] + (both[rows:, :width] + both[:rows, width:])


def slot_products(blocks, rows_here, cols_here, live_count, row_tiles, column_tiles, rows_k):
    slot_count, tile, _ = blocks.shape
    sums_shape = lambda v: (rows_k, v.shape[1])
    group = group_width
    groups = slot_count // group

    def tile_map(g, rows, cols, count):
        last = jnp.maximum(count[0] - 1, 0) // group
        return (jnp.minimum(g, last), 0, 0)

    def whole(g, rows, cols, count):
        return (0, 0)

    grid_spec = pltpu.PrefetchScalarGridSpec(
        num_scalar_prefetch=3,
        grid=(groups,),
        in_specs=[
            pl.BlockSpec((group, tile, tile), tile_map),
            pl.BlockSpec(row_tiles.shape, whole),
            pl.BlockSpec(column_tiles.shape, whole),
        ],
        out_specs=[
            pl.BlockSpec(sums_shape(row_tiles), whole),
            pl.BlockSpec(sums_shape(column_tiles), whole),
        ],
    )
    return pl.pallas_call(
        functools.partial(_slots_kernel, group, rows_k, tile),
        grid_spec=grid_spec,
        out_shape=(
            jax.ShapeDtypeStruct(sums_shape(row_tiles), jnp.float32),
            jax.ShapeDtypeStruct(sums_shape(column_tiles), jnp.float32),
        ),
        compiler_params=pltpu.CompilerParams(dimension_semantics=("arbitrary",)),
    )(rows_here, cols_here, live_count.reshape(1), blocks, row_tiles, column_tiles)


def tile_dot(left, right):
    return jnp.dot(left, right.T, precision=highest)


def dot_rows(left, right):
    return jnp.dot(left, right.T, precision=highest)


def local(n_row, n_col, tile_values, tile_row, tile_col, counts, diagonal, current, previous, previous_image):
    k = current.shape[0]
    tile = tile_values.shape[-1]
    slot_count = tile_values.shape[2]
    blocks = tile_values.reshape(slot_count, tile, tile)
    rows_here = tile_row.reshape(slot_count)
    cols_here = tile_col.reshape(slot_count)
    live_count = counts.reshape(())

    row_cp, col_cp = gather_tiles(jnp.concatenate([current, previous], 0), n_row, n_col, 0)
    row_sum, col_sum = slot_products(blocks, rows_here, cols_here, live_count, row_cp, col_cp, k)
    row_cur, col_cur = row_cp[:k], col_cp[:k]
    scaled = diagonal[None, :] * current
    small_gram = dot_rows(current, current)
    proj_part = dot_rows(current, scaled) + tile_dot(row_cur, row_sum) + tile_dot(col_cur, col_sum)
    image_tiles, small, row_img, col_img = reduce_tiles(
        scaled, row_sum, col_sum, pack_small((small_gram, proj_part)), n_row, n_col, 1,
        forward=True,
    )
    image = image_tiles
    small_gram, small_proj = unpack_small(small, (small_gram, proj_part))

    factor = jnp.linalg.cholesky(small_gram)
    ritz_matrix = jax.scipy.linalg.cho_solve((factor, True), small_proj)
    residual = image - jnp.dot(ritz_matrix.T, current, precision=highest)

    def residual_of(img_tiles, cur_tiles):
        fitted = sum(ritz_matrix[l][:, None] * cur_tiles[l:l + 1, :] for l in range(k))
        return img_tiles - fitted

    row_res = residual_of(row_img, row_cur)
    col_res = residual_of(col_img, col_cur)
    row_sum, col_sum = slot_products(blocks, rows_here, cols_here, live_count, row_res, col_res, k)
    search_basis = jnp.concatenate([current, residual, previous], 0)
    row_basis = jnp.concatenate([row_cur, row_res, row_cp[k:]], 0)
    col_basis = jnp.concatenate([col_cur, col_res, col_cp[k:]], 0)
    scaled = diagonal[None, :] * residual
    correlation = dot_rows(search_basis, search_basis)
    residual_part = (
        dot_rows(search_basis, scaled) + tile_dot(row_basis, row_sum) + tile_dot(col_basis, col_sum)
    )
    mixed_part = jnp.concatenate(
        [dot_rows(search_basis, image), residual_part, dot_rows(search_basis, previous_image)], 1
    )
    image_tiles, small = reduce_tiles(
        scaled, row_sum, col_sum, pack_small((correlation, mixed_part)), n_row, n_col, 2
    )
    residual_image = image_tiles
    correlation, mixed_terms = unpack_small(small, (correlation, mixed_part))
    pencil = 0.5 * (mixed_terms + mixed_terms.T)
    lower_factor = jnp.linalg.cholesky(correlation)
    half_solve = jax.scipy.linalg.solve_triangular(lower_factor, pencil, lower=True)
    reduced = jax.scipy.linalg.solve_triangular(lower_factor, half_solve.T, lower=True)
    return (image, residual, residual_image, reduced)


def solution(mesh):
    n_row = mesh.shape["row"]
    n_col = mesh.shape["col"]
    return jax.shard_map(
        functools.partial(local, n_row, n_col),
        mesh=mesh,
        in_specs=(
            P("row", "col", None, None, None),
            P("row", "col", None),
            P("row", "col", None),
            P("row", "col"),
            P(("row", "col")),
            P(None, ("row", "col")),
            P(None, ("row", "col")),
            P(None, ("row", "col")),
        ),
        out_specs=(P(None, ("row", "col")), P(None, ("row", "col")), P(None, ("row", "col")), P()),
        check_vma=False,
    )
```

```python
import functools

import jax
import jax.numpy as jnp
from jax import lax
from jax.experimental import pallas as pl
from jax.experimental.pallas import tpu as pltpu
from jax.sharding import PartitionSpec as P

highest = lax.Precision.HIGHEST
group_width = 8
MESH = pl.DeviceIdType.MESH


def _barrier(n_row, n_col, r, c):
    barrier = pltpu.get_barrier_semaphore()

    def greet_col(k, carry):
        pl.semaphore_signal(barrier, 1, device_id=(r, lax.rem(c + k, n_col)), device_id_type=MESH)
        return carry

    def greet_row(k, carry):
        pl.semaphore_signal(barrier, 1, device_id=(lax.rem(r + k, n_row), c), device_id_type=MESH)
        return carry

    lax.fori_loop(1, n_col, greet_col, 0)
    lax.fori_loop(1, n_row, greet_row, 0)
    pl.semaphore_wait(barrier, n_row + n_col - 2)


def _gather_kernel(n_row, n_col, x_ref, rowv_ref, colv_ref, send_row, recv_row, send_col, recv_col, local_sem):
    vt = x_ref.shape[1]
    r = lax.axis_index("row")
    c = lax.axis_index("col")
    _barrier(n_row, n_col, r, c)

    def row_copy(j, src):
        return pltpu.make_async_remote_copy(
            src_ref=x_ref,
            dst_ref=rowv_ref.at[:, pl.ds(src * vt, vt)],
            send_sem=send_row.at[j],
            recv_sem=recv_row.at[src],
            device_id=(r, j),
            device_id_type=MESH,
        )

    def col_copy(i, src):
        return pltpu.make_async_remote_copy(
            src_ref=x_ref,
            dst_ref=colv_ref.at[:, pl.ds(src * vt, vt)],
            send_sem=send_col.at[i],
            recv_sem=recv_col.at[src],
            device_id=(i, c),
            device_id_type=MESH,
        )

    own_row = pltpu.make_async_copy(x_ref, rowv_ref.at[:, pl.ds(c * vt, vt)], local_sem.at[0])
    own_col = pltpu.make_async_copy(x_ref, colv_ref.at[:, pl.ds(r * vt, vt)], local_sem.at[1])
    own_row.start()
    own_col.start()

    def start_col(k, carry):
        row_copy(lax.rem(c + k, n_col), c).start()
        return carry

    def start_row(k, carry):
        col_copy(lax.rem(r + k, n_row), r).start()
        return carry

    lax.fori_loop(1, n_col, start_col, 0)
    lax.fori_loop(1, n_row, start_row, 0)

    def wait_col(k, carry):
        row_copy(lax.rem(c + k, n_col), c).wait_send()
        row_copy(c, lax.rem(c + n_col - k, n_col)).wait_recv()
        return carry

    def wait_row(k, carry):
        col_copy(lax.rem(r + k, n_row), r).wait_send()
        col_copy(r, lax.rem(r + n_row - k, n_row)).wait_recv()
        return carry

    lax.fori_loop(1, n_col, wait_col, 0)
    lax.fori_loop(1, n_row, wait_row, 0)
    own_row.wait()
    own_col.wait()


def gather_tiles(x_tiles, n_row, n_col, collective_id):
    k, vt = x_tiles.shape
    vmem = pl.BlockSpec(memory_space=pltpu.VMEM)
    return pl.pallas_call(
        functools.partial(_gather_kernel, n_row, n_col),
        out_shape=(
            jax.ShapeDtypeStruct((k, n_col * vt), x_tiles.dtype),
            jax.ShapeDtypeStruct((k, n_row * vt), x_tiles.dtype),
        ),
        in_specs=[vmem],
        out_specs=(vmem, vmem),
        scratch_shapes=[
            pltpu.SemaphoreType.DMA((n_col,)),
            pltpu.SemaphoreType.DMA((n_col,)),
            pltpu.SemaphoreType.DMA((n_row,)),
            pltpu.SemaphoreType.DMA((n_row,)),
            pltpu.SemaphoreType.DMA((2,)),
        ],
        compiler_params=pltpu.CompilerParams(collective_id=collective_id, has_side_effects=True),
    )(x_tiles)


def _reduce_kernel(n_row, n_col, forward, base_ref, rsum_ref, csum_ref, small_ref, out_ref, small_out, *rest):
    if forward:
        img_row, img_col = rest[:2]
        rest = rest[2:]
    (got_row, got_col, got_small_col, mid, got_small_row,
     send_row, recv_row, send_col, recv_col,
     send_small_col, recv_small_col, send_small_row, recv_small_row, local_sem) = rest[:14]
    vt = base_ref.shape[1]
    r = lax.axis_index("row")
    c = lax.axis_index("col")
    _barrier(n_row, n_col, r, c)

    def small_col_copy(j, src):
        return pltpu.make_async_remote_copy(
            src_ref=small_ref,
            dst_ref=got_small_col.at[src],
            send_sem=send_small_col.at[j],
            recv_sem=recv_small_col.at[src],
            device_id=(r, j),
            device_id_type=MESH,
        )

    def small_row_copy(i, src):
        return pltpu.make_async_remote_copy(
            src_ref=mid,
            dst_ref=got_small_row.at[src],
            send_sem=send_small_row.at[i],
            recv_sem=recv_small_row.at[src],
            device_id=(i, c),
            device_id_type=MESH,
        )

    def row_copy(j, src):
        return pltpu.make_async_remote_copy(
            src_ref=rsum_ref.at[:, pl.ds(j * vt, vt)],
            dst_ref=got_row.at[src],
            send_sem=send_row.at[j],
            recv_sem=recv_row.at[src],
            device_id=(r, j),
            device_id_type=MESH,
        )

    def col_copy(i, src):
        return pltpu.make_async_remote_copy(
            src_ref=csum_ref.at[:, pl.ds(i * vt, vt)],
            dst_ref=got_col.at[src],
            send_sem=send_col.at[i],
            recv_sem=recv_col.at[src],
            device_id=(i, c),
            device_id_type=MESH,
        )

    own_small = pltpu.make_async_copy(small_ref, got_small_col.at[c], local_sem.at[2])
    own_small.start()

    def start_small_col(k, carry):
        small_col_copy(lax.rem(c + k, n_col), c).start()
        return carry

    lax.fori_loop(1, n_col, start_small_col, 0)

    own_row = pltpu.make_async_copy(rsum_ref.at[:, pl.ds(c * vt, vt)], got_row.at[c], local_sem.at[0])
    own_col = pltpu.make_async_copy(csum_ref.at[:, pl.ds(r * vt, vt)], got_col.at[r], local_sem.at[1])
    own_row.start()
    own_col.start()

    def start_col(k, carry):
        row_copy(lax.rem(c + k, n_col), c).start()
        return carry

    def start_row(k, carry):
        col_copy(lax.rem(r + k, n_row), r).start()
        return carry

    lax.fori_loop(1, n_row, start_row, 0)
    lax.fori_loop(1, n_col, start_col, 0)

    def wait_small_col(k, carry):
        small_col_copy(lax.rem(c + k, n_col), c).wait_send()
        small_col_copy(c, lax.rem(c + n_col - k, n_col)).wait_recv()
        return carry

    lax.fori_loop(1, n_col, wait_small_col, 0)
    own_small.wait()
    mid[...] = jnp.sum(got_small_col[...], axis=0)

    own_mid = pltpu.make_async_copy(mid, got_small_row.at[r], local_sem.at[3])
    own_mid.start()

    def start_small_row(k, carry):
        small_row_copy(lax.rem(r + k, n_row), r).start()
        return carry

    lax.fori_loop(1, n_row, start_small_row, 0)

    def wait_col(k, carry):
        row_copy(lax.rem(c + k, n_col), c).wait_send()
        row_copy(c, lax.rem(c + n_col - k, n_col)).wait_recv()
        return carry

    def wait_row(k, carry):
        col_copy(lax.rem(r + k, n_row), r).wait_send()
        col_copy(r, lax.rem(r + n_row - k, n_row)).wait_recv()
        return carry

    lax.fori_loop(1, n_col, wait_col, 0)
    lax.fori_loop(1, n_row, wait_row, 0)
    own_row.wait()
    own_col.wait()
    out_ref[...] = base_ref[...] + jnp.sum(got_row[...], axis=0) + jnp.sum(got_col[...], axis=0)

    if forward:
        send_fr, recv_fr, send_fc, recv_fc = rest[14:]

        def fwd_row_copy(j, src):
            return pltpu.make_async_remote_copy(
                src_ref=out_ref,
                dst_ref=img_row.at[:, pl.ds(src * vt, vt)],
                send_sem=send_fr.at[j],
                recv_sem=recv_fr.at[src],
                device_id=(r, j),
                device_id_type=MESH,
            )

        def fwd_col_copy(i, src):
            return pltpu.make_async_remote_copy(
                src_ref=out_ref,
                dst_ref=img_col.at[:, pl.ds(src * vt, vt)],
                send_sem=send_fc.at[i],
                recv_sem=recv_fc.at[src],
                device_id=(i, c),
                device_id_type=MESH,
            )

        own_fr = pltpu.make_async_copy(out_ref, img_row.at[:, pl.ds(c * vt, vt)], local_sem.at[4])
        own_fc = pltpu.make_async_copy(out_ref, img_col.at[:, pl.ds(r * vt, vt)], local_sem.at[5])
        own_fr.start()
        own_fc.start()

        def start_fr(k, carry):
            fwd_row_copy(lax.rem(c + k, n_col), c).start()
            return carry

        def start_fc(k, carry):
            fwd_col_copy(lax.rem(r + k, n_row), r).start()
            return carry

        lax.fori_loop(1, n_row, start_fc, 0)
        lax.fori_loop(1, n_col, start_fr, 0)

    def wait_small_row(k, carry):
        small_row_copy(lax.rem(r + k, n_row), r).wait_send()
        small_row_copy(r, lax.rem(r + n_row - k, n_row)).wait_recv()
        return carry

    lax.fori_loop(1, n_row, wait_small_row, 0)
    own_mid.wait()
    small_out[...] = jnp.sum(got_small_row[...], axis=0)

    if forward:
        def wait_fr(k, carry):
            fwd_row_copy(lax.rem(c + k, n_col), c).wait_send()
            fwd_row_copy(c, lax.rem(c + n_col - k, n_col)).wait_recv()
            return carry

        def wait_fc(k, carry):
            fwd_col_copy(lax.rem(r + k, n_row), r).wait_send()
            fwd_col_copy(r, lax.rem(r + n_row - k, n_row)).wait_recv()
            return carry

        lax.fori_loop(1, n_col, wait_fr, 0)
        lax.fori_loop(1, n_row, wait_fc, 0)
        own_fr.wait()
        own_fc.wait()


def pack_small(values):
    flat = jnp.concatenate([v.reshape(-1) for v in values])
    tile = 8 * 128
    padded = -(-flat.shape[0] // tile) * tile
    return jnp.pad(flat, (0, padded - flat.shape[0])).reshape(-1, 128)


def unpack_small(total, values):
    total = total.reshape(-1)
    out, start = [], 0
    for v in values:
        out.append(total[start:start + v.size].reshape(v.shape))
        start += v.size
    return out


def reduce_tiles(base_tiles, row_sum, col_sum, small, n_row, n_col, collective_id, forward=False):
    k, vt = base_tiles.shape
    s = small.shape[0]
    vmem = pl.BlockSpec(memory_space=pltpu.VMEM)
    out_shape = [
        jax.ShapeDtypeStruct((k, vt), base_tiles.dtype),
        jax.ShapeDtypeStruct((s, 128), jnp.float32),
    ]
    extra_sems = []
    if forward:
        out_shape += [
            jax.ShapeDtypeStruct((k, n_col * vt), base_tiles.dtype),
            jax.ShapeDtypeStruct((k, n_row * vt), base_tiles.dtype),
        ]
        extra_sems = [
            pltpu.SemaphoreType.DMA((n_col,)),
            pltpu.SemaphoreType.DMA((n_col,)),
            pltpu.SemaphoreType.DMA((n_row,)),
            pltpu.SemaphoreType.DMA((n_row,)),
        ]
    return pl.pallas_call(
        functools.partial(_reduce_kernel, n_row, n_col, forward),
        out_shape=tuple(out_shape),
        in_specs=[vmem, vmem, vmem, vmem],
        out_specs=tuple(vmem for _ in out_shape),
        scratch_shapes=[
            pltpu.VMEM((n_col, k, vt), jnp.float32),
            pltpu.VMEM((n_row, k, vt), jnp.float32),
            pltpu.VMEM((n_col, s, 128), jnp.float32),
            pltpu.VMEM((s, 128), jnp.float32),
            pltpu.VMEM((n_row, s, 128), jnp.float32),
            pltpu.SemaphoreType.DMA((n_col,)),
            pltpu.SemaphoreType.DMA((n_col,)),
            pltpu.SemaphoreType.DMA((n_row,)),
            pltpu.SemaphoreType.DMA((n_row,)),
            pltpu.SemaphoreType.DMA((n_col,)),
            pltpu.SemaphoreType.DMA((n_col,)),
            pltpu.SemaphoreType.DMA((n_row,)),
            pltpu.SemaphoreType.DMA((n_row,)),
            pltpu.SemaphoreType.DMA((6,)),
        ] + extra_sems,
        compiler_params=pltpu.CompilerParams(collective_id=collective_id, has_side_effects=True),
    )(base_tiles, row_sum, col_sum, small)


def _slots_kernel(group, rows_k, tile, rows_ref, cols_ref, count_ref, tiles_ref, rowv_ref, colv_ref,
                  rsum_ref, csum_ref):
    g = pl.program_id(0)

    @pl.when(g == 0)
    def _():
        rsum_ref[...] = jnp.zeros_like(rsum_ref)
        csum_ref[...] = jnp.zeros_like(csum_ref)

    for s in range(group):
        slot = g * group + s

        @pl.when(slot < count_ref[0])
        def _():
            a = pl.multiple_of(rows_ref[slot] * tile, tile)
            b = pl.multiple_of(cols_ref[slot] * tile, tile)
            high, low = split_bf16(tiles_ref[s])
            rsum_ref[:, pl.ds(a, tile)] += dot3(
                split_bf16(colv_ref[pl.ds(0, rows_k), pl.ds(b, tile)]),
                jnp.concatenate([high, low], axis=0), (((1,), (1,)), ((), ())),
            )
            csum_ref[:, pl.ds(b, tile)] += dot3(
                split_bf16(rowv_ref[pl.ds(0, rows_k), pl.ds(a, tile)]),
                jnp.concatenate([high, low], axis=1), (((1,), (0,)), ((), ())),
            )


def split_bf16(x):
    high = x.astype(jnp.bfloat16)
    return high, (x - high.astype(jnp.float32)).astype(jnp.bfloat16)


def dot3(left, right, dims):
    rows = left[0].shape[0]
    both = lax.dot_general(
        jnp.concatenate([left[0], left[1]], axis=0), right, dims, preferred_element_type=jnp.float32
    )
    width = both.shape[1] // 2
    return both[:rows, :width] + (both[rows:, :width] + both[:rows, width:])


def slot_products(blocks, rows_here, cols_here, live_count, row_tiles, column_tiles, rows_k):
    slot_count, tile, _ = blocks.shape
    sums_shape = lambda v: (rows_k, v.shape[1])
    group = group_width
    groups = slot_count // group

    def tile_map(g, rows, cols, count):
        last = jnp.maximum(count[0] - 1, 0) // group
        return (jnp.minimum(g, last), 0, 0)

    def whole(g, rows, cols, count):
        return (0, 0)

    grid_spec = pltpu.PrefetchScalarGridSpec(
        num_scalar_prefetch=3,
        grid=(groups,),
        in_specs=[
            pl.BlockSpec((group, tile, tile), tile_map),
            pl.BlockSpec(row_tiles.shape, whole),
            pl.BlockSpec(column_tiles.shape, whole),
        ],
        out_specs=[
            pl.BlockSpec(sums_shape(row_tiles), whole),
            pl.BlockSpec(sums_shape(column_tiles), whole),
        ],
    )
    return pl.pallas_call(
        functools.partial(_slots_kernel, group, rows_k, tile),
        grid_spec=grid_spec,
        out_shape=(
            jax.ShapeDtypeStruct(sums_shape(row_tiles), jnp.float32),
            jax.ShapeDtypeStruct(sums_shape(column_tiles), jnp.float32),
        ),
        compiler_params=pltpu.CompilerParams(dimension_semantics=("arbitrary",)),
    )(rows_here, cols_here, live_count.reshape(1), blocks, row_tiles, column_tiles)


def tile_dot(left, right):
    return jnp.dot(left, right.T, precision=highest)


def lower_solve(factor, rhs, transpose_a=False):
    return lax.linalg.triangular_solve(factor, rhs, left_side=True, lower=True, transpose_a=transpose_a)


def dot_rows(left, right):
    return jnp.dot(left, right.T, precision=highest)


def local(n_row, n_col, tile_values, tile_row, tile_col, counts, diagonal, current, previous, previous_image):
    k = current.shape[0]
    tile = tile_values.shape[-1]
    slot_count = tile_values.shape[2]
    blocks = tile_values.reshape(slot_count, tile, tile)
    rows_here = tile_row.reshape(slot_count)
    cols_here = tile_col.reshape(slot_count)
    live_count = counts.reshape(())

    row_cp, col_cp = gather_tiles(jnp.concatenate([current, previous], 0), n_row, n_col, 0)
    row_sum, col_sum = slot_products(blocks, rows_here, cols_here, live_count, row_cp, col_cp, k)
    row_cur, col_cur = row_cp[:k], col_cp[:k]
    scaled = diagonal[None, :] * current
    small_gram = dot_rows(current, current)
    proj_part = dot_rows(current, scaled) + tile_dot(row_cur, row_sum) + tile_dot(col_cur, col_sum)
    image_tiles, small, row_img, col_img = reduce_tiles(
        scaled, row_sum, col_sum, pack_small((small_gram, proj_part)), n_row, n_col, 1,
        forward=True,
    )
    image = image_tiles
    small_gram, small_proj = unpack_small(small, (small_gram, proj_part))

    factor = lax.linalg.cholesky(small_gram, symmetrize_input=False)
    ritz_matrix = lower_solve(factor, lower_solve(factor, small_proj), transpose_a=True)
    residual = image - jnp.dot(ritz_matrix.T, current, precision=highest)

    def residual_of(img_tiles, cur_tiles):
        fitted = sum(ritz_matrix[l][:, None] * cur_tiles[l:l + 1, :] for l in range(k))
        return img_tiles - fitted

    row_res = residual_of(row_img, row_cur)
    col_res = residual_of(col_img, col_cur)
    row_sum, col_sum = slot_products(blocks, rows_here, cols_here, live_count, row_res, col_res, k)
    search_basis = jnp.concatenate([current, residual, previous], 0)
    row_basis = jnp.concatenate([row_cur, row_res, row_cp[k:]], 0)
    col_basis = jnp.concatenate([col_cur, col_res, col_cp[k:]], 0)
    scaled = diagonal[None, :] * residual
    correlation = dot_rows(search_basis, search_basis)
    residual_part = (
        dot_rows(search_basis, scaled) + tile_dot(row_basis, row_sum) + tile_dot(col_basis, col_sum)
    )
    mixed_part = jnp.concatenate(
        [dot_rows(search_basis, image), residual_part, dot_rows(search_basis, previous_image)], 1
    )
    image_tiles, small = reduce_tiles(
        scaled, row_sum, col_sum, pack_small((correlation, mixed_part)), n_row, n_col, 2
    )
    residual_image = image_tiles
    correlation, mixed_terms = unpack_small(small, (correlation, mixed_part))
    pencil = 0.5 * (mixed_terms + mixed_terms.T)
    lower_factor = lax.linalg.cholesky(correlation, symmetrize_input=False)
    half_solve = lower_solve(lower_factor, pencil)
    reduced = lower_solve(lower_factor, half_solve.T)
    return (image, residual, residual_image, reduced)


def solution(mesh):
    n_row = mesh.shape["row"]
    n_col = mesh.shape["col"]
    return jax.shard_map(
        functools.partial(local, n_row, n_col),
        mesh=mesh,
        in_specs=(
            P("row", "col", None, None, None),
            P("row", "col", None),
            P("row", "col", None),
            P("row", "col"),
            P(("row", "col")),
            P(None, ("row", "col")),
            P(None, ("row", "col")),
            P(None, ("row", "col")),
        ),
        out_specs=(P(None, ("row", "col")), P(None, ("row", "col")), P(None, ("row", "col")), P()),
        check_vma=False,
    )
```

```python
import functools

import jax
import jax.numpy as jnp
from jax import lax
from jax.experimental import pallas as pl
from jax.experimental.pallas import tpu as pltpu
from jax.sharding import PartitionSpec as P

highest = lax.Precision.HIGHEST
group_width = 16
MESH = pl.DeviceIdType.MESH


def _barrier(n_row, n_col, r, c):
    barrier = pltpu.get_barrier_semaphore()

    def greet_col(k, carry):
        pl.semaphore_signal(barrier, 1, device_id=(r, lax.rem(c + k, n_col)), device_id_type=MESH)
        return carry

    def greet_row(k, carry):
        pl.semaphore_signal(barrier, 1, device_id=(lax.rem(r + k, n_row), c), device_id_type=MESH)
        return carry

    lax.fori_loop(1, n_col, greet_col, 0)
    lax.fori_loop(1, n_row, greet_row, 0)
    pl.semaphore_wait(barrier, n_row + n_col - 2)


def _gather_kernel(n_row, n_col, x_ref, rowv_ref, colv_ref, send_row, recv_row, send_col, recv_col, local_sem):
    vt = x_ref.shape[1]
    r = lax.axis_index("row")
    c = lax.axis_index("col")
    _barrier(n_row, n_col, r, c)

    def row_copy(j, src):
        return pltpu.make_async_remote_copy(
            src_ref=x_ref,
            dst_ref=rowv_ref.at[:, pl.ds(src * vt, vt)],
            send_sem=send_row.at[j],
            recv_sem=recv_row.at[src],
            device_id=(r, j),
            device_id_type=MESH,
        )

    def col_copy(i, src):
        return pltpu.make_async_remote_copy(
            src_ref=x_ref,
            dst_ref=colv_ref.at[:, pl.ds(src * vt, vt)],
            send_sem=send_col.at[i],
            recv_sem=recv_col.at[src],
            device_id=(i, c),
            device_id_type=MESH,
        )

    own_row = pltpu.make_async_copy(x_ref, rowv_ref.at[:, pl.ds(c * vt, vt)], local_sem.at[0])
    own_col = pltpu.make_async_copy(x_ref, colv_ref.at[:, pl.ds(r * vt, vt)], local_sem.at[1])
    own_row.start()
    own_col.start()

    def start_col(k, carry):
        row_copy(lax.rem(c + k, n_col), c).start()
        return carry

    def start_row(k, carry):
        col_copy(lax.rem(r + k, n_row), r).start()
        return carry

    lax.fori_loop(1, n_col, start_col, 0)
    lax.fori_loop(1, n_row, start_row, 0)

    def wait_col(k, carry):
        row_copy(lax.rem(c + k, n_col), c).wait_send()
        row_copy(c, lax.rem(c + n_col - k, n_col)).wait_recv()
        return carry

    def wait_row(k, carry):
        col_copy(lax.rem(r + k, n_row), r).wait_send()
        col_copy(r, lax.rem(r + n_row - k, n_row)).wait_recv()
        return carry

    lax.fori_loop(1, n_col, wait_col, 0)
    lax.fori_loop(1, n_row, wait_row, 0)
    own_row.wait()
    own_col.wait()


def gather_tiles(x_tiles, n_row, n_col, collective_id):
    k, vt = x_tiles.shape
    vmem = pl.BlockSpec(memory_space=pltpu.VMEM)
    return pl.pallas_call(
        functools.partial(_gather_kernel, n_row, n_col),
        out_shape=(
            jax.ShapeDtypeStruct((k, n_col * vt), x_tiles.dtype),
            jax.ShapeDtypeStruct((k, n_row * vt), x_tiles.dtype),
        ),
        in_specs=[vmem],
        out_specs=(vmem, vmem),
        scratch_shapes=[
            pltpu.SemaphoreType.DMA((n_col,)),
            pltpu.SemaphoreType.DMA((n_col,)),
            pltpu.SemaphoreType.DMA((n_row,)),
            pltpu.SemaphoreType.DMA((n_row,)),
            pltpu.SemaphoreType.DMA((2,)),
        ],
        compiler_params=pltpu.CompilerParams(collective_id=collective_id, has_side_effects=True),
    )(x_tiles)


def _reduce_kernel(n_row, n_col, forward, base_ref, rsum_ref, csum_ref, small_ref, out_ref, small_out, *rest):
    if forward:
        img_row, img_col = rest[:2]
        rest = rest[2:]
    (got_row, got_col, got_small_col, mid, got_small_row,
     send_row, recv_row, send_col, recv_col,
     send_small_col, recv_small_col, send_small_row, recv_small_row, local_sem) = rest[:14]
    vt = base_ref.shape[1]
    r = lax.axis_index("row")
    c = lax.axis_index("col")
    _barrier(n_row, n_col, r, c)

    def small_col_copy(j, src):
        return pltpu.make_async_remote_copy(
            src_ref=small_ref,
            dst_ref=got_small_col.at[src],
            send_sem=send_small_col.at[j],
            recv_sem=recv_small_col.at[src],
            device_id=(r, j),
            device_id_type=MESH,
        )

    def small_row_copy(i, src):
        return pltpu.make_async_remote_copy(
            src_ref=mid,
            dst_ref=got_small_row.at[src],
            send_sem=send_small_row.at[i],
            recv_sem=recv_small_row.at[src],
            device_id=(i, c),
            device_id_type=MESH,
        )

    def row_copy(j, src):
        return pltpu.make_async_remote_copy(
            src_ref=rsum_ref.at[:, pl.ds(j * vt, vt)],
            dst_ref=got_row.at[src],
            send_sem=send_row.at[j],
            recv_sem=recv_row.at[src],
            device_id=(r, j),
            device_id_type=MESH,
        )

    def col_copy(i, src):
        return pltpu.make_async_remote_copy(
            src_ref=csum_ref.at[:, pl.ds(i * vt, vt)],
            dst_ref=got_col.at[src],
            send_sem=send_col.at[i],
            recv_sem=recv_col.at[src],
            device_id=(i, c),
            device_id_type=MESH,
        )

    own_small = pltpu.make_async_copy(small_ref, got_small_col.at[c], local_sem.at[2])
    own_small.start()

    def start_small_col(k, carry):
        small_col_copy(lax.rem(c + k, n_col), c).start()
        return carry

    lax.fori_loop(1, n_col, start_small_col, 0)

    own_row = pltpu.make_async_copy(rsum_ref.at[:, pl.ds(c * vt, vt)], got_row.at[c], local_sem.at[0])
    own_col = pltpu.make_async_copy(csum_ref.at[:, pl.ds(r * vt, vt)], got_col.at[r], local_sem.at[1])
    own_row.start()
    own_col.start()

    def start_col(k, carry):
        row_copy(lax.rem(c + k, n_col), c).start()
        return carry

    def start_row(k, carry):
        col_copy(lax.rem(r + k, n_row), r).start()
        return carry

    lax.fori_loop(1, n_row, start_row, 0)
    lax.fori_loop(1, n_col, start_col, 0)

    def wait_small_col(k, carry):
        small_col_copy(lax.rem(c + k, n_col), c).wait_send()
        small_col_copy(c, lax.rem(c + n_col - k, n_col)).wait_recv()
        return carry

    lax.fori_loop(1, n_col, wait_small_col, 0)
    own_small.wait()
    mid[...] = jnp.sum(got_small_col[...], axis=0)

    own_mid = pltpu.make_async_copy(mid, got_small_row.at[r], local_sem.at[3])
    own_mid.start()

    def start_small_row(k, carry):
        small_row_copy(lax.rem(r + k, n_row), r).start()
        return carry

    lax.fori_loop(1, n_row, start_small_row, 0)

    def wait_col(k, carry):
        row_copy(lax.rem(c + k, n_col), c).wait_send()
        row_copy(c, lax.rem(c + n_col - k, n_col)).wait_recv()
        return carry

    def wait_row(k, carry):
        col_copy(lax.rem(r + k, n_row), r).wait_send()
        col_copy(r, lax.rem(r + n_row - k, n_row)).wait_recv()
        return carry

    lax.fori_loop(1, n_col, wait_col, 0)
    lax.fori_loop(1, n_row, wait_row, 0)
    own_row.wait()
    own_col.wait()
    out_ref[...] = base_ref[...] + jnp.sum(got_row[...], axis=0) + jnp.sum(got_col[...], axis=0)

    if forward:
        send_fr, recv_fr, send_fc, recv_fc = rest[14:]

        def fwd_row_copy(j, src):
            return pltpu.make_async_remote_copy(
                src_ref=out_ref,
                dst_ref=img_row.at[:, pl.ds(src * vt, vt)],
                send_sem=send_fr.at[j],
                recv_sem=recv_fr.at[src],
                device_id=(r, j),
                device_id_type=MESH,
            )

        def fwd_col_copy(i, src):
            return pltpu.make_async_remote_copy(
                src_ref=out_ref,
                dst_ref=img_col.at[:, pl.ds(src * vt, vt)],
                send_sem=send_fc.at[i],
                recv_sem=recv_fc.at[src],
                device_id=(i, c),
                device_id_type=MESH,
            )

        own_fr = pltpu.make_async_copy(out_ref, img_row.at[:, pl.ds(c * vt, vt)], local_sem.at[4])
        own_fc = pltpu.make_async_copy(out_ref, img_col.at[:, pl.ds(r * vt, vt)], local_sem.at[5])
        own_fr.start()
        own_fc.start()

        def start_fr(k, carry):
            fwd_row_copy(lax.rem(c + k, n_col), c).start()
            return carry

        def start_fc(k, carry):
            fwd_col_copy(lax.rem(r + k, n_row), r).start()
            return carry

        lax.fori_loop(1, n_row, start_fc, 0)
        lax.fori_loop(1, n_col, start_fr, 0)

    def wait_small_row(k, carry):
        small_row_copy(lax.rem(r + k, n_row), r).wait_send()
        small_row_copy(r, lax.rem(r + n_row - k, n_row)).wait_recv()
        return carry

    lax.fori_loop(1, n_row, wait_small_row, 0)
    own_mid.wait()
    small_out[...] = jnp.sum(got_small_row[...], axis=0)

    if forward:
        def wait_fr(k, carry):
            fwd_row_copy(lax.rem(c + k, n_col), c).wait_send()
            fwd_row_copy(c, lax.rem(c + n_col - k, n_col)).wait_recv()
            return carry

        def wait_fc(k, carry):
            fwd_col_copy(lax.rem(r + k, n_row), r).wait_send()
            fwd_col_copy(r, lax.rem(r + n_row - k, n_row)).wait_recv()
            return carry

        lax.fori_loop(1, n_col, wait_fr, 0)
        lax.fori_loop(1, n_row, wait_fc, 0)
        own_fr.wait()
        own_fc.wait()


def pack_small(values):
    flat = jnp.concatenate([v.reshape(-1) for v in values])
    tile = 8 * 128
    padded = -(-flat.shape[0] // tile) * tile
    return jnp.pad(flat, (0, padded - flat.shape[0])).reshape(-1, 128)


def unpack_small(total, values):
    total = total.reshape(-1)
    out, start = [], 0
    for v in values:
        out.append(total[start:start + v.size].reshape(v.shape))
        start += v.size
    return out


def reduce_tiles(base_tiles, row_sum, col_sum, small, n_row, n_col, collective_id, forward=False):
    k, vt = base_tiles.shape
    s = small.shape[0]
    vmem = pl.BlockSpec(memory_space=pltpu.VMEM)
    out_shape = [
        jax.ShapeDtypeStruct((k, vt), base_tiles.dtype),
        jax.ShapeDtypeStruct((s, 128), jnp.float32),
    ]
    extra_sems = []
    if forward:
        out_shape += [
            jax.ShapeDtypeStruct((k, n_col * vt), base_tiles.dtype),
            jax.ShapeDtypeStruct((k, n_row * vt), base_tiles.dtype),
        ]
        extra_sems = [
            pltpu.SemaphoreType.DMA((n_col,)),
            pltpu.SemaphoreType.DMA((n_col,)),
            pltpu.SemaphoreType.DMA((n_row,)),
            pltpu.SemaphoreType.DMA((n_row,)),
        ]
    return pl.pallas_call(
        functools.partial(_reduce_kernel, n_row, n_col, forward),
        out_shape=tuple(out_shape),
        in_specs=[vmem, vmem, vmem, vmem],
        out_specs=tuple(vmem for _ in out_shape),
        scratch_shapes=[
            pltpu.VMEM((n_col, k, vt), jnp.float32),
            pltpu.VMEM((n_row, k, vt), jnp.float32),
            pltpu.VMEM((n_col, s, 128), jnp.float32),
            pltpu.VMEM((s, 128), jnp.float32),
            pltpu.VMEM((n_row, s, 128), jnp.float32),
            pltpu.SemaphoreType.DMA((n_col,)),
            pltpu.SemaphoreType.DMA((n_col,)),
            pltpu.SemaphoreType.DMA((n_row,)),
            pltpu.SemaphoreType.DMA((n_row,)),
            pltpu.SemaphoreType.DMA((n_col,)),
            pltpu.SemaphoreType.DMA((n_col,)),
            pltpu.SemaphoreType.DMA((n_row,)),
            pltpu.SemaphoreType.DMA((n_row,)),
            pltpu.SemaphoreType.DMA((6,)),
        ] + extra_sems,
        compiler_params=pltpu.CompilerParams(collective_id=collective_id, has_side_effects=True),
    )(base_tiles, row_sum, col_sum, small)


def _slots_kernel(group, rows_k, tile, rows_ref, cols_ref, count_ref, tiles_ref, rowv_ref, colv_ref,
                  rsum_ref, csum_ref):
    g = pl.program_id(0)

    @pl.when(g == 0)
    def _():
        rsum_ref[...] = jnp.zeros_like(rsum_ref)
        csum_ref[...] = jnp.zeros_like(csum_ref)

    for s in range(group):
        slot = g * group + s

        @pl.when(slot < count_ref[0])
        def _():
            a = pl.multiple_of(rows_ref[slot] * tile, tile)
            b = pl.multiple_of(cols_ref[slot] * tile, tile)
            high, low = split_bf16(tiles_ref[s])
            rsum_ref[:, pl.ds(a, tile)] += dot3(
                split_bf16(colv_ref[pl.ds(0, rows_k), pl.ds(b, tile)]),
                jnp.concatenate([high, low], axis=0), (((1,), (1,)), ((), ())),
            )
            csum_ref[:, pl.ds(b, tile)] += dot3(
                split_bf16(rowv_ref[pl.ds(0, rows_k), pl.ds(a, tile)]),
                jnp.concatenate([high, low], axis=1), (((1,), (0,)), ((), ())),
            )


def split_bf16(x):
    high = x.astype(jnp.bfloat16)
    return high, (x - high.astype(jnp.float32)).astype(jnp.bfloat16)


def dot3(left, right, dims):
    rows = left[0].shape[0]
    both = lax.dot_general(
        jnp.concatenate([left[0], left[1]], axis=0), right, dims, preferred_element_type=jnp.float32
    )
    width = both.shape[1] // 2
    return both[:rows, :width] + (both[rows:, :width] + both[:rows, width:])


def slot_products(blocks, rows_here, cols_here, live_count, row_tiles, column_tiles, rows_k):
    slot_count, tile, _ = blocks.shape
    sums_shape = lambda v: (rows_k, v.shape[1])
    group = group_width
    groups = slot_count // group

    def tile_map(g, rows, cols, count):
        last = jnp.maximum(count[0] - 1, 0) // group
        return (jnp.minimum(g, last), 0, 0)

    def whole(g, rows, cols, count):
        return (0, 0)

    grid_spec = pltpu.PrefetchScalarGridSpec(
        num_scalar_prefetch=3,
        grid=(groups,),
        in_specs=[
            pl.BlockSpec((group, tile, tile), tile_map),
            pl.BlockSpec(row_tiles.shape, whole),
            pl.BlockSpec(column_tiles.shape, whole),
        ],
        out_specs=[
            pl.BlockSpec(sums_shape(row_tiles), whole),
            pl.BlockSpec(sums_shape(column_tiles), whole),
        ],
    )
    return pl.pallas_call(
        functools.partial(_slots_kernel, group, rows_k, tile),
        grid_spec=grid_spec,
        out_shape=(
            jax.ShapeDtypeStruct(sums_shape(row_tiles), jnp.float32),
            jax.ShapeDtypeStruct(sums_shape(column_tiles), jnp.float32),
        ),
        compiler_params=pltpu.CompilerParams(dimension_semantics=("arbitrary",)),
    )(rows_here, cols_here, live_count.reshape(1), blocks, row_tiles, column_tiles)


def tile_dot(left, right):
    return jnp.dot(left, right.T, precision=highest)


def lower_solve(factor, rhs, transpose_a=False):
    return lax.linalg.triangular_solve(factor, rhs, left_side=True, lower=True, transpose_a=transpose_a)


def dot_rows(left, right):
    return jnp.dot(left, right.T, precision=highest)


def local(n_row, n_col, tile_values, tile_row, tile_col, counts, diagonal, current, previous, previous_image):
    k = current.shape[0]
    tile = tile_values.shape[-1]
    slot_count = tile_values.shape[2]
    blocks = tile_values.reshape(slot_count, tile, tile)
    rows_here = tile_row.reshape(slot_count)
    cols_here = tile_col.reshape(slot_count)
    live_count = counts.reshape(())

    row_cp, col_cp = gather_tiles(jnp.concatenate([current, previous], 0), n_row, n_col, 0)
    row_sum, col_sum = slot_products(blocks, rows_here, cols_here, live_count, row_cp, col_cp, k)
    row_cur, col_cur = row_cp[:k], col_cp[:k]
    scaled = diagonal[None, :] * current
    small_gram = dot_rows(current, current)
    proj_part = dot_rows(current, scaled) + tile_dot(row_cur, row_sum) + tile_dot(col_cur, col_sum)
    image_tiles, small, row_img, col_img = reduce_tiles(
        scaled, row_sum, col_sum, pack_small((small_gram, proj_part)), n_row, n_col, 1,
        forward=True,
    )
    image = image_tiles
    small_gram, small_proj = unpack_small(small, (small_gram, proj_part))

    factor = lax.linalg.cholesky(small_gram, symmetrize_input=False)
    ritz_matrix = lower_solve(factor, lower_solve(factor, small_proj), transpose_a=True)
    residual = image - jnp.dot(ritz_matrix.T, current, precision=highest)

    def residual_of(img_tiles, cur_tiles):
        fitted = sum(ritz_matrix[l][:, None] * cur_tiles[l:l + 1, :] for l in range(k))
        return img_tiles - fitted

    row_res = residual_of(row_img, row_cur)
    col_res = residual_of(col_img, col_cur)
    row_sum, col_sum = slot_products(blocks, rows_here, cols_here, live_count, row_res, col_res, k)
    search_basis = jnp.concatenate([current, residual, previous], 0)
    row_basis = jnp.concatenate([row_cur, row_res, row_cp[k:]], 0)
    col_basis = jnp.concatenate([col_cur, col_res, col_cp[k:]], 0)
    scaled = diagonal[None, :] * residual
    correlation = dot_rows(search_basis, search_basis)
    residual_part = (
        dot_rows(search_basis, scaled) + tile_dot(row_basis, row_sum) + tile_dot(col_basis, col_sum)
    )
    mixed_part = jnp.concatenate(
        [dot_rows(search_basis, image), residual_part, dot_rows(search_basis, previous_image)], 1
    )
    image_tiles, small = reduce_tiles(
        scaled, row_sum, col_sum, pack_small((correlation, mixed_part)), n_row, n_col, 2
    )
    residual_image = image_tiles
    correlation, mixed_terms = unpack_small(small, (correlation, mixed_part))
    pencil = 0.5 * (mixed_terms + mixed_terms.T)
    lower_factor = lax.linalg.cholesky(correlation, symmetrize_input=False)
    half_solve = lower_solve(lower_factor, pencil)
    reduced = lower_solve(lower_factor, half_solve.T)
    return (image, residual, residual_image, reduced)


def solution(mesh):
    n_row = mesh.shape["row"]
    n_col = mesh.shape["col"]
    return jax.shard_map(
        functools.partial(local, n_row, n_col),
        mesh=mesh,
        in_specs=(
            P("row", "col", None, None, None),
            P("row", "col", None),
            P("row", "col", None),
            P("row", "col"),
            P(("row", "col")),
            P(None, ("row", "col")),
            P(None, ("row", "col")),
            P(None, ("row", "col")),
        ),
        out_specs=(P(None, ("row", "col")), P(None, ("row", "col")), P(None, ("row", "col")), P()),
        check_vma=False,
    )
```

```python
import functools

import jax
import jax.numpy as jnp
from jax import lax
from jax.experimental import pallas as pl
from jax.experimental.pallas import tpu as pltpu
from jax.sharding import PartitionSpec as P

highest = lax.Precision.HIGHEST
group_width = 4
MESH = pl.DeviceIdType.MESH


def _barrier(n_row, n_col, r, c):
    barrier = pltpu.get_barrier_semaphore()

    def greet_col(k, carry):
        pl.semaphore_signal(barrier, 1, device_id=(r, lax.rem(c + k, n_col)), device_id_type=MESH)
        return carry

    def greet_row(k, carry):
        pl.semaphore_signal(barrier, 1, device_id=(lax.rem(r + k, n_row), c), device_id_type=MESH)
        return carry

    lax.fori_loop(1, n_col, greet_col, 0)
    lax.fori_loop(1, n_row, greet_row, 0)
    pl.semaphore_wait(barrier, n_row + n_col - 2)


def _gather_kernel(n_row, n_col, x_ref, rowv_ref, colv_ref, send_row, recv_row, send_col, recv_col, local_sem):
    vt = x_ref.shape[1]
    r = lax.axis_index("row")
    c = lax.axis_index("col")
    _barrier(n_row, n_col, r, c)

    def row_copy(j, src):
        return pltpu.make_async_remote_copy(
            src_ref=x_ref,
            dst_ref=rowv_ref.at[:, pl.ds(src * vt, vt)],
            send_sem=send_row.at[j],
            recv_sem=recv_row.at[src],
            device_id=(r, j),
            device_id_type=MESH,
        )

    def col_copy(i, src):
        return pltpu.make_async_remote_copy(
            src_ref=x_ref,
            dst_ref=colv_ref.at[:, pl.ds(src * vt, vt)],
            send_sem=send_col.at[i],
            recv_sem=recv_col.at[src],
            device_id=(i, c),
            device_id_type=MESH,
        )

    own_row = pltpu.make_async_copy(x_ref, rowv_ref.at[:, pl.ds(c * vt, vt)], local_sem.at[0])
    own_col = pltpu.make_async_copy(x_ref, colv_ref.at[:, pl.ds(r * vt, vt)], local_sem.at[1])
    own_row.start()
    own_col.start()

    def start_col(k, carry):
        row_copy(lax.rem(c + k, n_col), c).start()
        return carry

    def start_row(k, carry):
        col_copy(lax.rem(r + k, n_row), r).start()
        return carry

    lax.fori_loop(1, n_col, start_col, 0)
    lax.fori_loop(1, n_row, start_row, 0)

    def wait_col(k, carry):
        row_copy(lax.rem(c + k, n_col), c).wait_send()
        row_copy(c, lax.rem(c + n_col - k, n_col)).wait_recv()
        return carry

    def wait_row(k, carry):
        col_copy(lax.rem(r + k, n_row), r).wait_send()
        col_copy(r, lax.rem(r + n_row - k, n_row)).wait_recv()
        return carry

    lax.fori_loop(1, n_col, wait_col, 0)
    lax.fori_loop(1, n_row, wait_row, 0)
    own_row.wait()
    own_col.wait()


def gather_tiles(x_tiles, n_row, n_col, collective_id):
    k, vt = x_tiles.shape
    vmem = pl.BlockSpec(memory_space=pltpu.VMEM)
    return pl.pallas_call(
        functools.partial(_gather_kernel, n_row, n_col),
        out_shape=(
            jax.ShapeDtypeStruct((k, n_col * vt), x_tiles.dtype),
            jax.ShapeDtypeStruct((k, n_row * vt), x_tiles.dtype),
        ),
        in_specs=[vmem],
        out_specs=(vmem, vmem),
        scratch_shapes=[
            pltpu.SemaphoreType.DMA((n_col,)),
            pltpu.SemaphoreType.DMA((n_col,)),
            pltpu.SemaphoreType.DMA((n_row,)),
            pltpu.SemaphoreType.DMA((n_row,)),
            pltpu.SemaphoreType.DMA((2,)),
        ],
        compiler_params=pltpu.CompilerParams(collective_id=collective_id, has_side_effects=True),
    )(x_tiles)


def _reduce_kernel(n_row, n_col, forward, base_ref, rsum_ref, csum_ref, small_ref, out_ref, small_out, *rest):
    if forward:
        img_row, img_col = rest[:2]
        rest = rest[2:]
    (got_row, got_col, got_small_col, mid, got_small_row,
     send_row, recv_row, send_col, recv_col,
     send_small_col, recv_small_col, send_small_row, recv_small_row, local_sem) = rest[:14]
    vt = base_ref.shape[1]
    r = lax.axis_index("row")
    c = lax.axis_index("col")
    _barrier(n_row, n_col, r, c)

    def small_col_copy(j, src):
        return pltpu.make_async_remote_copy(
            src_ref=small_ref,
            dst_ref=got_small_col.at[src],
            send_sem=send_small_col.at[j],
            recv_sem=recv_small_col.at[src],
            device_id=(r, j),
            device_id_type=MESH,
        )

    def small_row_copy(i, src):
        return pltpu.make_async_remote_copy(
            src_ref=mid,
            dst_ref=got_small_row.at[src],
            send_sem=send_small_row.at[i],
            recv_sem=recv_small_row.at[src],
            device_id=(i, c),
            device_id_type=MESH,
        )

    def row_copy(j, src):
        return pltpu.make_async_remote_copy(
            src_ref=rsum_ref.at[:, pl.ds(j * vt, vt)],
            dst_ref=got_row.at[src],
            send_sem=send_row.at[j],
            recv_sem=recv_row.at[src],
            device_id=(r, j),
            device_id_type=MESH,
        )

    def col_copy(i, src):
        return pltpu.make_async_remote_copy(
            src_ref=csum_ref.at[:, pl.ds(i * vt, vt)],
            dst_ref=got_col.at[src],
            send_sem=send_col.at[i],
            recv_sem=recv_col.at[src],
            device_id=(i, c),
            device_id_type=MESH,
        )

    own_small = pltpu.make_async_copy(small_ref, got_small_col.at[c], local_sem.at[2])
    own_small.start()

    def start_small_col(k, carry):
        small_col_copy(lax.rem(c + k, n_col), c).start()
        return carry

    lax.fori_loop(1, n_col, start_small_col, 0)

    own_row = pltpu.make_async_copy(rsum_ref.at[:, pl.ds(c * vt, vt)], got_row.at[c], local_sem.at[0])
    own_col = pltpu.make_async_copy(csum_ref.at[:, pl.ds(r * vt, vt)], got_col.at[r], local_sem.at[1])
    own_row.start()
    own_col.start()

    def start_col(k, carry):
        row_copy(lax.rem(c + k, n_col), c).start()
        return carry

    def start_row(k, carry):
        col_copy(lax.rem(r + k, n_row), r).start()
        return carry

    lax.fori_loop(1, n_row, start_row, 0)
    lax.fori_loop(1, n_col, start_col, 0)

    def wait_small_col(k, carry):
        small_col_copy(lax.rem(c + k, n_col), c).wait_send()
        small_col_copy(c, lax.rem(c + n_col - k, n_col)).wait_recv()
        return carry

    lax.fori_loop(1, n_col, wait_small_col, 0)
    own_small.wait()
    mid[...] = jnp.sum(got_small_col[...], axis=0)

    own_mid = pltpu.make_async_copy(mid, got_small_row.at[r], local_sem.at[3])
    own_mid.start()

    def start_small_row(k, carry):
        small_row_copy(lax.rem(r + k, n_row), r).start()
        return carry

    lax.fori_loop(1, n_row, start_small_row, 0)

    def wait_col(k, carry):
        row_copy(lax.rem(c + k, n_col), c).wait_send()
        row_copy(c, lax.rem(c + n_col - k, n_col)).wait_recv()
        return carry

    def wait_row(k, carry):
        col_copy(lax.rem(r + k, n_row), r).wait_send()
        col_copy(r, lax.rem(r + n_row - k, n_row)).wait_recv()
        return carry

    lax.fori_loop(1, n_col, wait_col, 0)
    lax.fori_loop(1, n_row, wait_row, 0)
    own_row.wait()
    own_col.wait()
    out_ref[...] = base_ref[...] + jnp.sum(got_row[...], axis=0) + jnp.sum(got_col[...], axis=0)

    if forward:
        send_fr, recv_fr, send_fc, recv_fc = rest[14:]

        def fwd_row_copy(j, src):
            return pltpu.make_async_remote_copy(
                src_ref=out_ref,
                dst_ref=img_row.at[:, pl.ds(src * vt, vt)],
                send_sem=send_fr.at[j],
                recv_sem=recv_fr.at[src],
                device_id=(r, j),
                device_id_type=MESH,
            )

        def fwd_col_copy(i, src):
            return pltpu.make_async_remote_copy(
                src_ref=out_ref,
                dst_ref=img_col.at[:, pl.ds(src * vt, vt)],
                send_sem=send_fc.at[i],
                recv_sem=recv_fc.at[src],
                device_id=(i, c),
                device_id_type=MESH,
            )

        own_fr = pltpu.make_async_copy(out_ref, img_row.at[:, pl.ds(c * vt, vt)], local_sem.at[4])
        own_fc = pltpu.make_async_copy(out_ref, img_col.at[:, pl.ds(r * vt, vt)], local_sem.at[5])
        own_fr.start()
        own_fc.start()

        def start_fr(k, carry):
            fwd_row_copy(lax.rem(c + k, n_col), c).start()
            return carry

        def start_fc(k, carry):
            fwd_col_copy(lax.rem(r + k, n_row), r).start()
            return carry

        lax.fori_loop(1, n_row, start_fc, 0)
        lax.fori_loop(1, n_col, start_fr, 0)

    def wait_small_row(k, carry):
        small_row_copy(lax.rem(r + k, n_row), r).wait_send()
        small_row_copy(r, lax.rem(r + n_row - k, n_row)).wait_recv()
        return carry

    lax.fori_loop(1, n_row, wait_small_row, 0)
    own_mid.wait()
    small_out[...] = jnp.sum(got_small_row[...], axis=0)

    if forward:
        def wait_fr(k, carry):
            fwd_row_copy(lax.rem(c + k, n_col), c).wait_send()
            fwd_row_copy(c, lax.rem(c + n_col - k, n_col)).wait_recv()
            return carry

        def wait_fc(k, carry):
            fwd_col_copy(lax.rem(r + k, n_row), r).wait_send()
            fwd_col_copy(r, lax.rem(r + n_row - k, n_row)).wait_recv()
            return carry

        lax.fori_loop(1, n_col, wait_fr, 0)
        lax.fori_loop(1, n_row, wait_fc, 0)
        own_fr.wait()
        own_fc.wait()


def pack_small(values):
    flat = jnp.concatenate([v.reshape(-1) for v in values])
    tile = 8 * 128
    padded = -(-flat.shape[0] // tile) * tile
    return jnp.pad(flat, (0, padded - flat.shape[0])).reshape(-1, 128)


def unpack_small(total, values):
    total = total.reshape(-1)
    out, start = [], 0
    for v in values:
        out.append(total[start:start + v.size].reshape(v.shape))
        start += v.size
    return out


def reduce_tiles(base_tiles, row_sum, col_sum, small, n_row, n_col, collective_id, forward=False):
    k, vt = base_tiles.shape
    s = small.shape[0]
    vmem = pl.BlockSpec(memory_space=pltpu.VMEM)
    out_shape = [
        jax.ShapeDtypeStruct((k, vt), base_tiles.dtype),
        jax.ShapeDtypeStruct((s, 128), jnp.float32),
    ]
    extra_sems = []
    if forward:
        out_shape += [
            jax.ShapeDtypeStruct((k, n_col * vt), base_tiles.dtype),
            jax.ShapeDtypeStruct((k, n_row * vt), base_tiles.dtype),
        ]
        extra_sems = [
            pltpu.SemaphoreType.DMA((n_col,)),
            pltpu.SemaphoreType.DMA((n_col,)),
            pltpu.SemaphoreType.DMA((n_row,)),
            pltpu.SemaphoreType.DMA((n_row,)),
        ]
    return pl.pallas_call(
        functools.partial(_reduce_kernel, n_row, n_col, forward),
        out_shape=tuple(out_shape),
        in_specs=[vmem, vmem, vmem, vmem],
        out_specs=tuple(vmem for _ in out_shape),
        scratch_shapes=[
            pltpu.VMEM((n_col, k, vt), jnp.float32),
            pltpu.VMEM((n_row, k, vt), jnp.float32),
            pltpu.VMEM((n_col, s, 128), jnp.float32),
            pltpu.VMEM((s, 128), jnp.float32),
            pltpu.VMEM((n_row, s, 128), jnp.float32),
            pltpu.SemaphoreType.DMA((n_col,)),
            pltpu.SemaphoreType.DMA((n_col,)),
            pltpu.SemaphoreType.DMA((n_row,)),
            pltpu.SemaphoreType.DMA((n_row,)),
            pltpu.SemaphoreType.DMA((n_col,)),
            pltpu.SemaphoreType.DMA((n_col,)),
            pltpu.SemaphoreType.DMA((n_row,)),
            pltpu.SemaphoreType.DMA((n_row,)),
            pltpu.SemaphoreType.DMA((6,)),
        ] + extra_sems,
        compiler_params=pltpu.CompilerParams(collective_id=collective_id, has_side_effects=True),
    )(base_tiles, row_sum, col_sum, small)


def _slots_kernel(group, rows_k, tile, rows_ref, cols_ref, count_ref, tiles_ref, rowv_ref, colv_ref,
                  rsum_ref, csum_ref):
    g = pl.program_id(0)

    @pl.when(g == 0)
    def _():
        rsum_ref[...] = jnp.zeros_like(rsum_ref)
        csum_ref[...] = jnp.zeros_like(csum_ref)

    for s in range(group):
        slot = g * group + s

        @pl.when(slot < count_ref[0])
        def _():
            a = pl.multiple_of(rows_ref[slot] * tile, tile)
            b = pl.multiple_of(cols_ref[slot] * tile, tile)
            high, low = split_bf16(tiles_ref[s])
            rsum_ref[:, pl.ds(a, tile)] += dot3(
                split_bf16(colv_ref[pl.ds(0, rows_k), pl.ds(b, tile)]),
                jnp.concatenate([high, low], axis=0), (((1,), (1,)), ((), ())),
            )
            csum_ref[:, pl.ds(b, tile)] += dot3(
                split_bf16(rowv_ref[pl.ds(0, rows_k), pl.ds(a, tile)]),
                jnp.concatenate([high, low], axis=1), (((1,), (0,)), ((), ())),
            )


def split_bf16(x):
    high = x.astype(jnp.bfloat16)
    return high, (x - high.astype(jnp.float32)).astype(jnp.bfloat16)


def dot3(left, right, dims):
    rows = left[0].shape[0]
    both = lax.dot_general(
        jnp.concatenate([left[0], left[1]], axis=0), right, dims, preferred_element_type=jnp.float32
    )
    width = both.shape[1] // 2
    return both[:rows, :width] + (both[rows:, :width] + both[:rows, width:])


def slot_products(blocks, rows_here, cols_here, live_count, row_tiles, column_tiles, rows_k):
    slot_count, tile, _ = blocks.shape
    sums_shape = lambda v: (rows_k, v.shape[1])
    group = group_width
    groups = slot_count // group

    def tile_map(g, rows, cols, count):
        last = jnp.maximum(count[0] - 1, 0) // group
        return (jnp.minimum(g, last), 0, 0)

    def whole(g, rows, cols, count):
        return (0, 0)

    grid_spec = pltpu.PrefetchScalarGridSpec(
        num_scalar_prefetch=3,
        grid=(groups,),
        in_specs=[
            pl.BlockSpec((group, tile, tile), tile_map),
            pl.BlockSpec(row_tiles.shape, whole),
            pl.BlockSpec(column_tiles.shape, whole),
        ],
        out_specs=[
            pl.BlockSpec(sums_shape(row_tiles), whole),
            pl.BlockSpec(sums_shape(column_tiles), whole),
        ],
    )
    return pl.pallas_call(
        functools.partial(_slots_kernel, group, rows_k, tile),
        grid_spec=grid_spec,
        out_shape=(
            jax.ShapeDtypeStruct(sums_shape(row_tiles), jnp.float32),
            jax.ShapeDtypeStruct(sums_shape(column_tiles), jnp.float32),
        ),
        compiler_params=pltpu.CompilerParams(dimension_semantics=("arbitrary",)),
    )(rows_here, cols_here, live_count.reshape(1), blocks, row_tiles, column_tiles)


def tile_dot(left, right):
    return jnp.dot(left, right.T, precision=highest)


def lower_solve(factor, rhs, transpose_a=False):
    return lax.linalg.triangular_solve(factor, rhs, left_side=True, lower=True, transpose_a=transpose_a)


def dot_rows(left, right):
    return jnp.dot(left, right.T, precision=highest)


def local(n_row, n_col, tile_values, tile_row, tile_col, counts, diagonal, current, previous, previous_image):
    k = current.shape[0]
    tile = tile_values.shape[-1]
    slot_count = tile_values.shape[2]
    blocks = tile_values.reshape(slot_count, tile, tile)
    rows_here = tile_row.reshape(slot_count)
    cols_here = tile_col.reshape(slot_count)
    live_count = counts.reshape(())

    row_cp, col_cp = gather_tiles(jnp.concatenate([current, previous], 0), n_row, n_col, 0)
    row_sum, col_sum = slot_products(blocks, rows_here, cols_here, live_count, row_cp, col_cp, k)
    row_cur, col_cur = row_cp[:k], col_cp[:k]
    scaled = diagonal[None, :] * current
    small_gram = dot_rows(current, current)
    proj_part = dot_rows(current, scaled) + tile_dot(row_cur, row_sum) + tile_dot(col_cur, col_sum)
    image_tiles, small, row_img, col_img = reduce_tiles(
        scaled, row_sum, col_sum, pack_small((small_gram, proj_part)), n_row, n_col, 1,
        forward=True,
    )
    image = image_tiles
    small_gram, small_proj = unpack_small(small, (small_gram, proj_part))

    factor = lax.linalg.cholesky(small_gram, symmetrize_input=False)
    ritz_matrix = lower_solve(factor, lower_solve(factor, small_proj), transpose_a=True)
    residual = image - jnp.dot(ritz_matrix.T, current, precision=highest)

    def residual_of(img_tiles, cur_tiles):
        fitted = sum(ritz_matrix[l][:, None] * cur_tiles[l:l + 1, :] for l in range(k))
        return img_tiles - fitted

    row_res = residual_of(row_img, row_cur)
    col_res = residual_of(col_img, col_cur)
    row_sum, col_sum = slot_products(blocks, rows_here, cols_here, live_count, row_res, col_res, k)
    search_basis = jnp.concatenate([current, residual, previous], 0)
    row_basis = jnp.concatenate([row_cur, row_res, row_cp[k:]], 0)
    col_basis = jnp.concatenate([col_cur, col_res, col_cp[k:]], 0)
    scaled = diagonal[None, :] * residual
    correlation = dot_rows(search_basis, search_basis)
    residual_part = (
        dot_rows(search_basis, scaled) + tile_dot(row_basis, row_sum) + tile_dot(col_basis, col_sum)
    )
    mixed_part = jnp.concatenate(
        [dot_rows(search_basis, image), residual_part, dot_rows(search_basis, previous_image)], 1
    )
    image_tiles, small = reduce_tiles(
        scaled, row_sum, col_sum, pack_small((correlation, mixed_part)), n_row, n_col, 2
    )
    residual_image = image_tiles
    correlation, mixed_terms = unpack_small(small, (correlation, mixed_part))
    pencil = 0.5 * (mixed_terms + mixed_terms.T)
    lower_factor = lax.linalg.cholesky(correlation, symmetrize_input=False)
    half_solve = lower_solve(lower_factor, pencil)
    reduced = lower_solve(lower_factor, half_solve.T)
    return (image, residual, residual_image, reduced)


def solution(mesh):
    n_row = mesh.shape["row"]
    n_col = mesh.shape["col"]
    return jax.shard_map(
        functools.partial(local, n_row, n_col),
        mesh=mesh,
        in_specs=(
            P("row", "col", None, None, None),
            P("row", "col", None),
            P("row", "col", None),
            P("row", "col"),
            P(("row", "col")),
            P(None, ("row", "col")),
            P(None, ("row", "col")),
            P(None, ("row", "col")),
        ),
        out_specs=(P(None, ("row", "col")), P(None, ("row", "col")), P(None, ("row", "col")), P()),
        check_vma=False,
    )
```

```python
import functools

import jax
import jax.numpy as jnp
from jax import lax
from jax.experimental import pallas as pl
from jax.experimental.pallas import tpu as pltpu
from jax.sharding import PartitionSpec as P

highest = lax.Precision.HIGHEST
group_width = 8
MESH = pl.DeviceIdType.MESH


def _barrier(n_row, n_col, r, c):
    barrier = pltpu.get_barrier_semaphore()

    def greet_col(k, carry):
        pl.semaphore_signal(barrier, 1, device_id=(r, lax.rem(c + k, n_col)), device_id_type=MESH)
        return carry

    def greet_row(k, carry):
        pl.semaphore_signal(barrier, 1, device_id=(lax.rem(r + k, n_row), c), device_id_type=MESH)
        return carry

    lax.fori_loop(1, n_row, greet_row, 0)
    lax.fori_loop(1, n_col, greet_col, 0)
    pl.semaphore_wait(barrier, n_row + n_col - 2)


def _gather_kernel(n_row, n_col, x_ref, rowv_ref, colv_ref, send_row, recv_row, send_col, recv_col, local_sem):
    vt = x_ref.shape[1]
    r = lax.axis_index("row")
    c = lax.axis_index("col")
    _barrier(n_row, n_col, r, c)

    def row_copy(j, src):
        return pltpu.make_async_remote_copy(
            src_ref=x_ref,
            dst_ref=rowv_ref.at[:, pl.ds(src * vt, vt)],
            send_sem=send_row.at[j],
            recv_sem=recv_row.at[src],
            device_id=(r, j),
            device_id_type=MESH,
        )

    def col_copy(i, src):
        return pltpu.make_async_remote_copy(
            src_ref=x_ref,
            dst_ref=colv_ref.at[:, pl.ds(src * vt, vt)],
            send_sem=send_col.at[i],
            recv_sem=recv_col.at[src],
            device_id=(i, c),
            device_id_type=MESH,
        )

    own_row = pltpu.make_async_copy(x_ref, rowv_ref.at[:, pl.ds(c * vt, vt)], local_sem.at[0])
    own_col = pltpu.make_async_copy(x_ref, colv_ref.at[:, pl.ds(r * vt, vt)], local_sem.at[1])
    own_row.start()
    own_col.start()

    def start_col(k, carry):
        row_copy(lax.rem(c + k, n_col), c).start()
        return carry

    def start_row(k, carry):
        col_copy(lax.rem(r + k, n_row), r).start()
        return carry

    lax.fori_loop(1, n_row, start_row, 0)
    lax.fori_loop(1, n_col, start_col, 0)

    def wait_col(k, carry):
        row_copy(lax.rem(c + k, n_col), c).wait_send()
        row_copy(c, lax.rem(c + n_col - k, n_col)).wait_recv()
        return carry

    def wait_row(k, carry):
        col_copy(lax.rem(r + k, n_row), r).wait_send()
        col_copy(r, lax.rem(r + n_row - k, n_row)).wait_recv()
        return carry

    lax.fori_loop(1, n_col, wait_col, 0)
    lax.fori_loop(1, n_row, wait_row, 0)
    own_row.wait()
    own_col.wait()


def gather_tiles(x_tiles, n_row, n_col, collective_id):
    k, vt = x_tiles.shape
    vmem = pl.BlockSpec(memory_space=pltpu.VMEM)
    return pl.pallas_call(
        functools.partial(_gather_kernel, n_row, n_col),
        out_shape=(
            jax.ShapeDtypeStruct((k, n_col * vt), x_tiles.dtype),
            jax.ShapeDtypeStruct((k, n_row * vt), x_tiles.dtype),
        ),
        in_specs=[vmem],
        out_specs=(vmem, vmem),
        scratch_shapes=[
            pltpu.SemaphoreType.DMA((n_col,)),
            pltpu.SemaphoreType.DMA((n_col,)),
            pltpu.SemaphoreType.DMA((n_row,)),
            pltpu.SemaphoreType.DMA((n_row,)),
            pltpu.SemaphoreType.DMA((2,)),
        ],
        compiler_params=pltpu.CompilerParams(collective_id=collective_id, has_side_effects=True),
    )(x_tiles)


def _reduce_kernel(n_row, n_col, forward, base_ref, rsum_ref, csum_ref, small_ref, out_ref, small_out, *rest):
    if forward:
        img_row, img_col = rest[:2]
        rest = rest[2:]
    (got_row, got_col, got_small_col, mid, got_small_row,
     send_row, recv_row, send_col, recv_col,
     send_small_col, recv_small_col, send_small_row, recv_small_row, local_sem) = rest[:14]
    vt = base_ref.shape[1]
    r = lax.axis_index("row")
    c = lax.axis_index("col")
    _barrier(n_row, n_col, r, c)

    def small_col_copy(j, src):
        return pltpu.make_async_remote_copy(
            src_ref=small_ref,
            dst_ref=got_small_col.at[src],
            send_sem=send_small_col.at[j],
            recv_sem=recv_small_col.at[src],
            device_id=(r, j),
            device_id_type=MESH,
        )

    def small_row_copy(i, src):
        return pltpu.make_async_remote_copy(
            src_ref=mid,
            dst_ref=got_small_row.at[src],
            send_sem=send_small_row.at[i],
            recv_sem=recv_small_row.at[src],
            device_id=(i, c),
            device_id_type=MESH,
        )

    def row_copy(j, src):
        return pltpu.make_async_remote_copy(
            src_ref=rsum_ref.at[:, pl.ds(j * vt, vt)],
            dst_ref=got_row.at[src],
            send_sem=send_row.at[j],
            recv_sem=recv_row.at[src],
            device_id=(r, j),
            device_id_type=MESH,
        )

    def col_copy(i, src):
        return pltpu.make_async_remote_copy(
            src_ref=csum_ref.at[:, pl.ds(i * vt, vt)],
            dst_ref=got_col.at[src],
            send_sem=send_col.at[i],
            recv_sem=recv_col.at[src],
            device_id=(i, c),
            device_id_type=MESH,
        )

    own_small = pltpu.make_async_copy(small_ref, got_small_col.at[c], local_sem.at[2])
    own_small.start()

    def start_small_col(k, carry):
        small_col_copy(lax.rem(c + k, n_col), c).start()
        return carry

    lax.fori_loop(1, n_col, start_small_col, 0)

    own_row = pltpu.make_async_copy(rsum_ref.at[:, pl.ds(c * vt, vt)], got_row.at[c], local_sem.at[0])
    own_col = pltpu.make_async_copy(csum_ref.at[:, pl.ds(r * vt, vt)], got_col.at[r], local_sem.at[1])
    own_row.start()
    own_col.start()

    def start_col(k, carry):
        row_copy(lax.rem(c + k, n_col), c).start()
        return carry

    def start_row(k, carry):
        col_copy(lax.rem(r + k, n_row), r).start()
        return carry

    lax.fori_loop(1, n_row, start_row, 0)
    lax.fori_loop(1, n_col, start_col, 0)

    def wait_small_col(k, carry):
        small_col_copy(lax.rem(c + k, n_col), c).wait_send()
        small_col_copy(c, lax.rem(c + n_col - k, n_col)).wait_recv()
        return carry

    lax.fori_loop(1, n_col, wait_small_col, 0)
    own_small.wait()
    mid[...] = jnp.sum(got_small_col[...], axis=0)

    own_mid = pltpu.make_async_copy(mid, got_small_row.at[r], local_sem.at[3])
    own_mid.start()

    def start_small_row(k, carry):
        small_row_copy(lax.rem(r + k, n_row), r).start()
        return carry

    lax.fori_loop(1, n_row, start_small_row, 0)

    def wait_col(k, carry):
        row_copy(lax.rem(c + k, n_col), c).wait_send()
        row_copy(c, lax.rem(c + n_col - k, n_col)).wait_recv()
        return carry

    def wait_row(k, carry):
        col_copy(lax.rem(r + k, n_row), r).wait_send()
        col_copy(r, lax.rem(r + n_row - k, n_row)).wait_recv()
        return carry

    lax.fori_loop(1, n_col, wait_col, 0)
    lax.fori_loop(1, n_row, wait_row, 0)
    own_row.wait()
    own_col.wait()
    out_ref[...] = base_ref[...] + jnp.sum(got_row[...], axis=0) + jnp.sum(got_col[...], axis=0)

    if forward:
        send_fr, recv_fr, send_fc, recv_fc = rest[14:]

        def fwd_row_copy(j, src):
            return pltpu.make_async_remote_copy(
                src_ref=out_ref,
                dst_ref=img_row.at[:, pl.ds(src * vt, vt)],
                send_sem=send_fr.at[j],
                recv_sem=recv_fr.at[src],
                device_id=(r, j),
                device_id_type=MESH,
            )

        def fwd_col_copy(i, src):
            return pltpu.make_async_remote_copy(
                src_ref=out_ref,
                dst_ref=img_col.at[:, pl.ds(src * vt, vt)],
                send_sem=send_fc.at[i],
                recv_sem=recv_fc.at[src],
                device_id=(i, c),
                device_id_type=MESH,
            )

        own_fr = pltpu.make_async_copy(out_ref, img_row.at[:, pl.ds(c * vt, vt)], local_sem.at[4])
        own_fc = pltpu.make_async_copy(out_ref, img_col.at[:, pl.ds(r * vt, vt)], local_sem.at[5])
        own_fr.start()
        own_fc.start()

        def start_fr(k, carry):
            fwd_row_copy(lax.rem(c + k, n_col), c).start()
            return carry

        def start_fc(k, carry):
            fwd_col_copy(lax.rem(r + k, n_row), r).start()
            return carry

        lax.fori_loop(1, n_row, start_fc, 0)
        lax.fori_loop(1, n_col, start_fr, 0)

    def wait_small_row(k, carry):
        small_row_copy(lax.rem(r + k, n_row), r).wait_send()
        small_row_copy(r, lax.rem(r + n_row - k, n_row)).wait_recv()
        return carry

    lax.fori_loop(1, n_row, wait_small_row, 0)
    own_mid.wait()
    small_out[...] = jnp.sum(got_small_row[...], axis=0)

    if forward:
        def wait_fr(k, carry):
            fwd_row_copy(lax.rem(c + k, n_col), c).wait_send()
            fwd_row_copy(c, lax.rem(c + n_col - k, n_col)).wait_recv()
            return carry

        def wait_fc(k, carry):
            fwd_col_copy(lax.rem(r + k, n_row), r).wait_send()
            fwd_col_copy(r, lax.rem(r + n_row - k, n_row)).wait_recv()
            return carry

        lax.fori_loop(1, n_col, wait_fr, 0)
        lax.fori_loop(1, n_row, wait_fc, 0)
        own_fr.wait()
        own_fc.wait()


def pack_small(values):
    flat = jnp.concatenate([v.reshape(-1) for v in values])
    tile = 8 * 128
    padded = -(-flat.shape[0] // tile) * tile
    return jnp.pad(flat, (0, padded - flat.shape[0])).reshape(-1, 128)


def unpack_small(total, values):
    total = total.reshape(-1)
    out, start = [], 0
    for v in values:
        out.append(total[start:start + v.size].reshape(v.shape))
        start += v.size
    return out


def reduce_tiles(base_tiles, row_sum, col_sum, small, n_row, n_col, collective_id, forward=False):
    k, vt = base_tiles.shape
    s = small.shape[0]
    vmem = pl.BlockSpec(memory_space=pltpu.VMEM)
    out_shape = [
        jax.ShapeDtypeStruct((k, vt), base_tiles.dtype),
        jax.ShapeDtypeStruct((s, 128), jnp.float32),
    ]
    extra_sems = []
    if forward:
        out_shape += [
            jax.ShapeDtypeStruct((k, n_col * vt), base_tiles.dtype),
            jax.ShapeDtypeStruct((k, n_row * vt), base_tiles.dtype),
        ]
        extra_sems = [
            pltpu.SemaphoreType.DMA((n_col,)),
            pltpu.SemaphoreType.DMA((n_col,)),
            pltpu.SemaphoreType.DMA((n_row,)),
            pltpu.SemaphoreType.DMA((n_row,)),
        ]
    return pl.pallas_call(
        functools.partial(_reduce_kernel, n_row, n_col, forward),
        out_shape=tuple(out_shape),
        in_specs=[vmem, vmem, vmem, vmem],
        out_specs=tuple(vmem for _ in out_shape),
        scratch_shapes=[
            pltpu.VMEM((n_col, k, vt), jnp.float32),
            pltpu.VMEM((n_row, k, vt), jnp.float32),
            pltpu.VMEM((n_col, s, 128), jnp.float32),
            pltpu.VMEM((s, 128), jnp.float32),
            pltpu.VMEM((n_row, s, 128), jnp.float32),
            pltpu.SemaphoreType.DMA((n_col,)),
            pltpu.SemaphoreType.DMA((n_col,)),
            pltpu.SemaphoreType.DMA((n_row,)),
            pltpu.SemaphoreType.DMA((n_row,)),
            pltpu.SemaphoreType.DMA((n_col,)),
            pltpu.SemaphoreType.DMA((n_col,)),
            pltpu.SemaphoreType.DMA((n_row,)),
            pltpu.SemaphoreType.DMA((n_row,)),
            pltpu.SemaphoreType.DMA((6,)),
        ] + extra_sems,
        compiler_params=pltpu.CompilerParams(collective_id=collective_id, has_side_effects=True),
    )(base_tiles, row_sum, col_sum, small)


def _slots_kernel(group, rows_k, tile, rows_ref, cols_ref, count_ref, tiles_ref, rowv_ref, colv_ref,
                  rsum_ref, csum_ref):
    g = pl.program_id(0)

    @pl.when(g == 0)
    def _():
        rsum_ref[...] = jnp.zeros_like(rsum_ref)
        csum_ref[...] = jnp.zeros_like(csum_ref)

    for s in range(group):
        slot = g * group + s

        @pl.when(slot < count_ref[0])
        def _():
            a = pl.multiple_of(rows_ref[slot] * tile, tile)
            b = pl.multiple_of(cols_ref[slot] * tile, tile)
            high, low = split_bf16(tiles_ref[s])
            rsum_ref[:, pl.ds(a, tile)] += dot3(
                split_bf16(colv_ref[pl.ds(0, rows_k), pl.ds(b, tile)]),
                jnp.concatenate([high, low], axis=0), (((1,), (1,)), ((), ())),
            )
            csum_ref[:, pl.ds(b, tile)] += dot3(
                split_bf16(rowv_ref[pl.ds(0, rows_k), pl.ds(a, tile)]),
                jnp.concatenate([high, low], axis=1), (((1,), (0,)), ((), ())),
            )


def split_bf16(x):
    high = x.astype(jnp.bfloat16)
    return high, (x - high.astype(jnp.float32)).astype(jnp.bfloat16)


def dot3(left, right, dims):
    rows = left[0].shape[0]
    both = lax.dot_general(
        jnp.concatenate([left[0], left[1]], axis=0), right, dims, preferred_element_type=jnp.float32
    )
    width = both.shape[1] // 2
    return both[:rows, :width] + (both[rows:, :width] + both[:rows, width:])


def slot_products(blocks, rows_here, cols_here, live_count, row_tiles, column_tiles, rows_k):
    slot_count, tile, _ = blocks.shape
    sums_shape = lambda v: (rows_k, v.shape[1])
    group = group_width
    groups = slot_count // group

    def tile_map(g, rows, cols, count):
        last = jnp.maximum(count[0] - 1, 0) // group
        return (jnp.minimum(g, last), 0, 0)

    def whole(g, rows, cols, count):
        return (0, 0)

    grid_spec = pltpu.PrefetchScalarGridSpec(
        num_scalar_prefetch=3,
        grid=(groups,),
        in_specs=[
            pl.BlockSpec((group, tile, tile), tile_map),
            pl.BlockSpec(row_tiles.shape, whole),
            pl.BlockSpec(column_tiles.shape, whole),
        ],
        out_specs=[
            pl.BlockSpec(sums_shape(row_tiles), whole),
            pl.BlockSpec(sums_shape(column_tiles), whole),
        ],
    )
    return pl.pallas_call(
        functools.partial(_slots_kernel, group, rows_k, tile),
        grid_spec=grid_spec,
        out_shape=(
            jax.ShapeDtypeStruct(sums_shape(row_tiles), jnp.float32),
            jax.ShapeDtypeStruct(sums_shape(column_tiles), jnp.float32),
        ),
        compiler_params=pltpu.CompilerParams(dimension_semantics=("arbitrary",)),
    )(rows_here, cols_here, live_count.reshape(1), blocks, row_tiles, column_tiles)


def tile_dot(left, right):
    return jnp.dot(left, right.T, precision=highest)


def lower_solve(factor, rhs, transpose_a=False):
    return lax.linalg.triangular_solve(factor, rhs, left_side=True, lower=True, transpose_a=transpose_a)


def dot_rows(left, right):
    return jnp.dot(left, right.T, precision=highest)


def local(n_row, n_col, tile_values, tile_row, tile_col, counts, diagonal, current, previous, previous_image):
    k = current.shape[0]
    tile = tile_values.shape[-1]
    slot_count = tile_values.shape[2]
    blocks = tile_values.reshape(slot_count, tile, tile)
    rows_here = tile_row.reshape(slot_count)
    cols_here = tile_col.reshape(slot_count)
    live_count = counts.reshape(())

    row_cp, col_cp = gather_tiles(jnp.concatenate([current, previous], 0), n_row, n_col, 0)
    row_sum, col_sum = slot_products(blocks, rows_here, cols_here, live_count, row_cp, col_cp, k)
    row_cur, col_cur = row_cp[:k], col_cp[:k]
    scaled = diagonal[None, :] * current
    small_gram = dot_rows(current, current)
    proj_part = dot_rows(current, scaled) + tile_dot(row_cur, row_sum) + tile_dot(col_cur, col_sum)
    image_tiles, small, row_img, col_img = reduce_tiles(
        scaled, row_sum, col_sum, pack_small((small_gram, proj_part)), n_row, n_col, 1,
        forward=True,
    )
    image = image_tiles
    small_gram, small_proj = unpack_small(small, (small_gram, proj_part))

    factor = lax.linalg.cholesky(small_gram, symmetrize_input=False)
    ritz_matrix = lower_solve(factor, lower_solve(factor, small_proj), transpose_a=True)
    residual = image - jnp.dot(ritz_matrix.T, current, precision=highest)

    def residual_of(img_tiles, cur_tiles):
        fitted = sum(ritz_matrix[l][:, None] * cur_tiles[l:l + 1, :] for l in range(k))
        return img_tiles - fitted

    row_res = residual_of(row_img, row_cur)
    col_res = residual_of(col_img, col_cur)
    row_sum, col_sum = slot_products(blocks, rows_here, cols_here, live_count, row_res, col_res, k)
    search_basis = jnp.concatenate([current, residual, previous], 0)
    row_basis = jnp.concatenate([row_cur, row_res, row_cp[k:]], 0)
    col_basis = jnp.concatenate([col_cur, col_res, col_cp[k:]], 0)
    scaled = diagonal[None, :] * residual
    correlation = dot_rows(search_basis, search_basis)
    residual_part = (
        dot_rows(search_basis, scaled) + tile_dot(row_basis, row_sum) + tile_dot(col_basis, col_sum)
    )
    mixed_part = jnp.concatenate(
        [dot_rows(search_basis, image), residual_part, dot_rows(search_basis, previous_image)], 1
    )
    image_tiles, small = reduce_tiles(
        scaled, row_sum, col_sum, pack_small((correlation, mixed_part)), n_row, n_col, 2
    )
    residual_image = image_tiles
    correlation, mixed_terms = unpack_small(small, (correlation, mixed_part))
    pencil = 0.5 * (mixed_terms + mixed_terms.T)
    lower_factor = lax.linalg.cholesky(correlation, symmetrize_input=False)
    half_solve = lower_solve(lower_factor, pencil)
    reduced = lower_solve(lower_factor, half_solve.T)
    return (image, residual, residual_image, reduced)


def solution(mesh):
    n_row = mesh.shape["row"]
    n_col = mesh.shape["col"]
    return jax.shard_map(
        functools.partial(local, n_row, n_col),
        mesh=mesh,
        in_specs=(
            P("row", "col", None, None, None),
            P("row", "col", None),
            P("row", "col", None),
            P("row", "col"),
            P(("row", "col")),
            P(None, ("row", "col")),
            P(None, ("row", "col")),
            P(None, ("row", "col")),
        ),
        out_specs=(P(None, ("row", "col")), P(None, ("row", "col")), P(None, ("row", "col")), P()),
        check_vma=False,
    )
```

```python
import functools

import jax
import jax.numpy as jnp
from jax import lax
from jax.experimental import pallas as pl
from jax.experimental.pallas import tpu as pltpu
from jax.sharding import PartitionSpec as P

highest = lax.Precision.HIGHEST
group_width = 8
MESH = pl.DeviceIdType.MESH


def _barrier(n_row, n_col, r, c):
    barrier = pltpu.get_barrier_semaphore()

    def greet_col(k, carry):
        pl.semaphore_signal(barrier, 1, device_id=(r, lax.rem(c + k, n_col)), device_id_type=MESH)
        return carry

    def greet_row(k, carry):
        pl.semaphore_signal(barrier, 1, device_id=(lax.rem(r + k, n_row), c), device_id_type=MESH)
        return carry

    lax.fori_loop(1, n_col, greet_col, 0)
    lax.fori_loop(1, n_row, greet_row, 0)
    pl.semaphore_wait(barrier, n_row + n_col - 2)


def _gather_kernel(n_row, n_col, x_ref, rowv_ref, colv_ref, send_row, recv_row, send_col, recv_col, local_sem):
    vt = x_ref.shape[1]
    r = lax.axis_index("row")
    c = lax.axis_index("col")
    _barrier(n_row, n_col, r, c)

    def row_copy(j, src):
        return pltpu.make_async_remote_copy(
            src_ref=x_ref,
            dst_ref=rowv_ref.at[:, pl.ds(src * vt, vt)],
            send_sem=send_row.at[j],
            recv_sem=recv_row.at[src],
            device_id=(r, j),
            device_id_type=MESH,
        )

    def col_copy(i, src):
        return pltpu.make_async_remote_copy(
            src_ref=x_ref,
            dst_ref=colv_ref.at[:, pl.ds(src * vt, vt)],
            send_sem=send_col.at[i],
            recv_sem=recv_col.at[src],
            device_id=(i, c),
            device_id_type=MESH,
        )

    own_row = pltpu.make_async_copy(x_ref, rowv_ref.at[:, pl.ds(c * vt, vt)], local_sem.at[0])
    own_col = pltpu.make_async_copy(x_ref, colv_ref.at[:, pl.ds(r * vt, vt)], local_sem.at[1])
    own_row.start()
    own_col.start()

    def start_col(k, carry):
        row_copy(lax.rem(c + k, n_col), c).start()
        return carry

    def start_row(k, carry):
        col_copy(lax.rem(r + k, n_row), r).start()
        return carry

    lax.fori_loop(1, n_col, start_col, 0)
    lax.fori_loop(1, n_row, start_row, 0)

    def wait_col(k, carry):
        row_copy(lax.rem(c + k, n_col), c).wait_send()
        row_copy(c, lax.rem(c + n_col - k, n_col)).wait_recv()
        return carry

    def wait_row(k, carry):
        col_copy(lax.rem(r + k, n_row), r).wait_send()
        col_copy(r, lax.rem(r + n_row - k, n_row)).wait_recv()
        return carry

    lax.fori_loop(1, n_col, wait_col, 0)
    lax.fori_loop(1, n_row, wait_row, 0)
    own_row.wait()
    own_col.wait()


def gather_tiles(x_tiles, n_row, n_col, collective_id):
    k, vt = x_tiles.shape
    vmem = pl.BlockSpec(memory_space=pltpu.VMEM)
    return pl.pallas_call(
        functools.partial(_gather_kernel, n_row, n_col),
        out_shape=(
            jax.ShapeDtypeStruct((k, n_col * vt), x_tiles.dtype),
            jax.ShapeDtypeStruct((k, n_row * vt), x_tiles.dtype),
        ),
        in_specs=[vmem],
        out_specs=(vmem, vmem),
        scratch_shapes=[
            pltpu.SemaphoreType.DMA((n_col,)),
            pltpu.SemaphoreType.DMA((n_col,)),
            pltpu.SemaphoreType.DMA((n_row,)),
            pltpu.SemaphoreType.DMA((n_row,)),
            pltpu.SemaphoreType.DMA((2,)),
        ],
        compiler_params=pltpu.CompilerParams(collective_id=collective_id, has_side_effects=True),
    )(x_tiles)


def _reduce_kernel(n_row, n_col, forward, base_ref, rsum_ref, csum_ref, small_ref, out_ref, small_out, *rest):
    if forward:
        img_row, img_col = rest[:2]
        rest = rest[2:]
    (got_row, got_col, got_small_col, mid, got_small_row,
     send_row, recv_row, send_col, recv_col,
     send_small_col, recv_small_col, send_small_row, recv_small_row, local_sem) = rest[:14]
    vt = base_ref.shape[1]
    r = lax.axis_index("row")
    c = lax.axis_index("col")
    _barrier(n_row, n_col, r, c)

    def small_col_copy(j, src):
        return pltpu.make_async_remote_copy(
            src_ref=small_ref,
            dst_ref=got_small_col.at[src],
            send_sem=send_small_col.at[j],
            recv_sem=recv_small_col.at[src],
            device_id=(r, j),
            device_id_type=MESH,
        )

    def small_row_copy(i, src):
        return pltpu.make_async_remote_copy(
            src_ref=mid,
            dst_ref=got_small_row.at[src],
            send_sem=send_small_row.at[i],
            recv_sem=recv_small_row.at[src],
            device_id=(i, c),
            device_id_type=MESH,
        )

    def row_copy(j, src):
        return pltpu.make_async_remote_copy(
            src_ref=rsum_ref.at[:, pl.ds(j * vt, vt)],
            dst_ref=got_row.at[src],
            send_sem=send_row.at[j],
            recv_sem=recv_row.at[src],
            device_id=(r, j),
            device_id_type=MESH,
        )

    def col_copy(i, src):
        return pltpu.make_async_remote_copy(
            src_ref=csum_ref.at[:, pl.ds(i * vt, vt)],
            dst_ref=got_col.at[src],
            send_sem=send_col.at[i],
            recv_sem=recv_col.at[src],
            device_id=(i, c),
            device_id_type=MESH,
        )

    own_small = pltpu.make_async_copy(small_ref, got_small_col.at[c], local_sem.at[2])
    own_small.start()

    def start_small_col(k, carry):
        small_col_copy(lax.rem(c + k, n_col), c).start()
        return carry

    lax.fori_loop(1, n_col, start_small_col, 0)

    own_row = pltpu.make_async_copy(rsum_ref.at[:, pl.ds(c * vt, vt)], got_row.at[c], local_sem.at[0])
    own_col = pltpu.make_async_copy(csum_ref.at[:, pl.ds(r * vt, vt)], got_col.at[r], local_sem.at[1])
    own_row.start()
    own_col.start()

    def start_col(k, carry):
        row_copy(lax.rem(c + k, n_col), c).start()
        return carry

    def start_row(k, carry):
        col_copy(lax.rem(r + k, n_row), r).start()
        return carry

    lax.fori_loop(1, n_row, start_row, 0)
    lax.fori_loop(1, n_col, start_col, 0)

    def wait_small_col(k, carry):
        small_col_copy(lax.rem(c + k, n_col), c).wait_send()
        small_col_copy(c, lax.rem(c + n_col - k, n_col)).wait_recv()
        return carry

    lax.fori_loop(1, n_col, wait_small_col, 0)
    own_small.wait()
    mid[...] = jnp.sum(got_small_col[...], axis=0)

    own_mid = pltpu.make_async_copy(mid, got_small_row.at[r], local_sem.at[3])
    own_mid.start()

    def start_small_row(k, carry):
        small_row_copy(lax.rem(r + k, n_row), r).start()
        return carry

    lax.fori_loop(1, n_row, start_small_row, 0)

    def wait_col(k, carry):
        row_copy(lax.rem(c + k, n_col), c).wait_send()
        row_copy(c, lax.rem(c + n_col - k, n_col)).wait_recv()
        return carry

    def wait_row(k, carry):
        col_copy(lax.rem(r + k, n_row), r).wait_send()
        col_copy(r, lax.rem(r + n_row - k, n_row)).wait_recv()
        return carry

    lax.fori_loop(1, n_col, wait_col, 0)
    lax.fori_loop(1, n_row, wait_row, 0)
    own_row.wait()
    own_col.wait()
    out_ref[...] = base_ref[...] + jnp.sum(got_row[...], axis=0) + jnp.sum(got_col[...], axis=0)

    if forward:
        send_fr, recv_fr, send_fc, recv_fc = rest[14:]

        def fwd_row_copy(j, src):
            return pltpu.make_async_remote_copy(
                src_ref=out_ref,
                dst_ref=img_row.at[:, pl.ds(src * vt, vt)],
                send_sem=send_fr.at[j],
                recv_sem=recv_fr.at[src],
                device_id=(r, j),
                device_id_type=MESH,
            )

        def fwd_col_copy(i, src):
            return pltpu.make_async_remote_copy(
                src_ref=out_ref,
                dst_ref=img_col.at[:, pl.ds(src * vt, vt)],
                send_sem=send_fc.at[i],
                recv_sem=recv_fc.at[src],
                device_id=(i, c),
                device_id_type=MESH,
            )

        own_fr = pltpu.make_async_copy(out_ref, img_row.at[:, pl.ds(c * vt, vt)], local_sem.at[4])
        own_fc = pltpu.make_async_copy(out_ref, img_col.at[:, pl.ds(r * vt, vt)], local_sem.at[5])
        own_fr.start()
        own_fc.start()

        def start_fr(k, carry):
            fwd_row_copy(lax.rem(c + k, n_col), c).start()
            return carry

        def start_fc(k, carry):
            fwd_col_copy(lax.rem(r + k, n_row), r).start()
            return carry

        lax.fori_loop(1, n_row, start_fc, 0)
        lax.fori_loop(1, n_col, start_fr, 0)

    def wait_small_row(k, carry):
        small_row_copy(lax.rem(r + k, n_row), r).wait_send()
        small_row_copy(r, lax.rem(r + n_row - k, n_row)).wait_recv()
        return carry

    lax.fori_loop(1, n_row, wait_small_row, 0)
    own_mid.wait()
    small_out[...] = jnp.sum(got_small_row[...], axis=0)

    if forward:
        def wait_fr(k, carry):
            fwd_row_copy(lax.rem(c + k, n_col), c).wait_send()
            fwd_row_copy(c, lax.rem(c + n_col - k, n_col)).wait_recv()
            return carry

        def wait_fc(k, carry):
            fwd_col_copy(lax.rem(r + k, n_row), r).wait_send()
            fwd_col_copy(r, lax.rem(r + n_row - k, n_row)).wait_recv()
            return carry

        lax.fori_loop(1, n_col, wait_fr, 0)
        lax.fori_loop(1, n_row, wait_fc, 0)
        own_fr.wait()
        own_fc.wait()


def pack_small(values):
    flat = jnp.concatenate([v.reshape(-1) for v in values])
    tile = 8 * 128
    padded = -(-flat.shape[0] // tile) * tile
    return jnp.pad(flat, (0, padded - flat.shape[0])).reshape(-1, 128)


def unpack_small(total, values):
    total = total.reshape(-1)
    out, start = [], 0
    for v in values:
        out.append(total[start:start + v.size].reshape(v.shape))
        start += v.size
    return out


def reduce_tiles(base_tiles, row_sum, col_sum, small, n_row, n_col, collective_id, forward=False):
    k, vt = base_tiles.shape
    s = small.shape[0]
    vmem = pl.BlockSpec(memory_space=pltpu.VMEM)
    out_shape = [
        jax.ShapeDtypeStruct((k, vt), base_tiles.dtype),
        jax.ShapeDtypeStruct((s, 128), jnp.float32),
    ]
    extra_sems = []
    if forward:
        out_shape += [
            jax.ShapeDtypeStruct((k, n_col * vt), base_tiles.dtype),
            jax.ShapeDtypeStruct((k, n_row * vt), base_tiles.dtype),
        ]
        extra_sems = [
            pltpu.SemaphoreType.DMA((n_col,)),
            pltpu.SemaphoreType.DMA((n_col,)),
            pltpu.SemaphoreType.DMA((n_row,)),
            pltpu.SemaphoreType.DMA((n_row,)),
        ]
    return pl.pallas_call(
        functools.partial(_reduce_kernel, n_row, n_col, forward),
        out_shape=tuple(out_shape),
        in_specs=[vmem, vmem, vmem, vmem],
        out_specs=tuple(vmem for _ in out_shape),
        scratch_shapes=[
            pltpu.VMEM((n_col, k, vt), jnp.float32),
            pltpu.VMEM((n_row, k, vt), jnp.float32),
            pltpu.VMEM((n_col, s, 128), jnp.float32),
            pltpu.VMEM((s, 128), jnp.float32),
            pltpu.VMEM((n_row, s, 128), jnp.float32),
            pltpu.SemaphoreType.DMA((n_col,)),
            pltpu.SemaphoreType.DMA((n_col,)),
            pltpu.SemaphoreType.DMA((n_row,)),
            pltpu.SemaphoreType.DMA((n_row,)),
            pltpu.SemaphoreType.DMA((n_col,)),
            pltpu.SemaphoreType.DMA((n_col,)),
            pltpu.SemaphoreType.DMA((n_row,)),
            pltpu.SemaphoreType.DMA((n_row,)),
            pltpu.SemaphoreType.DMA((6,)),
        ] + extra_sems,
        compiler_params=pltpu.CompilerParams(collective_id=collective_id, has_side_effects=True),
    )(base_tiles, row_sum, col_sum, small)


def _slots_kernel(group, rows_k, tile, rows_ref, cols_ref, count_ref, tiles_ref, rowv_ref, colv_ref,
                  rsum_ref, csum_ref):
    g = pl.program_id(0)

    @pl.when(g == 0)
    def _():
        rsum_ref[...] = jnp.zeros_like(rsum_ref)
        csum_ref[...] = jnp.zeros_like(csum_ref)

    for s in range(group):
        slot = g * group + s

        @pl.when(slot < count_ref[0])
        def _():
            a = pl.multiple_of(rows_ref[slot] * tile, tile)
            b = pl.multiple_of(cols_ref[slot] * tile, tile)
            high, low = split_bf16(tiles_ref[s])
            rsum_ref[:, pl.ds(a, tile)] += dot3(
                split_bf16(colv_ref[pl.ds(0, rows_k), pl.ds(b, tile)]),
                jnp.concatenate([high, low], axis=0), (((1,), (1,)), ((), ())),
            )
            csum_ref[:, pl.ds(b, tile)] += dot3(
                split_bf16(rowv_ref[pl.ds(0, rows_k), pl.ds(a, tile)]),
                jnp.concatenate([high, low], axis=1), (((1,), (0,)), ((), ())),
            )


def split_bf16(x):
    high = x.astype(jnp.bfloat16)
    return high, (x - high.astype(jnp.float32)).astype(jnp.bfloat16)


def dot3(left, right, dims):
    rows = left[0].shape[0]
    both = lax.dot_general(
        jnp.concatenate([left[0], left[1]], axis=0), right, dims, preferred_element_type=jnp.float32
    )
    width = both.shape[1] // 2
    return both[:rows, :width] + (both[rows:, :width] + both[:rows, width:])


def slot_products(blocks, rows_here, cols_here, live_count, row_tiles, column_tiles, rows_k):
    slot_count, tile, _ = blocks.shape
    sums_shape = lambda v: (rows_k, v.shape[1])
    group = group_width
    groups = slot_count // group

    def tile_map(g, rows, cols, count):
        last = jnp.maximum(count[0] - 1, 0) // group
        return (jnp.minimum(g, last), 0, 0)

    def whole(g, rows, cols, count):
        return (0, 0)

    grid_spec = pltpu.PrefetchScalarGridSpec(
        num_scalar_prefetch=3,
        grid=(groups,),
        in_specs=[
            pl.BlockSpec((group, tile, tile), tile_map),
            pl.BlockSpec(row_tiles.shape, whole),
            pl.BlockSpec(column_tiles.shape, whole),
        ],
        out_specs=[
            pl.BlockSpec(sums_shape(row_tiles), whole),
            pl.BlockSpec(sums_shape(column_tiles), whole),
        ],
    )
    return pl.pallas_call(
        functools.partial(_slots_kernel, group, rows_k, tile),
        grid_spec=grid_spec,
        out_shape=(
            jax.ShapeDtypeStruct(sums_shape(row_tiles), jnp.float32),
            jax.ShapeDtypeStruct(sums_shape(column_tiles), jnp.float32),
        ),
        compiler_params=pltpu.CompilerParams(dimension_semantics=("arbitrary",)),
    )(rows_here, cols_here, live_count.reshape(1), blocks, row_tiles, column_tiles)


def tile_dot(left, right):
    return jnp.dot(left, right.T, precision=highest)


def lower_solve(factor, rhs, transpose_a=False):
    return lax.linalg.triangular_solve(factor, rhs, left_side=True, lower=True, transpose_a=transpose_a)


def dot_rows(left, right):
    return jnp.dot(left, right.T, precision=highest)


def local(n_row, n_col, tile_values, tile_row, tile_col, counts, diagonal, current, previous, previous_image):
    k = current.shape[0]
    tile = tile_values.shape[-1]
    slot_count = tile_values.shape[2]
    blocks = tile_values.reshape(slot_count, tile, tile)
    rows_here = tile_row.reshape(slot_count)
    cols_here = tile_col.reshape(slot_count)
    live_count = counts.reshape(())

    row_cp, col_cp = gather_tiles(jnp.concatenate([current, previous], 0), n_row, n_col, 0)
    row_sum, col_sum = slot_products(blocks, rows_here, cols_here, live_count, row_cp, col_cp, k)
    row_cur, col_cur = row_cp[:k], col_cp[:k]
    scaled = diagonal[None, :] * current
    small_gram = dot_rows(current, current)
    proj_part = dot_rows(current, scaled) + tile_dot(row_cur, row_sum) + tile_dot(col_cur, col_sum)
    image_tiles, small, row_img, col_img = reduce_tiles(
        scaled, row_sum, col_sum, pack_small((small_gram, proj_part)), n_row, n_col, 1,
        forward=True,
    )
    image = image_tiles
    small_gram, small_proj = unpack_small(small, (small_gram, proj_part))

    factor = lax.linalg.cholesky(small_gram, symmetrize_input=False)
    ritz_matrix = lower_solve(factor, lower_solve(factor, small_proj), transpose_a=True)
    residual = image - jnp.dot(ritz_matrix.T, current, precision=highest)

    def residual_of(img_tiles, cur_tiles):
        return img_tiles - jnp.dot(ritz_matrix.T, cur_tiles, precision=highest)

    row_res = residual_of(row_img, row_cur)
    col_res = residual_of(col_img, col_cur)
    row_sum, col_sum = slot_products(blocks, rows_here, cols_here, live_count, row_res, col_res, k)
    search_basis = jnp.concatenate([current, residual, previous], 0)
    row_basis = jnp.concatenate([row_cur, row_res, row_cp[k:]], 0)
    col_basis = jnp.concatenate([col_cur, col_res, col_cp[k:]], 0)
    scaled = diagonal[None, :] * residual
    correlation = dot_rows(search_basis, search_basis)
    residual_part = (
        dot_rows(search_basis, scaled) + tile_dot(row_basis, row_sum) + tile_dot(col_basis, col_sum)
    )
    mixed_part = jnp.concatenate(
        [dot_rows(search_basis, image), residual_part, dot_rows(search_basis, previous_image)], 1
    )
    image_tiles, small = reduce_tiles(
        scaled, row_sum, col_sum, pack_small((correlation, mixed_part)), n_row, n_col, 2
    )
    residual_image = image_tiles
    correlation, mixed_terms = unpack_small(small, (correlation, mixed_part))
    pencil = 0.5 * (mixed_terms + mixed_terms.T)
    lower_factor = lax.linalg.cholesky(correlation, symmetrize_input=False)
    half_solve = lower_solve(lower_factor, pencil)
    reduced = lower_solve(lower_factor, half_solve.T)
    return (image, residual, residual_image, reduced)


def solution(mesh):
    n_row = mesh.shape["row"]
    n_col = mesh.shape["col"]
    return jax.shard_map(
        functools.partial(local, n_row, n_col),
        mesh=mesh,
        in_specs=(
            P("row", "col", None, None, None),
            P("row", "col", None),
            P("row", "col", None),
            P("row", "col"),
            P(("row", "col")),
            P(None, ("row", "col")),
            P(None, ("row", "col")),
            P(None, ("row", "col")),
        ),
        out_specs=(P(None, ("row", "col")), P(None, ("row", "col")), P(None, ("row", "col")), P()),
        check_vma=False,
    )
```

```python
import functools

import jax
import jax.numpy as jnp
from jax import lax
from jax.experimental import pallas as pl
from jax.experimental.pallas import tpu as pltpu
from jax.sharding import PartitionSpec as P

highest = lax.Precision.HIGHEST
group_width = 8
MESH = pl.DeviceIdType.MESH


def _barrier(n_row, n_col, r, c):
    barrier = pltpu.get_barrier_semaphore()

    def greet_col(k, carry):
        pl.semaphore_signal(barrier, 1, device_id=(r, lax.rem(c + k, n_col)), device_id_type=MESH)
        return carry

    def greet_row(k, carry):
        pl.semaphore_signal(barrier, 1, device_id=(lax.rem(r + k, n_row), c), device_id_type=MESH)
        return carry

    lax.fori_loop(1, n_col, greet_col, 0)
    lax.fori_loop(1, n_row, greet_row, 0)
    pl.semaphore_wait(barrier, n_row + n_col - 2)


def _gather_kernel(n_row, n_col, x_ref, rowv_ref, colv_ref, send_row, recv_row, send_col, recv_col, local_sem):
    vt = x_ref.shape[1]
    r = lax.axis_index("row")
    c = lax.axis_index("col")
    _barrier(n_row, n_col, r, c)

    def row_copy(j, src):
        return pltpu.make_async_remote_copy(
            src_ref=x_ref,
            dst_ref=rowv_ref.at[:, pl.ds(src * vt, vt)],
            send_sem=send_row.at[j],
            recv_sem=recv_row.at[src],
            device_id=(r, j),
            device_id_type=MESH,
        )

    def col_copy(i, src):
        return pltpu.make_async_remote_copy(
            src_ref=x_ref,
            dst_ref=colv_ref.at[:, pl.ds(src * vt, vt)],
            send_sem=send_col.at[i],
            recv_sem=recv_col.at[src],
            device_id=(i, c),
            device_id_type=MESH,
        )

    own_row = pltpu.make_async_copy(x_ref, rowv_ref.at[:, pl.ds(c * vt, vt)], local_sem.at[0])
    own_col = pltpu.make_async_copy(x_ref, colv_ref.at[:, pl.ds(r * vt, vt)], local_sem.at[1])
    own_row.start()
    own_col.start()

    def start_col(k, carry):
        row_copy(lax.rem(c + k, n_col), c).start()
        return carry

    def start_row(k, carry):
        col_copy(lax.rem(r + k, n_row), r).start()
        return carry

    lax.fori_loop(1, n_col, start_col, 0)
    lax.fori_loop(1, n_row, start_row, 0)

    def wait_col(k, carry):
        row_copy(lax.rem(c + k, n_col), c).wait_send()
        row_copy(c, lax.rem(c + n_col - k, n_col)).wait_recv()
        return carry

    def wait_row(k, carry):
        col_copy(lax.rem(r + k, n_row), r).wait_send()
        col_copy(r, lax.rem(r + n_row - k, n_row)).wait_recv()
        return carry

    lax.fori_loop(1, n_col, wait_col, 0)
    lax.fori_loop(1, n_row, wait_row, 0)
    own_row.wait()
    own_col.wait()


def gather_tiles(x_tiles, n_row, n_col, collective_id):
    k, vt = x_tiles.shape
    vmem = pl.BlockSpec(memory_space=pltpu.VMEM)
    return pl.pallas_call(
        functools.partial(_gather_kernel, n_row, n_col),
        out_shape=(
            jax.ShapeDtypeStruct((k, n_col * vt), x_tiles.dtype),
            jax.ShapeDtypeStruct((k, n_row * vt), x_tiles.dtype),
        ),
        in_specs=[vmem],
        out_specs=(vmem, vmem),
        scratch_shapes=[
            pltpu.SemaphoreType.DMA((n_col,)),
            pltpu.SemaphoreType.DMA((n_col,)),
            pltpu.SemaphoreType.DMA((n_row,)),
            pltpu.SemaphoreType.DMA((n_row,)),
            pltpu.SemaphoreType.DMA((2,)),
        ],
        compiler_params=pltpu.CompilerParams(collective_id=collective_id, has_side_effects=True),
    )(x_tiles)


def _reduce_kernel(n_row, n_col, forward, base_ref, rsum_ref, csum_ref, small_ref, out_ref, small_out, *rest):
    if forward:
        img_row, img_col = rest[:2]
        rest = rest[2:]
    (got_row, got_col, got_small_col, mid, got_small_row,
     send_row, recv_row, send_col, recv_col,
     send_small_col, recv_small_col, send_small_row, recv_small_row, local_sem) = rest[:14]
    vt = base_ref.shape[1]
    r = lax.axis_index("row")
    c = lax.axis_index("col")
    _barrier(n_row, n_col, r, c)

    def small_col_copy(j, src):
        return pltpu.make_async_remote_copy(
            src_ref=small_ref,
            dst_ref=got_small_col.at[src],
            send_sem=send_small_col.at[j],
            recv_sem=recv_small_col.at[src],
            device_id=(r, j),
            device_id_type=MESH,
        )

    def small_row_copy(i, src):
        return pltpu.make_async_remote_copy(
            src_ref=mid,
            dst_ref=got_small_row.at[src],
            send_sem=send_small_row.at[i],
            recv_sem=recv_small_row.at[src],
            device_id=(i, c),
            device_id_type=MESH,
        )

    def row_copy(j, src):
        return pltpu.make_async_remote_copy(
            src_ref=rsum_ref.at[:, pl.ds(j * vt, vt)],
            dst_ref=got_row.at[src],
            send_sem=send_row.at[j],
            recv_sem=recv_row.at[src],
            device_id=(r, j),
            device_id_type=MESH,
        )

    def col_copy(i, src):
        return pltpu.make_async_remote_copy(
            src_ref=csum_ref.at[:, pl.ds(i * vt, vt)],
            dst_ref=got_col.at[src],
            send_sem=send_col.at[i],
            recv_sem=recv_col.at[src],
            device_id=(i, c),
            device_id_type=MESH,
        )

    own_small = pltpu.make_async_copy(small_ref, got_small_col.at[c], local_sem.at[2])
    own_small.start()

    def start_small_col(k, carry):
        small_col_copy(lax.rem(c + k, n_col), c).start()
        return carry

    lax.fori_loop(1, n_col, start_small_col, 0)

    own_row = pltpu.make_async_copy(rsum_ref.at[:, pl.ds(c * vt, vt)], got_row.at[c], local_sem.at[0])
    own_col = pltpu.make_async_copy(csum_ref.at[:, pl.ds(r * vt, vt)], got_col.at[r], local_sem.at[1])
    own_row.start()
    own_col.start()

    def start_col(k, carry):
        row_copy(lax.rem(c + k, n_col), c).start()
        return carry

    def start_row(k, carry):
        col_copy(lax.rem(r + k, n_row), r).start()
        return carry

    lax.fori_loop(1, n_row, start_row, 0)
    lax.fori_loop(1, n_col, start_col, 0)

    def wait_small_col(k, carry):
        small_col_copy(lax.rem(c + k, n_col), c).wait_send()
        small_col_copy(c, lax.rem(c + n_col - k, n_col)).wait_recv()
        return carry

    lax.fori_loop(1, n_col, wait_small_col, 0)
    own_small.wait()
    mid[...] = jnp.sum(got_small_col[...], axis=0)

    own_mid = pltpu.make_async_copy(mid, got_small_row.at[r], local_sem.at[3])
    own_mid.start()

    def start_small_row(k, carry):
        small_row_copy(lax.rem(r + k, n_row), r).start()
        return carry

    lax.fori_loop(1, n_row, start_small_row, 0)

    def wait_col(k, carry):
        row_copy(lax.rem(c + k, n_col), c).wait_send()
        row_copy(c, lax.rem(c + n_col - k, n_col)).wait_recv()
        return carry

    def wait_row(k, carry):
        col_copy(lax.rem(r + k, n_row), r).wait_send()
        col_copy(r, lax.rem(r + n_row - k, n_row)).wait_recv()
        return carry

    lax.fori_loop(1, n_col, wait_col, 0)
    lax.fori_loop(1, n_row, wait_row, 0)
    own_row.wait()
    own_col.wait()
    out_ref[...] = base_ref[...] + jnp.sum(got_row[...], axis=0) + jnp.sum(got_col[...], axis=0)

    if forward:
        send_fr, recv_fr, send_fc, recv_fc = rest[14:]

        def fwd_row_copy(j, src):
            return pltpu.make_async_remote_copy(
                src_ref=out_ref,
                dst_ref=img_row.at[:, pl.ds(src * vt, vt)],
                send_sem=send_fr.at[j],
                recv_sem=recv_fr.at[src],
                device_id=(r, j),
                device_id_type=MESH,
            )

        def fwd_col_copy(i, src):
            return pltpu.make_async_remote_copy(
                src_ref=out_ref,
                dst_ref=img_col.at[:, pl.ds(src * vt, vt)],
                send_sem=send_fc.at[i],
                recv_sem=recv_fc.at[src],
                device_id=(i, c),
                device_id_type=MESH,
            )

        own_fr = pltpu.make_async_copy(out_ref, img_row.at[:, pl.ds(c * vt, vt)], local_sem.at[4])
        own_fc = pltpu.make_async_copy(out_ref, img_col.at[:, pl.ds(r * vt, vt)], local_sem.at[5])
        own_fr.start()
        own_fc.start()

        def start_fr(k, carry):
            fwd_row_copy(lax.rem(c + k, n_col), c).start()
            return carry

        def start_fc(k, carry):
            fwd_col_copy(lax.rem(r + k, n_row), r).start()
            return carry

        lax.fori_loop(1, n_row, start_fc, 0)
        lax.fori_loop(1, n_col, start_fr, 0)

    def wait_small_row(k, carry):
        small_row_copy(lax.rem(r + k, n_row), r).wait_send()
        small_row_copy(r, lax.rem(r + n_row - k, n_row)).wait_recv()
        return carry

    lax.fori_loop(1, n_row, wait_small_row, 0)
    own_mid.wait()
    small_out[...] = jnp.sum(got_small_row[...], axis=0)

    if forward:
        def wait_fr(k, carry):
            fwd_row_copy(lax.rem(c + k, n_col), c).wait_send()
            fwd_row_copy(c, lax.rem(c + n_col - k, n_col)).wait_recv()
            return carry

        def wait_fc(k, carry):
            fwd_col_copy(lax.rem(r + k, n_row), r).wait_send()
            fwd_col_copy(r, lax.rem(r + n_row - k, n_row)).wait_recv()
            return carry

        lax.fori_loop(1, n_col, wait_fr, 0)
        lax.fori_loop(1, n_row, wait_fc, 0)
        own_fr.wait()
        own_fc.wait()


def pack_small(values):
    flat = jnp.concatenate([v.reshape(-1) for v in values])
    tile = 8 * 128
    padded = -(-flat.shape[0] // tile) * tile
    return jnp.pad(flat, (0, padded - flat.shape[0])).reshape(-1, 128)


def unpack_small(total, values):
    total = total.reshape(-1)
    out, start = [], 0
    for v in values:
        out.append(total[start:start + v.size].reshape(v.shape))
        start += v.size
    return out


def reduce_tiles(base_tiles, row_sum, col_sum, small, n_row, n_col, collective_id, forward=False):
    k, vt = base_tiles.shape
    s = small.shape[0]
    vmem = pl.BlockSpec(memory_space=pltpu.VMEM)
    out_shape = [
        jax.ShapeDtypeStruct((k, vt), base_tiles.dtype),
        jax.ShapeDtypeStruct((s, 128), jnp.float32),
    ]
    extra_sems = []
    if forward:
        out_shape += [
            jax.ShapeDtypeStruct((k, n_col * vt), base_tiles.dtype),
            jax.ShapeDtypeStruct((k, n_row * vt), base_tiles.dtype),
        ]
        extra_sems = [
            pltpu.SemaphoreType.DMA((n_col,)),
            pltpu.SemaphoreType.DMA((n_col,)),
            pltpu.SemaphoreType.DMA((n_row,)),
            pltpu.SemaphoreType.DMA((n_row,)),
        ]
    return pl.pallas_call(
        functools.partial(_reduce_kernel, n_row, n_col, forward),
        out_shape=tuple(out_shape),
        in_specs=[vmem, vmem, vmem, vmem],
        out_specs=tuple(vmem for _ in out_shape),
        scratch_shapes=[
            pltpu.VMEM((n_col, k, vt), jnp.float32),
            pltpu.VMEM((n_row, k, vt), jnp.float32),
            pltpu.VMEM((n_col, s, 128), jnp.float32),
            pltpu.VMEM((s, 128), jnp.float32),
            pltpu.VMEM((n_row, s, 128), jnp.float32),
            pltpu.SemaphoreType.DMA((n_col,)),
            pltpu.SemaphoreType.DMA((n_col,)),
            pltpu.SemaphoreType.DMA((n_row,)),
            pltpu.SemaphoreType.DMA((n_row,)),
            pltpu.SemaphoreType.DMA((n_col,)),
            pltpu.SemaphoreType.DMA((n_col,)),
            pltpu.SemaphoreType.DMA((n_row,)),
            pltpu.SemaphoreType.DMA((n_row,)),
            pltpu.SemaphoreType.DMA((6,)),
        ] + extra_sems,
        compiler_params=pltpu.CompilerParams(collective_id=collective_id, has_side_effects=True),
    )(base_tiles, row_sum, col_sum, small)


def _slots_kernel(group, rows_k, tile, rows_ref, cols_ref, count_ref, tiles_ref, rowv_ref, colv_ref,
                  rsum_ref, csum_ref):
    g = pl.program_id(0)

    @pl.when(g == 0)
    def _():
        rsum_ref[...] = jnp.zeros_like(rsum_ref)
        csum_ref[...] = jnp.zeros_like(csum_ref)

    for s in range(group):
        slot = g * group + s

        @pl.when(slot < count_ref[0])
        def _():
            a = pl.multiple_of(rows_ref[slot] * tile, tile)
            b = pl.multiple_of(cols_ref[slot] * tile, tile)
            high, low = split_bf16(tiles_ref[s])
            rsum_ref[:, pl.ds(a, tile)] += dot3(
                split_bf16(colv_ref[pl.ds(0, rows_k), pl.ds(b, tile)]),
                jnp.concatenate([high, low], axis=0), (((1,), (1,)), ((), ())),
            )
            csum_ref[:, pl.ds(b, tile)] += dot3(
                split_bf16(rowv_ref[pl.ds(0, rows_k), pl.ds(a, tile)]),
                jnp.concatenate([high, low], axis=1), (((1,), (0,)), ((), ())),
            )


def split_bf16(x):
    high = x.astype(jnp.bfloat16)
    return high, (x - high.astype(jnp.float32)).astype(jnp.bfloat16)


def dot3(left, right, dims):
    rows = left[0].shape[0]
    both = lax.dot_general(
        jnp.concatenate([left[0], left[1]], axis=0), right, dims, preferred_element_type=jnp.float32
    )
    width = both.shape[1] // 2
    return both[:rows, :width] + (both[rows:, :width] + both[:rows, width:])


def slot_products(blocks, rows_here, cols_here, live_count, row_tiles, column_tiles, rows_k):
    slot_count, tile, _ = blocks.shape
    sums_shape = lambda v: (rows_k, v.shape[1])
    group = group_width
    groups = slot_count // group

    def tile_map(g, rows, cols, count):
        last = jnp.maximum(count[0] - 1, 0) // group
        return (jnp.minimum(g, last), 0, 0)

    def whole(g, rows, cols, count):
        return (0, 0)

    grid_spec = pltpu.PrefetchScalarGridSpec(
        num_scalar_prefetch=3,
        grid=(groups,),
        in_specs=[
            pl.BlockSpec((group, tile, tile), tile_map),
            pl.BlockSpec(row_tiles.shape, whole),
            pl.BlockSpec(column_tiles.shape, whole),
        ],
        out_specs=[
            pl.BlockSpec(sums_shape(row_tiles), whole),
            pl.BlockSpec(sums_shape(column_tiles), whole),
        ],
    )
    return pl.pallas_call(
        functools.partial(_slots_kernel, group, rows_k, tile),
        grid_spec=grid_spec,
        out_shape=(
            jax.ShapeDtypeStruct(sums_shape(row_tiles), jnp.float32),
            jax.ShapeDtypeStruct(sums_shape(column_tiles), jnp.float32),
        ),
        compiler_params=pltpu.CompilerParams(dimension_semantics=("arbitrary",)),
    )(rows_here, cols_here, live_count.reshape(1), blocks, row_tiles, column_tiles)


def tile_dot(left, right):
    return jnp.dot(left, right.T, precision=highest)


def lower_solve(factor, rhs, transpose_a=False):
    return lax.linalg.triangular_solve(factor, rhs, left_side=True, lower=True, transpose_a=transpose_a)


def dot_rows(left, right):
    return jnp.dot(left, right.T, precision=highest)


def local(n_row, n_col, tile_values, tile_row, tile_col, counts, diagonal, current, previous, previous_image):
    k = current.shape[0]
    tile = tile_values.shape[-1]
    slot_count = tile_values.shape[2]
    blocks = tile_values.reshape(slot_count, tile, tile)
    rows_here = tile_row.reshape(slot_count)
    cols_here = tile_col.reshape(slot_count)
    live_count = counts.reshape(())

    row_cp, col_cp = gather_tiles(jnp.concatenate([current, previous], 0), n_row, n_col, 0)
    row_sum, col_sum = slot_products(blocks, rows_here, cols_here, live_count, row_cp, col_cp, k)
    row_cur, col_cur = row_cp[:k], col_cp[:k]
    scaled = diagonal[None, :] * current
    small_gram = dot_rows(current, current)
    proj_part = dot_rows(current, scaled) + tile_dot(row_cur, row_sum) + tile_dot(col_cur, col_sum)
    image_tiles, small, row_img, col_img = reduce_tiles(
        scaled, row_sum, col_sum, pack_small((small_gram, proj_part)), n_row, n_col, 1,
        forward=True,
    )
    image = image_tiles
    small_gram, small_proj = unpack_small(small, (small_gram, proj_part))

    factor = lax.linalg.cholesky(small_gram, symmetrize_input=False)
    ritz_matrix = lower_solve(factor, lower_solve(factor, small_proj), transpose_a=True)
    residual = image - jnp.dot(ritz_matrix.T, current, precision=highest)

    def residual_of(img_tiles, cur_tiles):
        fitted = sum(ritz_matrix[l][:, None] * cur_tiles[l:l + 1, :] for l in range(k))
        return img_tiles - fitted

    row_res = residual_of(row_img, row_cur)
    col_res = residual_of(col_img, col_cur)
    row_sum, col_sum = slot_products(blocks, rows_here, cols_here, live_count, row_res, col_res, k)
    search_basis = jnp.concatenate([current, residual, previous], 0)
    scaled = diagonal[None, :] * residual
    correlation = dot_rows(search_basis, search_basis)
    residual_part = (
        dot_rows(search_basis, scaled)
        + jnp.concatenate([tile_dot(part, row_sum) for part in (row_cur, row_res, row_cp[k:])], 0)
        + jnp.concatenate([tile_dot(part, col_sum) for part in (col_cur, col_res, col_cp[k:])], 0)
    )
    mixed_part = jnp.concatenate(
        [dot_rows(search_basis, image), residual_part, dot_rows(search_basis, previous_image)], 1
    )
    image_tiles, small = reduce_tiles(
        scaled, row_sum, col_sum, pack_small((correlation, mixed_part)), n_row, n_col, 2
    )
    residual_image = image_tiles
    correlation, mixed_terms = unpack_small(small, (correlation, mixed_part))
    pencil = 0.5 * (mixed_terms + mixed_terms.T)
    lower_factor = lax.linalg.cholesky(correlation, symmetrize_input=False)
    half_solve = lower_solve(lower_factor, pencil)
    reduced = lower_solve(lower_factor, half_solve.T)
    return (image, residual, residual_image, reduced)


def solution(mesh):
    n_row = mesh.shape["row"]
    n_col = mesh.shape["col"]
    return jax.shard_map(
        functools.partial(local, n_row, n_col),
        mesh=mesh,
        in_specs=(
            P("row", "col", None, None, None),
            P("row", "col", None),
            P("row", "col", None),
            P("row", "col"),
            P(("row", "col")),
            P(None, ("row", "col")),
            P(None, ("row", "col")),
            P(None, ("row", "col")),
        ),
        out_specs=(P(None, ("row", "col")), P(None, ("row", "col")), P(None, ("row", "col")), P()),
        check_vma=False,
    )
```

```python
import functools

import jax
import jax.numpy as jnp
from jax import lax
from jax.experimental import pallas as pl
from jax.experimental.pallas import tpu as pltpu
from jax.sharding import PartitionSpec as P

highest = lax.Precision.HIGHEST
group_width = 8
MESH = pl.DeviceIdType.MESH


def _barrier(n_row, n_col, r, c):
    barrier = pltpu.get_barrier_semaphore()

    def greet_col(k, carry):
        pl.semaphore_signal(barrier, 1, device_id=(r, lax.rem(c + k, n_col)), device_id_type=MESH)
        return carry

    def greet_row(k, carry):
        pl.semaphore_signal(barrier, 1, device_id=(lax.rem(r + k, n_row), c), device_id_type=MESH)
        return carry

    lax.fori_loop(1, n_col, greet_col, 0)
    lax.fori_loop(1, n_row, greet_row, 0)
    pl.semaphore_wait(barrier, n_row + n_col - 2)


def _gather_kernel(n_row, n_col, cur_ref, prev_ref, rowv_ref, colv_ref, send_row, recv_row, send_col, recv_col,
                   local_sem, x_ref, stage_sem):
    vt = x_ref.shape[1]
    rows = cur_ref.shape[0]
    r = lax.axis_index("row")
    c = lax.axis_index("col")
    stage_cur = pltpu.make_async_copy(cur_ref, x_ref.at[pl.ds(0, rows)], stage_sem.at[0])
    stage_prev = pltpu.make_async_copy(prev_ref, x_ref.at[pl.ds(rows, rows)], stage_sem.at[1])
    stage_cur.start()
    stage_prev.start()
    _barrier(n_row, n_col, r, c)
    stage_cur.wait()
    stage_prev.wait()

    def row_copy(j, src):
        return pltpu.make_async_remote_copy(
            src_ref=x_ref,
            dst_ref=rowv_ref.at[:, pl.ds(src * vt, vt)],
            send_sem=send_row.at[j],
            recv_sem=recv_row.at[src],
            device_id=(r, j),
            device_id_type=MESH,
        )

    def col_copy(i, src):
        return pltpu.make_async_remote_copy(
            src_ref=x_ref,
            dst_ref=colv_ref.at[:, pl.ds(src * vt, vt)],
            send_sem=send_col.at[i],
            recv_sem=recv_col.at[src],
            device_id=(i, c),
            device_id_type=MESH,
        )

    own_row = pltpu.make_async_copy(x_ref, rowv_ref.at[:, pl.ds(c * vt, vt)], local_sem.at[0])
    own_col = pltpu.make_async_copy(x_ref, colv_ref.at[:, pl.ds(r * vt, vt)], local_sem.at[1])
    own_row.start()
    own_col.start()

    def start_col(k, carry):
        row_copy(lax.rem(c + k, n_col), c).start()
        return carry

    def start_row(k, carry):
        col_copy(lax.rem(r + k, n_row), r).start()
        return carry

    lax.fori_loop(1, n_col, start_col, 0)
    lax.fori_loop(1, n_row, start_row, 0)

    def wait_col(k, carry):
        row_copy(lax.rem(c + k, n_col), c).wait_send()
        row_copy(c, lax.rem(c + n_col - k, n_col)).wait_recv()
        return carry

    def wait_row(k, carry):
        col_copy(lax.rem(r + k, n_row), r).wait_send()
        col_copy(r, lax.rem(r + n_row - k, n_row)).wait_recv()
        return carry

    lax.fori_loop(1, n_col, wait_col, 0)
    lax.fori_loop(1, n_row, wait_row, 0)
    own_row.wait()
    own_col.wait()


def gather_tiles(current, previous, n_row, n_col, collective_id):
    rows, vt = current.shape
    k = 2 * rows
    vmem = pl.BlockSpec(memory_space=pltpu.VMEM)
    return pl.pallas_call(
        functools.partial(_gather_kernel, n_row, n_col),
        out_shape=(
            jax.ShapeDtypeStruct((k, n_col * vt), current.dtype),
            jax.ShapeDtypeStruct((k, n_row * vt), current.dtype),
        ),
        in_specs=[vmem, vmem],
        out_specs=(vmem, vmem),
        scratch_shapes=[
            pltpu.SemaphoreType.DMA((n_col,)),
            pltpu.SemaphoreType.DMA((n_col,)),
            pltpu.SemaphoreType.DMA((n_row,)),
            pltpu.SemaphoreType.DMA((n_row,)),
            pltpu.SemaphoreType.DMA((2,)),
            pltpu.VMEM((k, vt), current.dtype),
            pltpu.SemaphoreType.DMA((2,)),
        ],
        compiler_params=pltpu.CompilerParams(collective_id=collective_id, has_side_effects=True),
    )(current, previous)


def _reduce_kernel(n_row, n_col, forward, base_ref, rsum_ref, csum_ref, small_ref, out_ref, small_out, *rest):
    if forward:
        img_row, img_col = rest[:2]
        rest = rest[2:]
    (got_row, got_col, got_small_col, mid, got_small_row,
     send_row, recv_row, send_col, recv_col,
     send_small_col, recv_small_col, send_small_row, recv_small_row, local_sem) = rest[:14]
    vt = base_ref.shape[1]
    r = lax.axis_index("row")
    c = lax.axis_index("col")
    _barrier(n_row, n_col, r, c)

    def small_col_copy(j, src):
        return pltpu.make_async_remote_copy(
            src_ref=small_ref,
            dst_ref=got_small_col.at[src],
            send_sem=send_small_col.at[j],
            recv_sem=recv_small_col.at[src],
            device_id=(r, j),
            device_id_type=MESH,
        )

    def small_row_copy(i, src):
        return pltpu.make_async_remote_copy(
            src_ref=mid,
            dst_ref=got_small_row.at[src],
            send_sem=send_small_row.at[i],
            recv_sem=recv_small_row.at[src],
            device_id=(i, c),
            device_id_type=MESH,
        )

    def row_copy(j, src):
        return pltpu.make_async_remote_copy(
            src_ref=rsum_ref.at[:, pl.ds(j * vt, vt)],
            dst_ref=got_row.at[src],
            send_sem=send_row.at[j],
            recv_sem=recv_row.at[src],
            device_id=(r, j),
            device_id_type=MESH,
        )

    def col_copy(i, src):
        return pltpu.make_async_remote_copy(
            src_ref=csum_ref.at[:, pl.ds(i * vt, vt)],
            dst_ref=got_col.at[src],
            send_sem=send_col.at[i],
            recv_sem=recv_col.at[src],
            device_id=(i, c),
            device_id_type=MESH,
        )

    own_small = pltpu.make_async_copy(small_ref, got_small_col.at[c], local_sem.at[2])
    own_small.start()

    def start_small_col(k, carry):
        small_col_copy(lax.rem(c + k, n_col), c).start()
        return carry

    lax.fori_loop(1, n_col, start_small_col, 0)

    own_row = pltpu.make_async_copy(rsum_ref.at[:, pl.ds(c * vt, vt)], got_row.at[c], local_sem.at[0])
    own_col = pltpu.make_async_copy(csum_ref.at[:, pl.ds(r * vt, vt)], got_col.at[r], local_sem.at[1])
    own_row.start()
    own_col.start()

    def start_col(k, carry):
        row_copy(lax.rem(c + k, n_col), c).start()
        return carry

    def start_row(k, carry):
        col_copy(lax.rem(r + k, n_row), r).start()
        return carry

    lax.fori_loop(1, n_row, start_row, 0)
    lax.fori_loop(1, n_col, start_col, 0)

    def wait_small_col(k, carry):
        small_col_copy(lax.rem(c + k, n_col), c).wait_send()
        small_col_copy(c, lax.rem(c + n_col - k, n_col)).wait_recv()
        return carry

    lax.fori_loop(1, n_col, wait_small_col, 0)
    own_small.wait()
    mid[...] = jnp.sum(got_small_col[...], axis=0)

    own_mid = pltpu.make_async_copy(mid, got_small_row.at[r], local_sem.at[3])
    own_mid.start()

    def start_small_row(k, carry):
        small_row_copy(lax.rem(r + k, n_row), r).start()
        return carry

    lax.fori_loop(1, n_row, start_small_row, 0)

    def wait_col(k, carry):
        row_copy(lax.rem(c + k, n_col), c).wait_send()
        row_copy(c, lax.rem(c + n_col - k, n_col)).wait_recv()
        return carry

    def wait_row(k, carry):
        col_copy(lax.rem(r + k, n_row), r).wait_send()
        col_copy(r, lax.rem(r + n_row - k, n_row)).wait_recv()
        return carry

    lax.fori_loop(1, n_col, wait_col, 0)
    lax.fori_loop(1, n_row, wait_row, 0)
    own_row.wait()
    own_col.wait()
    out_ref[...] = base_ref[...] + jnp.sum(got_row[...], axis=0) + jnp.sum(got_col[...], axis=0)

    if forward:
        send_fr, recv_fr, send_fc, recv_fc = rest[14:]

        def fwd_row_copy(j, src):
            return pltpu.make_async_remote_copy(
                src_ref=out_ref,
                dst_ref=img_row.at[:, pl.ds(src * vt, vt)],
                send_sem=send_fr.at[j],
                recv_sem=recv_fr.at[src],
                device_id=(r, j),
                device_id_type=MESH,
            )

        def fwd_col_copy(i, src):
            return pltpu.make_async_remote_copy(
                src_ref=out_ref,
                dst_ref=img_col.at[:, pl.ds(src * vt, vt)],
                send_sem=send_fc.at[i],
                recv_sem=recv_fc.at[src],
                device_id=(i, c),
                device_id_type=MESH,
            )

        own_fr = pltpu.make_async_copy(out_ref, img_row.at[:, pl.ds(c * vt, vt)], local_sem.at[4])
        own_fc = pltpu.make_async_copy(out_ref, img_col.at[:, pl.ds(r * vt, vt)], local_sem.at[5])
        own_fr.start()
        own_fc.start()

        def start_fr(k, carry):
            fwd_row_copy(lax.rem(c + k, n_col), c).start()
            return carry

        def start_fc(k, carry):
            fwd_col_copy(lax.rem(r + k, n_row), r).start()
            return carry

        lax.fori_loop(1, n_row, start_fc, 0)
        lax.fori_loop(1, n_col, start_fr, 0)

    def wait_small_row(k, carry):
        small_row_copy(lax.rem(r + k, n_row), r).wait_send()
        small_row_copy(r, lax.rem(r + n_row - k, n_row)).wait_recv()
        return carry

    lax.fori_loop(1, n_row, wait_small_row, 0)
    own_mid.wait()
    small_out[...] = jnp.sum(got_small_row[...], axis=0)

    if forward:
        def wait_fr(k, carry):
            fwd_row_copy(lax.rem(c + k, n_col), c).wait_send()
            fwd_row_copy(c, lax.rem(c + n_col - k, n_col)).wait_recv()
            return carry

        def wait_fc(k, carry):
            fwd_col_copy(lax.rem(r + k, n_row), r).wait_send()
            fwd_col_copy(r, lax.rem(r + n_row - k, n_row)).wait_recv()
            return carry

        lax.fori_loop(1, n_col, wait_fr, 0)
        lax.fori_loop(1, n_row, wait_fc, 0)
        own_fr.wait()
        own_fc.wait()


def pack_small(values):
    flat = jnp.concatenate([v.reshape(-1) for v in values])
    tile = 8 * 128
    padded = -(-flat.shape[0] // tile) * tile
    return jnp.pad(flat, (0, padded - flat.shape[0])).reshape(-1, 128)


def unpack_small(total, values):
    total = total.reshape(-1)
    out, start = [], 0
    for v in values:
        out.append(total[start:start + v.size].reshape(v.shape))
        start += v.size
    return out


def reduce_tiles(base_tiles, row_sum, col_sum, small, n_row, n_col, collective_id, forward=False):
    k, vt = base_tiles.shape
    s = small.shape[0]
    vmem = pl.BlockSpec(memory_space=pltpu.VMEM)
    out_shape = [
        jax.ShapeDtypeStruct((k, vt), base_tiles.dtype),
        jax.ShapeDtypeStruct((s, 128), jnp.float32),
    ]
    extra_sems = []
    if forward:
        out_shape += [
            jax.ShapeDtypeStruct((k, n_col * vt), base_tiles.dtype),
            jax.ShapeDtypeStruct((k, n_row * vt), base_tiles.dtype),
        ]
        extra_sems = [
            pltpu.SemaphoreType.DMA((n_col,)),
            pltpu.SemaphoreType.DMA((n_col,)),
            pltpu.SemaphoreType.DMA((n_row,)),
            pltpu.SemaphoreType.DMA((n_row,)),
        ]
    return pl.pallas_call(
        functools.partial(_reduce_kernel, n_row, n_col, forward),
        out_shape=tuple(out_shape),
        in_specs=[vmem, vmem, vmem, vmem],
        out_specs=tuple(vmem for _ in out_shape),
        scratch_shapes=[
            pltpu.VMEM((n_col, k, vt), jnp.float32),
            pltpu.VMEM((n_row, k, vt), jnp.float32),
            pltpu.VMEM((n_col, s, 128), jnp.float32),
            pltpu.VMEM((s, 128), jnp.float32),
            pltpu.VMEM((n_row, s, 128), jnp.float32),
            pltpu.SemaphoreType.DMA((n_col,)),
            pltpu.SemaphoreType.DMA((n_col,)),
            pltpu.SemaphoreType.DMA((n_row,)),
            pltpu.SemaphoreType.DMA((n_row,)),
            pltpu.SemaphoreType.DMA((n_col,)),
            pltpu.SemaphoreType.DMA((n_col,)),
            pltpu.SemaphoreType.DMA((n_row,)),
            pltpu.SemaphoreType.DMA((n_row,)),
            pltpu.SemaphoreType.DMA((6,)),
        ] + extra_sems,
        compiler_params=pltpu.CompilerParams(collective_id=collective_id, has_side_effects=True),
    )(base_tiles, row_sum, col_sum, small)


def _slots_kernel(group, rows_k, tile, rows_ref, cols_ref, count_ref, tiles_ref, rowv_ref, colv_ref,
                  rsum_ref, csum_ref):
    g = pl.program_id(0)

    @pl.when(g == 0)
    def _():
        rsum_ref[...] = jnp.zeros_like(rsum_ref)
        csum_ref[...] = jnp.zeros_like(csum_ref)

    for s in range(group):
        slot = g * group + s

        @pl.when(slot < count_ref[0])
        def _():
            a = pl.multiple_of(rows_ref[slot] * tile, tile)
            b = pl.multiple_of(cols_ref[slot] * tile, tile)
            high, low = split_bf16(tiles_ref[s])
            rsum_ref[:, pl.ds(a, tile)] += dot3(
                split_bf16(colv_ref[pl.ds(0, rows_k), pl.ds(b, tile)]),
                jnp.concatenate([high, low], axis=0), (((1,), (1,)), ((), ())),
            )
            csum_ref[:, pl.ds(b, tile)] += dot3(
                split_bf16(rowv_ref[pl.ds(0, rows_k), pl.ds(a, tile)]),
                jnp.concatenate([high, low], axis=1), (((1,), (0,)), ((), ())),
            )


def split_bf16(x):
    high = x.astype(jnp.bfloat16)
    return high, (x - high.astype(jnp.float32)).astype(jnp.bfloat16)


def dot3(left, right, dims):
    rows = left[0].shape[0]
    both = lax.dot_general(
        jnp.concatenate([left[0], left[1]], axis=0), right, dims, preferred_element_type=jnp.float32
    )
    width = both.shape[1] // 2
    return both[:rows, :width] + (both[rows:, :width] + both[:rows, width:])


def slot_products(blocks, rows_here, cols_here, live_count, row_tiles, column_tiles, rows_k):
    slot_count, tile, _ = blocks.shape
    sums_shape = lambda v: (rows_k, v.shape[1])
    group = group_width
    groups = slot_count // group

    def tile_map(g, rows, cols, count):
        last = jnp.maximum(count[0] - 1, 0) // group
        return (jnp.minimum(g, last), 0, 0)

    def whole(g, rows, cols, count):
        return (0, 0)

    grid_spec = pltpu.PrefetchScalarGridSpec(
        num_scalar_prefetch=3,
        grid=(groups,),
        in_specs=[
            pl.BlockSpec((group, tile, tile), tile_map),
            pl.BlockSpec(row_tiles.shape, whole),
            pl.BlockSpec(column_tiles.shape, whole),
        ],
        out_specs=[
            pl.BlockSpec(sums_shape(row_tiles), whole),
            pl.BlockSpec(sums_shape(column_tiles), whole),
        ],
    )
    return pl.pallas_call(
        functools.partial(_slots_kernel, group, rows_k, tile),
        grid_spec=grid_spec,
        out_shape=(
            jax.ShapeDtypeStruct(sums_shape(row_tiles), jnp.float32),
            jax.ShapeDtypeStruct(sums_shape(column_tiles), jnp.float32),
        ),
        compiler_params=pltpu.CompilerParams(dimension_semantics=("arbitrary",)),
    )(rows_here, cols_here, live_count.reshape(1), blocks, row_tiles, column_tiles)


def tile_dot(left, right):
    return jnp.dot(left, right.T, precision=highest)


def lower_solve(factor, rhs, transpose_a=False):
    return lax.linalg.triangular_solve(factor, rhs, left_side=True, lower=True, transpose_a=transpose_a)


def dot_rows(left, right):
    return jnp.dot(left, right.T, precision=highest)


def local(n_row, n_col, tile_values, tile_row, tile_col, counts, diagonal, current, previous, previous_image):
    k = current.shape[0]
    tile = tile_values.shape[-1]
    slot_count = tile_values.shape[2]
    blocks = tile_values.reshape(slot_count, tile, tile)
    rows_here = tile_row.reshape(slot_count)
    cols_here = tile_col.reshape(slot_count)
    live_count = counts.reshape(())

    row_cp, col_cp = gather_tiles(current, previous, n_row, n_col, 0)
    row_sum, col_sum = slot_products(blocks, rows_here, cols_here, live_count, row_cp, col_cp, k)
    row_cur, col_cur = row_cp[:k], col_cp[:k]
    scaled = diagonal[None, :] * current
    small_gram = dot_rows(current, current)
    proj_part = dot_rows(current, scaled) + tile_dot(row_cur, row_sum) + tile_dot(col_cur, col_sum)
    image_tiles, small, row_img, col_img = reduce_tiles(
        scaled, row_sum, col_sum, pack_small((small_gram, proj_part)), n_row, n_col, 1,
        forward=True,
    )
    image = image_tiles
    small_gram, small_proj = unpack_small(small, (small_gram, proj_part))

    factor = lax.linalg.cholesky(small_gram, symmetrize_input=False)
    ritz_matrix = lower_solve(factor, lower_solve(factor, small_proj), transpose_a=True)
    residual = image - jnp.dot(ritz_matrix.T, current, precision=highest)

    def residual_of(img_tiles, cur_tiles):
        fitted = sum(ritz_matrix[l][:, None] * cur_tiles[l:l + 1, :] for l in range(k))
        return img_tiles - fitted

    row_res = residual_of(row_img, row_cur)
    col_res = residual_of(col_img, col_cur)
    row_sum, col_sum = slot_products(blocks, rows_here, cols_here, live_count, row_res, col_res, k)
    search_basis = jnp.concatenate([current, residual, previous], 0)
    row_basis = jnp.concatenate([row_cur, row_res, row_cp[k:]], 0)
    col_basis = jnp.concatenate([col_cur, col_res, col_cp[k:]], 0)
    scaled = diagonal[None, :] * residual
    correlation = dot_rows(search_basis, search_basis)
    residual_part = (
        dot_rows(search_basis, scaled) + tile_dot(row_basis, row_sum) + tile_dot(col_basis, col_sum)
    )
    mixed_part = jnp.concatenate(
        [dot_rows(search_basis, image), residual_part, dot_rows(search_basis, previous_image)], 1
    )
    image_tiles, small = reduce_tiles(
        scaled, row_sum, col_sum, pack_small((correlation, mixed_part)), n_row, n_col, 2
    )
    residual_image = image_tiles
    correlation, mixed_terms = unpack_small(small, (correlation, mixed_part))
    pencil = 0.5 * (mixed_terms + mixed_terms.T)
    lower_factor = lax.linalg.cholesky(correlation, symmetrize_input=False)
    half_solve = lower_solve(lower_factor, pencil)
    reduced = lower_solve(lower_factor, half_solve.T)
    return (image, residual, residual_image, reduced)


def solution(mesh):
    n_row = mesh.shape["row"]
    n_col = mesh.shape["col"]
    return jax.shard_map(
        functools.partial(local, n_row, n_col),
        mesh=mesh,
        in_specs=(
            P("row", "col", None, None, None),
            P("row", "col", None),
            P("row", "col", None),
            P("row", "col"),
            P(("row", "col")),
            P(None, ("row", "col")),
            P(None, ("row", "col")),
            P(None, ("row", "col")),
        ),
        out_specs=(P(None, ("row", "col")), P(None, ("row", "col")), P(None, ("row", "col")), P()),
        check_vma=False,
    )
```
